128 devices in a mesh: fluid: 32 (over z, y, core), shell: 4 (over x).
Axes of the slice: x: 4, y: 4, z: 4, core: 2. Of those that a mesh axis runs over, the one named last changes fastest.
Arguments:
- traction_base: float32 [32768, 3, 128], P(('fluid', 'shell')), may hold values from -6 to 6
- added_mass: float32 [32768, 128], P(('fluid', 'shell')), may hold values from 0.3 to 3
- interface_prev: float32 [32768, 3, 128], P(('fluid', 'shell')), may hold values from -6 to 6
- patch_route: int32 [32768, 1], P(('fluid', 'shell')), may hold values from 0 to 127; in each aligned block of 256 rows (0 to 255, 256 to 511, ...) at most 4 rows name the same one
- basis_pattern: int32 [32768], P(('fluid', 'shell')), may hold values from 0 to 7
- column_block: int32 [32768], P(('fluid', 'shell')), may hold values from 0 to 3
- basis_values_table: float32 [8, 128, 128], replicated, may hold values from -0.0625 to 0.0625
- stiffness: float32 [1024, 384, 384], P(('fluid', 'shell')), may hold values from -0.21875 to 0.21875
- stiff_row: int32 [1024], P(('fluid', 'shell')), may hold values from 0 to 15
- stiff_col: int32 [1024], P(('fluid', 'shell')), may hold values from 0 to 3
- block_inverse: float32 [512, 384, 384], P(('fluid', 'shell')), may hold values from -1 to 2.5
- previous_shell_displacement: float32 [512, 3, 128], P(('fluid', 'shell')), may hold values from -6 to 6
Outputs:
- shell_disp: float32 [512, 3, 128], P(('fluid', 'shell'))
- interface_disp: float32 [32768, 3, 128], P(('fluid', 'shell'))
The draws below stay inside these ranges and needn't reach their ends.
Inputs may be any that keep to these rules, and one draw needn't show every extreme that they name: `patch_route`: patch p belongs to index p of fluid+shell. At most 4 of the blocks of one device lie on one patch.
All inputs are finite; a program needn't handle non-finite values.
Results may differ from the reference program's by a relative error of at most 0.0001.
Values sent between devices are 32-bit elements; how exact they have to be, the bound alone decides.
A program may use at most 64 MiB of HBM per device.

```python
import math
import jax
import jax.numpy as jnp
import numpy as np
from jax import lax

QUAD_POINTS = 128
CONTROL_PER_COL = 128
PATTERN_COUNT = 8
ITERS = 2
DEVICE_QUAD_BLKS = 256
COLUMN_BLOCKS = 4
SHELL_PATCHES = 128
BLOCKS = 32768
CAP = 4
STIFF_BLOCKS = 8
N_SHELL = 4


def draw_block_inverse(key, part):
    block_width = 3 * CONTROL_PER_COL
    first_key, second_key = jax.random.split(key)
    spread_part = jax.random.normal(first_key, (SHELL_PATCHES * COLUMN_BLOCKS, block_width, block_width), jnp.float32) * (0.5 / math.sqrt(block_width))
    diagonal = jax.random.uniform(second_key, (SHELL_PATCHES * COLUMN_BLOCKS, block_width, 1), jnp.float32, 0.75, 1.25)
    identity = jnp.eye(block_width, dtype=jnp.float32)
    return spread_part + identity[None, :, :] * diagonal


def plant(result, stream_key, low, top_value):
    spot = [jax.random.randint(jax.random.fold_in(stream_key, axis), (), 0, length) for axis, length in enumerate(result.shape)]
    longest = result.shape.index(max(result.shape))
    beside = spot[:longest] + [(spot[longest] + 1) % result.shape[longest]] + spot[longest + 1:]
    return result.at[tuple(spot)].set(low).at[tuple(beside)].set(top_value)


def level_of(own_key, shape, pieces, smallest, largest):
    level, own = 1.0, jax.random.fold_in(own_key, 6)
    for axis_at, shards_of in pieces:
        steps = jnp.exp(jax.random.uniform(jax.random.fold_in(own, axis_at), (shards_of,), jnp.float32, smallest / len(pieces), largest / len(pieces)))
        level = level * jnp.repeat(steps, shape[axis_at] // shards_of).reshape([-1 if axis == axis_at else 1 for axis in range(len(shape))])
    return level


def shared_out(own_key, own, number, rows, amount, top, limit, lean):
    sequence = jax.random.permutation(own_key, amount)
    packed, ordinary = portions_of(amount, rows * top, limit, lean, True), portions_of(amount, rows * top, limit, lean, False)
    places = jnp.arange(amount)

    def named(lengths, rotation):
        used = int((lengths > 0).sum())
        fixed = max(1, used // 4)
        shifted = fixed + (places - fixed + rotation * (used - fixed)) % max(1, amount - fixed)
        return jnp.zeros((amount,), jnp.int32).at[sequence[jnp.where(places < fixed, places, shifted)]].set(jnp.asarray(lengths, jnp.int32))

    lengths = jnp.where(number % 4 == 0, named(packed, number // 4), named(ordinary, number - number // 4 - 1))
    mixed = jax.random.permutation(jax.random.fold_in(own, 3), amount)
    giver, taker = mixed[0:amount // 2 * 2:2], mixed[1:amount // 2 * 2:2]
    margin = jnp.minimum(lengths[giver] - 1, limit - lengths[taker]) // 2
    margin = jnp.where((giver == sequence[0]) | (taker == sequence[0]) | (lengths[taker] == 0), 0, jnp.maximum(margin, 0))
    shifted = jax.random.randint(jax.random.fold_in(own, 4), (amount // 2,), 0, 1 << 20) % (margin + 1)
    lengths = lengths.at[giver].add(-shifted).at[taker].add(shifted)
    items = jnp.searchsorted(jnp.cumsum(lengths), jnp.arange(rows * top), side="right").astype(jnp.int32)
    listing = items.reshape(top, rows).T
    listing = listing[jax.random.permutation(jax.random.fold_in(own, 1), rows)]
    rotation = jax.random.randint(jax.random.fold_in(own, 2), (rows, 1), 0, top)
    return jnp.take_along_axis(listing, (jnp.arange(top)[None, :] + rotation) % top, axis=1)


def portions_of(amount, total, limit, skew, full):
    loads = [(1 << 20) // math.isqrt(rank ** skew) + 1 for rank in range(1, amount + 1)]
    largest = limit if full else min(limit, max(-(-total // amount), total * loads[0] // sum(loads)))
    least = 1 if total - largest >= amount - 1 else 0
    counts, spare = [largest] + [least] * (amount - 1), total - largest - least * (amount - 1)
    while spare > 0:
        movable = [i for i in range(1, amount) if counts[i] < largest] or [i for i in range(1, amount) if counts[i] < limit]
        whole, remaining = sum([loads[i] for i in movable]), spare
        for i in movable:
            more = min(limit - counts[i], max(1, remaining * loads[i] // whole), spare)
            counts[i] = counts[i] + more
            spare = spare - more
    return np.array(counts)


def bell_draw(stream_key, extent, width, limit, cuts=(), kind=jnp.bfloat16):
    values = width * jax.random.normal(stream_key, extent, jnp.float32)
    if cuts:
        values = values * level_of(stream_key, extent, cuts, -0.22, 0.18)
    return jnp.clip(values, -limit, limit).astype(kind)


def setup_inputs(seed: int = 0) -> dict:
    streams_of = jax.random.split(jax.random.key(seed), 13)
    traction_base = bell_draw(streams_of[0], (BLOCKS, 3, QUAD_POINTS), 1.0, 6.0, ((0, 128),), jnp.float32)
    added_mass = jnp.clip(jnp.exp(math.log(3.0) - 2.3025851 * jax.random.uniform(streams_of[1], (BLOCKS, QUAD_POINTS), jnp.float32) ** level_of(streams_of[1], (BLOCKS, QUAD_POINTS), ((0, 128),), -0.2, 0.2)), 0.3, 3.0)
    interface_prev = bell_draw(streams_of[2], (BLOCKS, 3, QUAD_POINTS), 1.0, 6.0, ((0, 128),), jnp.float32)
    patch_route_keys = jax.random.split(jax.random.fold_in(streams_of[3], 1), BLOCKS // DEVICE_QUAD_BLKS)
    patch_route_turns = jax.random.permutation(jax.random.fold_in(streams_of[3], 3), BLOCKS // DEVICE_QUAD_BLKS)
    patch_route = jax.vmap(lambda own, number: shared_out(jax.random.fold_in(streams_of[3], 2), own, number, DEVICE_QUAD_BLKS, SHELL_PATCHES, 1, CAP, 2))(patch_route_keys, patch_route_turns).reshape((BLOCKS, 1))
    basis_pattern = plant(jax.random.randint(streams_of[4], (BLOCKS,), 0, PATTERN_COUNT), jax.random.fold_in(streams_of[4], 1), 0, PATTERN_COUNT - 1).astype(jnp.int32)
    column_block = plant(jax.random.randint(streams_of[5], (BLOCKS,), 0, COLUMN_BLOCKS), jax.random.fold_in(streams_of[5], 1), 0, COLUMN_BLOCKS - 1).astype(jnp.int32)
    basis_values_table = bell_draw(streams_of[6], (PATTERN_COUNT, QUAD_POINTS, CONTROL_PER_COL), (QUAD_POINTS * DEVICE_QUAD_BLKS // COLUMN_BLOCKS) ** -0.5, 0.0625, (), jnp.float32)
    stiffness = bell_draw(streams_of[7], (SHELL_PATCHES * STIFF_BLOCKS, 3 * CONTROL_PER_COL, 3 * CONTROL_PER_COL), (6 * CONTROL_PER_COL) ** -0.5, 0.21875, ((0, 128),), jnp.float32)
    stiff_row = plant(jax.random.randint(streams_of[8], (SHELL_PATCHES * STIFF_BLOCKS,), 0, N_SHELL * COLUMN_BLOCKS), jax.random.fold_in(streams_of[8], 1), 0, (N_SHELL * COLUMN_BLOCKS) - 1).astype(jnp.int32)
    stiff_col = plant(jax.random.randint(streams_of[9], (SHELL_PATCHES * STIFF_BLOCKS,), 0, COLUMN_BLOCKS), jax.random.fold_in(streams_of[9], 1), 0, COLUMN_BLOCKS - 1).astype(jnp.int32)
    block_inverse = draw_block_inverse(jax.random.fold_in(streams_of[12], 71), 0)
    previous_shell_displacement = bell_draw(streams_of[11], (SHELL_PATCHES * COLUMN_BLOCKS, 3, CONTROL_PER_COL), 1.0, 6.0, ((0, 128),), jnp.float32)
    return {"traction_base": traction_base, "added_mass": added_mass, "interface_prev": interface_prev, "patch_route": patch_route, "basis_pattern": basis_pattern, "column_block": column_block, "basis_values_table": basis_values_table, "stiffness": stiffness, "stiff_row": stiff_row, "stiff_col": stiff_col, "block_inverse": block_inverse, "previous_shell_displacement": previous_shell_displacement}


def reference(traction_base, added_mass, interface_prev, patch_route, basis_pattern, column_block, basis_values_table, stiffness, stiff_row, stiff_col, block_inverse, previous_shell_displacement):
    highest = lax.Precision.HIGHEST
    targets = patch_route[:, 0].astype(jnp.int32)
    group_code = (targets * COLUMN_BLOCKS + column_block) * PATTERN_COUNT + basis_pattern
    owner_patch = jnp.arange(SHELL_PATCHES * STIFF_BLOCKS, dtype=jnp.int32) // STIFF_BLOCKS
    target_rows = (owner_patch // N_SHELL) * (N_SHELL * COLUMN_BLOCKS) + stiff_row
    source_rows = owner_patch * COLUMN_BLOCKS + stiff_col
    displacement_field = previous_shell_displacement
    interface = interface_prev
    for iteration in range(ITERS):
        traction = traction_base - added_mass[:, None, :] * interface
        grouped = jax.ops.segment_sum(traction, group_code, num_segments=SHELL_PATCHES * COLUMN_BLOCKS * PATTERN_COUNT)
        grouped = grouped.reshape(SHELL_PATCHES * COLUMN_BLOCKS, PATTERN_COUNT, 3, QUAD_POINTS)
        shell_load_vector = jnp.einsum('knaq,nqc->kac', grouped, basis_values_table, precision=highest)
        flat_values = displacement_field.reshape(SHELL_PATCHES * COLUMN_BLOCKS, 3 * CONTROL_PER_COL)
        products = jnp.einsum('bij,bj->bi', stiffness, flat_values[source_rows], precision=highest)
        coupled_result = jax.ops.segment_sum(products, target_rows, num_segments=SHELL_PATCHES * COLUMN_BLOCKS)
        residual_row_values = shell_load_vector.reshape(SHELL_PATCHES * COLUMN_BLOCKS, 3 * CONTROL_PER_COL) - coupled_result
        flat_values = flat_values + jnp.einsum('kij,kj->ki', block_inverse, residual_row_values, precision=highest)
        displacement_field = flat_values.reshape(SHELL_PATCHES * COLUMN_BLOCKS, 3, CONTROL_PER_COL)
        evaluated = jnp.einsum('kac,nqc->knaq', displacement_field, basis_values_table, precision=highest)
        evaluated = evaluated.reshape(SHELL_PATCHES * COLUMN_BLOCKS * PATTERN_COUNT, 3, QUAD_POINTS)
        interface = evaluated[group_code]
    return displacement_field, interface
```

```python
import functools

import jax
import jax.numpy as jnp
from jax import lax
from jax.experimental import pallas as pl
from jax.experimental.pallas import tpu as pltpu
from jax.sharding import PartitionSpec as P

F32, BF16, I32 = jnp.float32, jnp.bfloat16, jnp.int32
NT = (((1,), (1,)), ((), ()))
NN = (((1,), (0,)), ((), ()))
PART_W = ((0, 1, 2), (3, 4, 5), (6, 7))
REST = ((0, 4), (4, 8), (8, 11))
FIRST = ((0, 1), (1, 2), (2, 3))


def split(value):
    high = value.astype(BF16)
    low = (value - high.astype(F32)).astype(BF16)
    return high, low


def dot(a, b, dims=NN):
    return lax.dot_general(a, b, dims, preferred_element_type=F32)


def kernel(
    n,
    base_h,
    mass_h,
    prev_h,
    route_ref,
    pattern_ref,
    column_ref,
    table_h,
    stiff_h,
    srow_ref,
    scol_ref,
    inverse_h,
    start_ref,
    out_u,
    out_i,
    base_v,
    mass_v,
    prev_v,
    table_v,
    stiff_v,
    inverse_v,
    stiff_hi,
    stiff_lo,
    inverse_hi,
    inverse_lo,
    nn_w,
    nt_w,
    nt_lo,
    codes,
    pmask,
    scatter_hot,
    gather_hot,
    d_first,
    d_rest,
    c_first,
    c_rest,
    r1_first,
    r1_rest,
    f_first,
    f_rest,
    r2_first,
    r2_rest,
    g_first,
    g_rest,
    r3_first,
    r3_rest,
    cpl_out,
    cpl_in,
    rows_s,
    wide_s,
    gather3,
    field,
    load_sem,
    core_send,
    core_recv,
    axis_send,
    axis_recv,
    cpl_send,
    cpl_recv,
    back_send,
    back_recv,
    home_send,
    home_recv,
):
    fluid, x = lax.axis_index("fluid"), lax.axis_index("shell")
    core = lax.rem(fluid, 2)
    y = lax.rem(lax.div(fluid, 2), n)
    z = lax.div(fluid, 2 * n)
    cols = 4
    half, rows1, rows2 = n * n * n * cols, n * n * cols, n * cols
    blocks = mass_v.shape[0]
    patterns = table_v.shape[0]
    points = table_v.shape[1]
    keys = 2 * half

    def at(axis, step):
        if axis == 0:
            return (fluid, lax.rem(x + step, n))
        if axis == 1:
            return ((z * n + lax.rem(y + step, n)) * 2 + core, x)
        return ((lax.rem(z + step, n) * n + y) * 2 + core, x)

    sibling = (fluid + 1 - 2 * core, x)
    place = (x, y, z)
    axes = ((0, 1, 2), (1, 2, 0), (2, 0, 1))
    MESH = pl.DeviceIdType.MESH

    loads = [
        pltpu.make_async_copy(src, dst, load_sem.at[i])
        for i, (src, dst) in enumerate(
            (
                (mass_h, mass_v),
                (prev_h, prev_v),
                (base_h, base_v),
                (table_h, table_v),
                (stiff_h, stiff_v),
                (inverse_h, inverse_v),
            )
        )
    ]
    for copy in loads:
        copy.start()

    barrier = pltpu.get_barrier_semaphore()
    partners = [sibling] + [at(axis, step) for axis in range(3) for step in range(1, n)]
    for partner in partners:
        pl.semaphore_signal(barrier, inc=1, device_id=partner, device_id_type=MESH)

    route, column, pattern = route_ref[...], column_ref[...], pattern_ref[...]
    bits = n.bit_length() - 1
    px = route & (n - 1)
    pcore = (route >> bits) & 1
    py = (route >> (bits + 1)) & (n - 1)
    pz = route >> (2 * bits + 1)
    where_is = (px, py, pz)
    code = [
        (((pcore * n + where_is[a]) * n + where_is[b]) * n + where_is[c]) * cols + column
        for a, b, c in axes
    ]
    codes[...] = jnp.zeros_like(codes)
    for part in range(3):
        codes[part : part + 1, :] = code[part].astype(F32)
    codes[3:4, :] = pattern.astype(F32)
    flipped = codes[...].T
    pattern_col = flipped[:, 3:4]
    for p in range(patterns):
        pmask[p] = jnp.broadcast_to(jnp.where(pattern_col == p, 1.0, 0.0), (blocks, points)).astype(BF16)
    sub = lax.broadcasted_iota(I32, (keys, blocks), 0)
    for part in range(3):
        scatter_hot[part] = jnp.where(sub == code[part], 1.0, 0.0).astype(BF16)

    loads[0].wait()
    high, low = split(mass_v[...])
    for part in range(3):
        for j, p in enumerate(PART_W[part]):
            masked = jnp.concatenate([high * pmask[p], low * pmask[p]], axis=1)
            summed = dot(scatter_hot[part], masked)
            d_rest[REST[part][0] + 1 + j] = summed[:, :points] + summed[:, points:]

    loads[3].wait()
    for p in range(patterns):
        th, tl = split(table_v[p])
        spot = slice(p * points, (p + 1) * points)
        nn_w[spot, :points] = th
        nn_w[spot, points:] = tl
        nt_w[spot, :points] = th
        nt_w[spot, points:] = th
        nt_lo[spot, :] = tl

    def project(value):
        vh, vl = split(value)
        both = None
        for v in (vh, vl):
            wide = jnp.concatenate([v * pmask[p] for p in range(patterns)], axis=1)
            got = dot(wide, nn_w[...])
            both = got if both is None else both + got
        ph, pl_ = split(both[:, :points] + both[:, points:])
        return jnp.concatenate([ph, pl_], axis=1)

    loads[1].wait()
    loads[2].wait()
    for part in range(3):
        force = base_v[part] - mass_v[...] * prev_v[part]
        summed = dot(scatter_hot[part], project(force))
        d_first[part] = summed[:, :points] + summed[:, points:]
    pl.semaphore_wait(barrier, len(partners))
    other = (1 - core) * half
    mine = core * half

    def to_sibling(group, source, target):
        return pltpu.make_async_remote_copy(
            src_ref=source.at[:, pl.ds(other, half), :],
            dst_ref=target,
            send_sem=core_send.at[group],
            recv_sem=core_recv.at[group],
            device_id=sibling,
            device_id_type=MESH,
        )

    core_copies = [to_sibling(0, d_first, c_first), to_sibling(1, d_rest, c_rest)]
    core_copies[0].start()
    for part in range(3):
        summed = dot(scatter_hot[part], project(base_v[part]))
        d_rest[REST[part][0]] = summed[:, :points] + summed[:, points:]
    core_copies[1].start()

    loads[4].wait()
    for i in range(stiff_v.shape[0]):
        stiff_hi[i], stiff_lo[i] = split(stiff_v[i])

    def stacked(value):
        vh, vl = split(value)
        vh, vl = vh.astype(F32), vl.astype(F32)
        return jnp.concatenate([vh, vl, jnp.zeros((8, value.shape[1]), F32)], axis=0).astype(BF16)

    width = 3 * points
    group_rows = n * cols

    def couple(value, turn):
        lhs = stacked(value)
        total = jnp.zeros((group_rows, width), F32)
        row_at = lax.broadcasted_iota(I32, (group_rows, width), 0)
        col_at = lax.broadcasted_iota(I32, (cols, width), 0)
        for i in range(stiff_v.shape[0]):
            a = dot(lhs, stiff_hi[i], NT)
            b = dot(lhs, stiff_lo[i], NT)
            every = a[0:cols] + a[cols : 2 * cols] + b[0:cols]
            picked = jnp.sum(jnp.where(col_at == scol_ref[i], every, 0.0), axis=0, keepdims=True)
            total = total + jnp.where(row_at == srow_ref[i], picked, 0.0)
        for s in range(n):
            cpl_out[turn, s] = total[s * cols : (s + 1) * cols]
        copies = []
        for step in range(1, n):
            copies.append(
                pltpu.make_async_remote_copy(
                    src_ref=cpl_out.at[turn, lax.rem(x + step, n)],
                    dst_ref=cpl_in.at[turn, step - 1],
                    send_sem=cpl_send.at[turn, step - 1],
                    recv_sem=cpl_recv.at[turn, step - 1],
                    device_id=at(0, step),
                    device_id_type=MESH,
                )
            )
            copies[-1].start()
        return copies

    def coupled(turn, copies):
        total = cpl_out[turn, x]
        for step in range(1, n):
            copies[step - 1].wait_recv()
            total = total + cpl_in[turn, step - 1]
        return total

    field0 = jnp.concatenate([start_ref[c] for c in range(3)], axis=1)
    cpl_copies0 = couple(field0, 0)

    def phase_copies(group, phase, source, target, size):
        spans = (FIRST, REST)[group]
        copies = []
        for step in range(1, n):
            for part in range(3):
                axis = axes[part][phase]
                low_t, high_t = spans[part]
                to = lax.rem(place[axis] + step, n)
                if phase < 2:
                    src = source.at[low_t:high_t, pl.ds(pl.multiple_of(to * size, 8), size), :]
                else:
                    src = source.at[low_t:high_t, to]
                copies.append(
                    pltpu.make_async_remote_copy(
                        src_ref=src,
                        dst_ref=target.at[step - 1, low_t:high_t],
                        send_sem=axis_send.at[group, phase, part * (n - 1) + step - 1],
                        recv_sem=axis_recv.at[group, phase, part * (n - 1) + step - 1],
                        device_id=at(axis, step),
                        device_id_type=MESH,
                    )
                )
                copies[-1].start()
        return copies

    def phase_sum(group, phase, source, target, size, copies, put):
        for copy in copies:
            copy.wait_recv()
        for part in range(3):
            own = place[axes[part][phase]]
            for t in range(*(FIRST, REST)[group][part]):
                if phase < 2:
                    total = source[t, pl.ds(pl.multiple_of(own * size, 8), size), :]
                else:
                    total = source[t, own]
                for step in range(1, n):
                    total = total + target[step - 1, t]
                put(t, total)

    d_all, c_all = (d_first, d_rest), (c_first, c_rest)
    r1_all, f_all = (r1_first, r1_rest), (f_first, f_rest)
    r2_all, g_all = (r2_first, r2_rest), (g_first, g_rest)
    r3_all = (r3_first, r3_rest)
    done = []

    def stage0(group):
        core_copies[group].wait_recv()
        for t in range(c_all[group].shape[0]):
            c_all[group][t] = c_all[group][t] + d_all[group][t, pl.ds(pl.multiple_of(mine, 8), half), :]
        copies = phase_copies(group, 0, c_all[group], r1_all[group], rows1)
        done.extend(copies)
        return copies

    def stage1(group, copies):
        def put(t, total):
            f_all[group][t] = total

        phase_sum(group, 0, c_all[group], r1_all[group], rows1, copies, put)
        copies = phase_copies(group, 1, f_all[group], r2_all[group], rows2)
        done.extend(copies)
        return copies

    def stage2(group, copies):
        def put(t, total):
            for s in range(n):
                g_all[group][t, s] = total[s * cols : (s + 1) * cols]

        phase_sum(group, 1, f_all[group], r2_all[group], rows2, copies, put)
        copies = phase_copies(group, 2, g_all[group], r3_all[group], cols)
        done.extend(copies)
        return copies

    def stage3(group, copies):
        ends = {}

        def put(t, total):
            ends[t] = total

        phase_sum(group, 2, g_all[group], r3_all[group], cols, copies, put)
        return ends

    first = stage0(0)
    rest = stage0(1)
    first = stage1(0, first)

    loads[5].wait()
    for i in range(cols):
        inverse_hi[i], inverse_lo[i] = split(inverse_v[i])
    lane = lax.broadcasted_iota(I32, (blocks, keys), 1).astype(F32)
    flipped = codes[...].T
    for part in range(3):
        gather_hot[part] = jnp.where(lane == flipped[:, part : part + 1], 1.0, 0.0).astype(BF16)

    first = stage2(0, first)

    def correct(residual):
        lhs = stacked(residual)
        total = jnp.zeros((cols, width), F32)
        col_at = lax.broadcasted_iota(I32, (cols, width), 0)
        for k in range(cols):
            a = dot(lhs, inverse_hi[k], NT)
            b = dot(lhs, inverse_lo[k], NT)
            total = total + jnp.where(col_at == k, a[0:cols] + a[cols : 2 * cols] + b[0:cols], 0.0)
        return total

    ends = stage3(0, first)
    load = jnp.concatenate([ends[c] for c in range(3)], axis=1)
    field1 = field0 + correct(load - coupled(0, cpl_copies0))
    cpl_copies1 = couple(field1, 1)
    rest = stage1(1, rest)

    rows_s[...] = jnp.zeros_like(rows_s)
    for c in range(3):
        rows_s[c * cols : (c + 1) * cols, :] = field1[:, c * points : (c + 1) * points]
    uh, ul = split(rows_s[...])
    spread = dot(jnp.concatenate([uh, ul], axis=1), nt_w[...], NT) + dot(uh, nt_lo[...], NT)

    rest = stage2(1, rest)
    ends = stage3(1, rest)
    wide_s[...] = jnp.zeros_like(wide_s)
    for part in range(3):
        for j, p in enumerate(PART_W[part]):
            for c in range(3):
                wide_s[c * cols : (c + 1) * cols, p * points : (p + 1) * points] = ends[REST[part][0] + 1 + j]
    eh, el = split(spread * wide_s[...])
    back = dot(eh, nn_w[...]) + dot(el, nn_w[...])
    rows_s[...] = back[:, :points] + back[:, points:]
    load = jnp.concatenate(
        [ends[REST[c][0]] - rows_s[c * cols : (c + 1) * cols, :] for c in range(3)], axis=1
    )
    field2 = field1 + correct(load - coupled(1, cpl_copies1))

    for c in range(3):
        out_u[c] = field2[:, c * points : (c + 1) * points]
        gather3[c, place[axes[c][2]]] = field2[:, c * points : (c + 1) * points]

    def back_copies(phase, view):
        copies = []
        for step in range(1, n):
            for c in range(3):
                copies.append(
                    pltpu.make_async_remote_copy(
                        src_ref=view(c),
                        dst_ref=view(c),
                        send_sem=back_send.at[phase, c * (n - 1) + step - 1],
                        recv_sem=back_recv.at[phase, c * (n - 1) + step - 1],
                        device_id=at(axes[c][phase], step),
                        device_id_type=MESH,
                    )
                )
                copies[-1].start()
        done.extend(copies)
        return copies

    copies = back_copies(2, lambda c: gather3.at[c, place[axes[c][2]]])
    for copy in copies:
        copy.wait_recv()
    offset1 = [mine + place[axes[c][0]] * rows1 for c in range(3)]
    offset2 = [offset1[c] + place[axes[c][1]] * rows2 for c in range(3)]
    for c in range(3):
        whole = jnp.concatenate([gather3[c, s] for s in range(n)], axis=0)
        field[c, pl.ds(pl.multiple_of(offset2[c], 8), rows2), :] = whole
    copies = back_copies(1, lambda c: field.at[c, pl.ds(pl.multiple_of(offset2[c], 8), rows2), :])
    for copy in copies:
        copy.wait_recv()
    copies = back_copies(0, lambda c: field.at[c, pl.ds(pl.multiple_of(offset1[c], 8), rows1), :])
    for copy in copies:
        copy.wait_recv()
    homes = []
    for c in range(3):
        view = field.at[c, pl.ds(pl.multiple_of(mine, 8), half), :]
        homes.append(
            pltpu.make_async_remote_copy(
                src_ref=view,
                dst_ref=view,
                send_sem=home_send.at[c],
                recv_sem=home_recv.at[c],
                device_id=sibling,
                device_id_type=MESH,
            )
        )
        homes[-1].start()

    flipped = codes[...].T
    pattern_col = flipped[:, 3:4]
    for c in range(3):
        homes[c].wait_recv()
        fh, fl = split(field[c])
        got = dot(gather_hot[c], jnp.concatenate([fh, fl], axis=1)).astype(BF16)
        acc = jnp.zeros((blocks, points), F32)
        for j in range(patterns // 2):
            spot = slice(2 * j * points, 2 * (j + 1) * points)
            pair = dot(got, nt_w[spot, :], NT) + dot(got[:, :points], nt_lo[spot, :], NT)
            acc = jnp.where(pattern_col == 2 * j, pair[:, :points], acc)
            acc = jnp.where(pattern_col == 2 * j + 1, pair[:, points:], acc)
        out_i[c] = acc

    for copy in core_copies + cpl_copies0 + cpl_copies1 + done + homes:
        copy.wait_send()


def on_device(
    n,
    traction_base,
    added_mass,
    interface_prev,
    patch_route,
    basis_pattern,
    column_block,
    basis_values_table,
    stiffness,
    stiff_row,
    stiff_col,
    block_inverse,
    previous_shell_displacement,
):
    blocks = added_mass.shape[0]
    patterns, points, _ = basis_values_table.shape
    width = 3 * points
    cols = 4
    half, rows1, rows2 = n * n * n * cols, n * n * cols, n * cols
    keys = 2 * half
    stiffs = stiffness.shape[0]
    f, r = 3, 11
    any_, vmem, smem = (pl.BlockSpec(memory_space=m) for m in (pl.ANY, pltpu.VMEM, pltpu.SMEM))
    V = pltpu.VMEM
    dma = pltpu.SemaphoreType.DMA
    out_u, out_i = pl.pallas_call(
        functools.partial(kernel, n),
        out_shape=(
            jax.ShapeDtypeStruct((3, cols, points), F32),
            jax.ShapeDtypeStruct((3, blocks, points), F32),
        ),
        in_specs=[any_, any_, any_, vmem, vmem, vmem, any_, any_, smem, smem, any_, vmem],
        out_specs=(vmem, vmem),
        scratch_shapes=[
            V((3, blocks, points), F32),
            V((blocks, points), F32),
            V((3, blocks, points), F32),
            V((patterns, points, points), F32),
            V((stiffs, width, width), F32),
            V((cols, width, width), F32),
            V((stiffs, width, width), BF16),
            V((stiffs, width, width), BF16),
            V((cols, width, width), BF16),
            V((cols, width, width), BF16),
            V((patterns * points, 2 * points), BF16),
            V((patterns * points, 2 * points), BF16),
            V((patterns * points, points), BF16),
            V((128, blocks), F32),
            V((patterns, blocks, points), BF16),
            V((3, keys, blocks), BF16),
            V((3, blocks, keys), BF16),
            V((f, keys, points), F32),
            V((r, keys, points), F32),
            V((f, half, points), F32),
            V((r, half, points), F32),
            V((n - 1, f, rows1, points), F32),
            V((n - 1, r, rows1, points), F32),
            V((f, rows1, points), F32),
            V((r, rows1, points), F32),
            V((n - 1, f, rows2, points), F32),
            V((n - 1, r, rows2, points), F32),
            V((f, n, cols, points), F32),
            V((r, n, cols, points), F32),
            V((n - 1, f, cols, points), F32),
            V((n - 1, r, cols, points), F32),
            V((2, n, cols, width), F32),
            V((2, n - 1, cols, width), F32),
            V((16, points), F32),
            V((16, patterns * points), F32),
            V((3, n, cols, points), F32),
            V((3, keys, points), F32),
            dma((6,)),
            dma((2,)),
            dma((2,)),
            dma((2, 3, 3 * (n - 1))),
            dma((2, 3, 3 * (n - 1))),
            dma((2, n - 1)),
            dma((2, n - 1)),
            dma((3, 3 * (n - 1))),
            dma((3, 3 * (n - 1))),
            dma((3,)),
            dma((3,)),
        ],
        compiler_params=pltpu.CompilerParams(
            collective_id=0, has_side_effects=True, vmem_limit_bytes=62 * 1024 * 1024
        ),
    )(
        jnp.transpose(traction_base, (1, 0, 2)),
        added_mass,
        jnp.transpose(interface_prev, (1, 0, 2)),
        patch_route.reshape(1, blocks),
        basis_pattern.reshape(1, blocks),
        column_block.reshape(1, blocks),
        basis_values_table,
        stiffness,
        stiff_row,
        stiff_col,
        block_inverse,
        jnp.transpose(previous_shell_displacement, (1, 0, 2)),
    )
    return jnp.transpose(out_u, (1, 0, 2)), jnp.transpose(out_i, (1, 0, 2))


def solution(mesh):
    both = P(("fluid", "shell"))
    n = mesh.shape["shell"]
    return jax.shard_map(
        functools.partial(on_device, n),
        mesh=mesh,
        in_specs=(
            P(("fluid", "shell"), None, None),
            P(("fluid", "shell"), None),
            P(("fluid", "shell"), None, None),
            P(("fluid", "shell"), None),
            both,
            both,
            P(),
            P(("fluid", "shell"), None, None),
            both,
            both,
            P(("fluid", "shell"), None, None),
            P(("fluid", "shell"), None, None),
        ),
        out_specs=(P(("fluid", "shell"), None, None), P(("fluid", "shell"), None, None)),
        check_vma=False,
    )
```

```python
import functools

import jax
import jax.numpy as jnp
from jax import lax
from jax.experimental import pallas as pl
from jax.experimental.pallas import tpu as pltpu
from jax.sharding import PartitionSpec as P

F32, BF16, I32 = jnp.float32, jnp.bfloat16, jnp.int32
NT = (((1,), (1,)), ((), ()))
NN = (((1,), (0,)), ((), ()))
PART_W = ((0, 1, 2), (3, 4, 5), (6, 7))


def split(value):
    high = value.astype(BF16)
    low = (value - high.astype(F32)).astype(BF16)
    return high, low


def dot(a, b, dims=NN):
    return lax.dot_general(a, b, dims, preferred_element_type=F32)


def kernel(
    n,
    base_h,
    mass_h,
    prev_h,
    route_h,
    pattern_h,
    column_h,
    table_h,
    stiff_h,
    srow_h,
    scol_h,
    inverse_h,
    start_h,
    out_u,
    out_i,
    base_v,
    mass_v,
    prev_v,
    route_v,
    pattern_v,
    column_v,
    table_v,
    stiff_v,
    srow_s,
    scol_s,
    inverse_v,
    start_v,
    stiff_hi,
    stiff_lo,
    inverse_hi,
    inverse_lo,
    nn_w,
    nt_w,
    nt_lo,
    codes,
    pmask,
    scatter_hot,
    gather_hot,
    d_all,
    c_all,
    r1_all,
    f_first,
    f_rest,
    r2_first,
    r2_rest,
    cpl_out,
    cpl_in,
    rows_s,
    wide_s,
    field,
    load_sem,
    core_send,
    core_recv,
    axis_send,
    axis_recv,
    plane_send,
    plane_recv,
    cpl_send,
    cpl_recv,
    back_send,
    back_recv,
    home_send,
    home_recv,
):
    fluid, x = lax.axis_index("fluid"), lax.axis_index("shell")
    core = lax.rem(fluid, 2)
    y = lax.rem(lax.div(fluid, 2), n)
    z = lax.div(fluid, 2 * n)
    cols = 4
    half, rows1 = n * n * n * cols, n * n * cols
    blocks = mass_v.shape[0]
    patterns = table_v.shape[0]
    points = table_v.shape[1]
    keys = 2 * half
    chips = n * n * n
    width = 3 * points
    place = (x, y, z)
    axes = ((0, 1, 2), (1, 2, 0), (2, 0, 1))
    MESH = pl.DeviceIdType.MESH

    def shifted(dx, dy, dz):
        to_x, to_y, to_z = lax.rem(x + dx, n), lax.rem(y + dy, n), lax.rem(z + dz, n)
        return ((to_z * n + to_y) * 2 + core, to_x)

    def far(offsets):
        return sum(min(v, n - v) for v in offsets)

    everywhere = sorted(
        ((a, b, c) for c in range(n) for b in range(n) for a in range(n) if a or b or c),
        key=far,
        reverse=True,
    )
    sibling = (fluid + 1 - 2 * core, x)

    sources = (route_h, pattern_h, column_h, mass_h, prev_h, base_h, table_h, start_h, srow_h, scol_h, stiff_h, inverse_h)
    places = (route_v, pattern_v, column_v, mass_v, prev_v, base_v, table_v, start_v, srow_s, scol_s, stiff_v, inverse_v)
    names = ("route", "pattern", "column", "mass", "prev", "base", "table", "start", "srow", "scol", "stiff", "inverse")
    loads = {}
    for i, (name, src, dst) in enumerate(zip(names, sources, places)):
        loads[name] = pltpu.make_async_copy(src, dst, load_sem.at[i])
        loads[name].start()

    barrier = pltpu.get_barrier_semaphore()
    partners = [sibling] + [shifted(*o) for o in everywhere]
    for partner in partners:
        pl.semaphore_signal(barrier, inc=1, device_id=partner, device_id_type=MESH)

    for name in ("route", "pattern", "column"):
        loads[name].wait()
    route, column, pattern = route_v[...], column_v[...], pattern_v[...]
    bits = n.bit_length() - 1
    px = route & (n - 1)
    pcore = (route >> bits) & 1
    py = (route >> (bits + 1)) & (n - 1)
    pz = route >> (2 * bits + 1)
    where_is = (px, py, pz)
    code = [
        (((pcore * n + where_is[a]) * n + where_is[b]) * n + where_is[c]) * cols + column
        for a, b, c in axes
    ]
    codes[...] = jnp.zeros_like(codes)
    codes[0:1, :] = ((((pcore * n + pz) * n + py) * n + px) * cols + column).astype(F32)
    codes[1:2, :] = pattern.astype(F32)
    flipped = codes[...].T
    for p in range(patterns):
        pmask[p] = jnp.broadcast_to(jnp.where(flipped[:, 1:2] == p, 1.0, 0.0), (blocks, points)).astype(BF16)
    sub = lax.broadcasted_iota(I32, (keys, blocks), 0)
    for part in range(3):
        scatter_hot[part] = jnp.where(sub == code[part], 1.0, 0.0).astype(BF16)

    loads["table"].wait()
    for p in range(patterns):
        th, tl = split(table_v[p])
        spot = slice(p * points, (p + 1) * points)
        nn_w[spot, :points] = th
        nn_w[spot, points:] = tl
        nt_w[spot, :points] = th
        nt_w[spot, points:] = th
        nt_lo[spot, :] = tl

    def folded(pair):
        return pair[:, :points] + pair[:, points:]

    def project(values):
        parts = []
        for value in values:
            parts.extend(split(value))
        wide = jnp.concatenate(
            [jnp.concatenate([v * pmask[p] for v in parts], axis=0) for p in range(patterns)], axis=1
        )
        got = dot(wide, nn_w[...])
        ends = []
        for i in range(3):
            both = got[2 * i * blocks : (2 * i + 1) * blocks] + got[(2 * i + 1) * blocks : (2 * i + 2) * blocks]
            ends.append(jnp.concatenate(split(folded(both)), axis=1))
        return ends

    GROUPS = ((0, 3), (3, 3 + patterns), (3 + patterns, 6 + patterns))
    SPANS = (
        ((0, 1), (1, 2), (2, 3)),
        ((3, 6), (6, 9), (9, 11)),
        ((11, 12), (12, 13), (13, 14)),
    )
    other = pl.multiple_of((1 - core) * half, 8)
    mine = pl.multiple_of(core * half, 8)

    def to_sibling(group):
        low_t, high_t = GROUPS[group]
        copy = pltpu.make_async_remote_copy(
            src_ref=d_all.at[low_t:high_t, pl.ds(other, half), :],
            dst_ref=c_all.at[low_t:high_t],
            send_sem=core_send.at[group],
            recv_sem=core_recv.at[group],
            device_id=sibling,
            device_id_type=MESH,
        )
        copy.start()
        return copy

    done = []

    def stage0(group, copy):
        copy.wait_recv()
        done.append(copy)
        for t in range(*GROUPS[group]):
            c_all[t] = c_all[t] + d_all[t, pl.ds(mine, half), :]
        copies = []
        for step in range(1, n):
            for part in range(3):
                axis = axes[part][0]
                low_t, high_t = SPANS[group][part]
                to = lax.rem(place[axis] + step, n)
                slot = part * (n - 1) + step - 1
                target = shifted(*[step if a == axis else 0 for a in range(3)])
                copies.append(
                    pltpu.make_async_remote_copy(
                        src_ref=c_all.at[low_t:high_t, pl.ds(pl.multiple_of(to * rows1, 8), rows1), :],
                        dst_ref=r1_all.at[step - 1, low_t:high_t],
                        send_sem=axis_send.at[group, slot],
                        recv_sem=axis_recv.at[group, slot],
                        device_id=target,
                        device_id_type=MESH,
                    )
                )
                copies[-1].start()
        done.extend(copies)
        return copies

    loads["mass"].wait()
    loads["prev"].wait()
    loads["base"].wait()
    force = project([base_v[c] - mass_v[...] * prev_v[c] for c in range(3)])
    for c in range(3):
        d_all[c] = folded(dot(scatter_hot[c], force[c]))
    pl.semaphore_wait(barrier, len(partners))
    core0 = to_sibling(0)

    high, low = split(mass_v[...])
    for part in range(3):
        for j, p in enumerate(PART_W[part]):
            masked = jnp.concatenate([high * pmask[p], low * pmask[p]], axis=1)
            d_all[SPANS[1][part][0] + j] = folded(dot(scatter_hot[part], masked))
    core1 = to_sibling(1)
    axis0 = stage0(0, core0)
    load = project([base_v[c] for c in range(3)])
    for c in range(3):
        d_all[SPANS[2][c][0]] = folded(dot(scatter_hot[c], load[c]))
    core2 = to_sibling(2)
    axis1 = stage0(1, core1)
    axis2 = stage0(2, core2)

    loads["stiff"].wait()
    loads["srow"].wait()
    loads["scol"].wait()
    loads["start"].wait()
    for i in range(stiff_v.shape[0]):
        stiff_hi[i], stiff_lo[i] = split(stiff_v[i])

    def stacked(value):
        vh, vl = split(value)
        vh, vl = vh.astype(F32), vl.astype(F32)
        return jnp.concatenate([vh, vl, jnp.zeros((8, value.shape[1]), F32)], axis=0).astype(BF16)

    group_rows = n * cols

    def couple(value, turn):
        lhs = stacked(value)
        total = jnp.zeros((group_rows, width), F32)
        row_at = lax.broadcasted_iota(I32, (group_rows, width), 0)
        col_at = lax.broadcasted_iota(I32, (cols, width), 0)
        for i in range(stiff_v.shape[0]):
            a = dot(lhs, stiff_hi[i], NT)
            b = dot(lhs, stiff_lo[i], NT)
            every = a[0:cols] + a[cols : 2 * cols] + b[0:cols]
            picked = jnp.sum(jnp.where(col_at == scol_s[i], every, 0.0), axis=0, keepdims=True)
            total = total + jnp.where(row_at == srow_s[i], picked, 0.0)
        for s in range(n):
            cpl_out[turn, s] = total[s * cols : (s + 1) * cols]
        copies = []
        for step in range(1, n):
            copies.append(
                pltpu.make_async_remote_copy(
                    src_ref=cpl_out.at[turn, lax.rem(x + step, n)],
                    dst_ref=cpl_in.at[turn, step - 1],
                    send_sem=cpl_send.at[turn, step - 1],
                    recv_sem=cpl_recv.at[turn, step - 1],
                    device_id=shifted(step, 0, 0),
                    device_id_type=MESH,
                )
            )
            copies[-1].start()
        done.extend(copies)
        return copies

    def coupled(turn, copies):
        total = cpl_out[turn, x]
        for step in range(1, n):
            copies[step - 1].wait_recv()
            total = total + cpl_in[turn, step - 1]
        return total

    field0 = jnp.concatenate([start_v[c] for c in range(3)], axis=1)
    cpl_copies0 = couple(field0, 0)

    flat = sorted(((a, b) for a in range(n) for b in range(n) if a or b), key=far, reverse=True)

    def stage1(groups, copies, f_ref):
        for copy in copies:
            copy.wait_recv()
        for part in range(3):
            own = pl.multiple_of(place[axes[part][0]] * rows1, 8)
            at = 0
            for group in groups:
                for t in range(*SPANS[group][part]):
                    total = c_all[t, pl.ds(own, rows1), :]
                    for step in range(1, n):
                        total = total + r1_all[step - 1, t]
                    for s in range(n * n):
                        f_ref[part, s, at] = total[s * cols : (s + 1) * cols]
                    at += 1

    def plane(kind, f_ref, r_ref, counts):
        for i, (da, db) in enumerate(flat):
            for part in range(3):
                _, a, b = axes[part]
                to = lax.rem(place[a] + da, n) * n + lax.rem(place[b] + db, n)
                step = [0, 0, 0]
                step[a], step[b] = da, db
                pltpu.make_async_remote_copy(
                    src_ref=f_ref.at[part, to, 0 : counts[part]],
                    dst_ref=r_ref[part].at[i],
                    send_sem=plane_send.at[kind, part],
                    recv_sem=plane_recv.at[kind, part],
                    device_id=shifted(*step),
                    device_id_type=MESH,
                ).start()

    def all_of(ref, send, recv):
        return pltpu.make_async_remote_copy(
            src_ref=ref, dst_ref=ref, send_sem=send, recv_sem=recv, device_id=sibling, device_id_type=MESH
        )

    def plane_end(kind, f_ref, r_ref, counts):
        ends = []
        for part in range(3):
            copy = all_of(r_ref[part], plane_send.at[kind, part], plane_recv.at[kind, part])
            copy.wait_recv()
            done.append(copy)
            _, a, b = axes[part]
            own = place[a] * n + place[b]
            rows = []
            for t in range(counts[part]):
                total = f_ref[part, own, t]
                for i in range(len(flat)):
                    total = total + r_ref[part][i, t]
                rows.append(total)
            ends.append(rows)
        return ends

    one, rest = (1, 1, 1), tuple(len(PART_W[part]) + 1 for part in range(3))
    stage1((0,), axis0, f_first)
    plane(0, f_first, r2_first, one)

    loads["inverse"].wait()
    for i in range(cols):
        inverse_hi[i], inverse_lo[i] = split(inverse_v[i])
    flipped = codes[...].T
    lane = lax.broadcasted_iota(I32, (blocks, keys), 1).astype(F32)
    gather_hot[...] = jnp.where(lane == flipped[:, 0:1], 1.0, 0.0).astype(BF16)

    def correct(residual):
        lhs = stacked(residual)
        total = jnp.zeros((cols, width), F32)
        col_at = lax.broadcasted_iota(I32, (cols, width), 0)
        for k in range(cols):
            a = dot(lhs, inverse_hi[k], NT)
            b = dot(lhs, inverse_lo[k], NT)
            total = total + jnp.where(col_at == k, a[0:cols] + a[cols : 2 * cols] + b[0:cols], 0.0)
        return total

    stage1((2, 1), axis1 + axis2, f_rest)
    plane(1, f_rest, r2_rest, rest)
    ends = plane_end(0, f_first, r2_first, one)
    load = jnp.concatenate([ends[c][0] for c in range(3)], axis=1)
    field1 = field0 + correct(load - coupled(0, cpl_copies0))
    cpl_copies1 = couple(field1, 1)

    rows_s[...] = jnp.zeros_like(rows_s)
    for c in range(3):
        rows_s[c * cols : (c + 1) * cols, :] = field1[:, c * points : (c + 1) * points]
    uh, ul = split(rows_s[...])
    spread = dot(jnp.concatenate([uh, ul], axis=1), nt_w[...], NT) + dot(uh, nt_lo[...], NT)

    ends = plane_end(1, f_rest, r2_rest, rest)
    wide_s[...] = jnp.zeros_like(wide_s)
    for part in range(3):
        for j, p in enumerate(PART_W[part]):
            for c in range(3):
                wide_s[c * cols : (c + 1) * cols, p * points : (p + 1) * points] = ends[part][1 + j]
    eh, el = split(spread * wide_s[...])
    rows_s[...] = folded(dot(eh, nn_w[...]) + dot(el, nn_w[...]))
    load = jnp.concatenate([ends[c][0] - rows_s[c * cols : (c + 1) * cols, :] for c in range(3)], axis=1)
    field2 = field1 + correct(load - coupled(1, cpl_copies1))

    for c in range(3):
        out_u[c] = field2[:, c * points : (c + 1) * points]
    chip = (z * n + y) * n + x
    home = pl.multiple_of(core * chips, 8)
    field[home + chip] = field2
    for offsets in everywhere:
        pltpu.make_async_remote_copy(
            src_ref=field.at[home + chip],
            dst_ref=field.at[home + chip],
            send_sem=back_send,
            recv_sem=back_recv,
            device_id=shifted(*offsets),
            device_id_type=MESH,
        ).start()
    copy = all_of(field.at[pl.ds(home, chips - 1)], back_send, back_recv)
    copy.wait_recv()
    done.append(copy)
    view = field.at[pl.ds(home, chips)]
    copy = pltpu.make_async_remote_copy(
        src_ref=view,
        dst_ref=view,
        send_sem=home_send,
        recv_sem=home_recv,
        device_id=sibling,
        device_id_type=MESH,
    )
    copy.start()
    copy.wait_recv()
    done.append(copy)

    flipped = codes[...].T
    pattern_col = flipped[:, 1:2]
    fh, fl = split(field[...].reshape(keys, width))
    rows = []
    for c in range(3):
        spot = slice(c * points, (c + 1) * points)
        rows.append(dot(gather_hot[...], jnp.concatenate([fh[:, spot], fl[:, spot]], axis=1)).astype(BF16))
    got = jnp.concatenate(rows, axis=0)
    acc = [jnp.zeros((blocks, points), F32) for _ in range(3)]
    for j in range(patterns // 2):
        spot = slice(2 * j * points, 2 * (j + 1) * points)
        pair = dot(got, nt_w[spot, :], NT) + dot(got[:, :points], nt_lo[spot, :], NT)
        for c in range(3):
            mid = pair[c * blocks : (c + 1) * blocks]
            acc[c] = jnp.where(pattern_col == 2 * j, mid[:, :points], acc[c])
            acc[c] = jnp.where(pattern_col == 2 * j + 1, mid[:, points:], acc[c])
    for c in range(3):
        out_i[c] = acc[c]

    for copy in done:
        copy.wait_send()


def on_device(
    n,
    traction_base,
    added_mass,
    interface_prev,
    patch_route,
    basis_pattern,
    column_block,
    basis_values_table,
    stiffness,
    stiff_row,
    stiff_col,
    block_inverse,
    previous_shell_displacement,
):
    blocks = added_mass.shape[0]
    patterns, points, _ = basis_values_table.shape
    width = 3 * points
    cols = 4
    chips = n * n * n
    half, rows1 = chips * cols, n * n * cols
    keys = 2 * half
    stiffs = stiffness.shape[0]
    total = 6 + patterns
    any_, vmem = (pl.BlockSpec(memory_space=m) for m in (pl.ANY, pltpu.VMEM))
    V = pltpu.VMEM
    dma = pltpu.SemaphoreType.DMA
    rest = [len(p) + 1 for p in PART_W]
    out_u, out_i = pl.pallas_call(
        functools.partial(kernel, n),
        out_shape=(
            jax.ShapeDtypeStruct((3, cols, points), F32),
            jax.ShapeDtypeStruct((3, blocks, points), F32),
        ),
        in_specs=[any_] * 12,
        out_specs=(vmem, vmem),
        scratch_shapes=[
            V((3, blocks, points), F32),
            V((blocks, points), F32),
            V((3, blocks, points), F32),
            V((1, blocks), I32),
            V((1, blocks), I32),
            V((1, blocks), I32),
            V((patterns, points, points), F32),
            V((stiffs, width, width), F32),
            pltpu.SMEM((stiffs,), I32),
            pltpu.SMEM((stiffs,), I32),
            V((cols, width, width), F32),
            V((3, cols, points), F32),
            V((stiffs, width, width), BF16),
            V((stiffs, width, width), BF16),
            V((cols, width, width), BF16),
            V((cols, width, width), BF16),
            V((patterns * points, 2 * points), BF16),
            V((patterns * points, 2 * points), BF16),
            V((patterns * points, points), BF16),
            V((128, blocks), F32),
            V((patterns, blocks, points), BF16),
            V((3, keys, blocks), BF16),
            V((blocks, keys), BF16),
            V((total, keys, points), F32),
            V((total, half, points), F32),
            V((n - 1, total, rows1, points), F32),
            V((3, n * n, 1, cols, points), F32),
            V((3, n * n, max(rest), cols, points), F32),
            [V((n * n - 1, 1, cols, points), F32) for _ in range(3)],
            [V((n * n - 1, rest[part], cols, points), F32) for part in range(3)],
            V((2, n, cols, width), F32),
            V((2, n - 1, cols, width), F32),
            V((16, points), F32),
            V((16, patterns * points), F32),
            V((2 * chips, cols, width), F32),
            dma((12,)),
            dma((3,)),
            dma((3,)),
            dma((3, 3 * (n - 1))),
            dma((3, 3 * (n - 1))),
            dma((2, 3)),
            dma((2, 3)),
            dma((2, n - 1)),
            dma((2, n - 1)),
            dma,
            dma,
            dma,
            dma,
        ],
        compiler_params=pltpu.CompilerParams(
            collective_id=0, has_side_effects=True, vmem_limit_bytes=62 * 1024 * 1024
        ),
    )(
        jnp.transpose(traction_base, (1, 0, 2)),
        added_mass,
        jnp.transpose(interface_prev, (1, 0, 2)),
        patch_route.reshape(1, blocks),
        basis_pattern.reshape(1, blocks),
        column_block.reshape(1, blocks),
        basis_values_table,
        stiffness,
        stiff_row,
        stiff_col,
        block_inverse,
        jnp.transpose(previous_shell_displacement, (1, 0, 2)),
    )
    return jnp.transpose(out_u, (1, 0, 2)), jnp.transpose(out_i, (1, 0, 2))


def solution(mesh):
    both = P(("fluid", "shell"))
    n = mesh.shape["shell"]
    return jax.shard_map(
        functools.partial(on_device, n),
        mesh=mesh,
        in_specs=(
            P(("fluid", "shell"), None, None),
            P(("fluid", "shell"), None),
            P(("fluid", "shell"), None, None),
            P(("fluid", "shell"), None),
            both,
            both,
            P(),
            P(("fluid", "shell"), None, None),
            both,
            both,
            P(("fluid", "shell"), None, None),
            P(("fluid", "shell"), None, None),
        ),
        out_specs=(P(("fluid", "shell"), None, None), P(("fluid", "shell"), None, None)),
        check_vma=False,
    )
```

```python
import functools

import jax
import jax.numpy as jnp
from jax import lax
from jax.experimental import pallas as pl
from jax.experimental.pallas import tpu as pltpu
from jax.sharding import PartitionSpec as P

F32, BF16, I32 = jnp.float32, jnp.bfloat16, jnp.int32
NT = (((1,), (1,)), ((), ()))
NN = (((1,), (0,)), ((), ()))
def split(value):
    high = value.astype(BF16)
    low = (value - high.astype(F32)).astype(BF16)
    return high, low


def dot(a, b, dims=NN):
    return lax.dot_general(a, b, dims, preferred_element_type=F32)


def kernel(
    n,
    base_h,
    mass_h,
    prev_h,
    route_h,
    pattern_h,
    column_h,
    table_h,
    stiff_h,
    srow_h,
    scol_h,
    inverse_h,
    start_h,
    out_u,
    out_i,
    base_v,
    mass_v,
    prev_v,
    route_v,
    pattern_v,
    column_v,
    table_v,
    stiff_v,
    srow_s,
    scol_s,
    inverse_v,
    start_v,
    stiff_hi,
    stiff_lo,
    inverse_hi,
    inverse_lo,
    nn_w,
    nt_w,
    nt_lo,
    codes,
    pmask,
    scatter_hot,
    gather_hot,
    d_all,
    c_all,
    r1_all,
    f_all,
    r2_all,
    slot_own,
    slot_out,
    slot_in,
    cpl_out,
    cpl_in,
    rows_s,
    wide_s,
    field,
    load_sem,
    core_send,
    core_recv,
    axis_send,
    axis_recv,
    plane_send,
    plane_recv,
    slot_send,
    slot_recv,
    cpl_send,
    cpl_recv,
    back_send,
    back_recv,
    home_send,
    home_recv,
):
    fluid, x = lax.axis_index("fluid"), lax.axis_index("shell")
    core = lax.rem(fluid, 2)
    y = lax.rem(lax.div(fluid, 2), n)
    z = lax.div(fluid, 2 * n)
    cols = 4
    half, rows1 = n * n * n * cols, n * n * cols
    blocks = mass_v.shape[0]
    patterns = table_v.shape[0]
    points = table_v.shape[1]
    keys = 2 * half
    chips = n * n * n
    width = 3 * points
    cap = 4
    tags = patterns * cols
    place = (x, y, z)
    axes = ((0, 1, 2), (1, 2, 0), (2, 0, 1))
    MESH = pl.DeviceIdType.MESH

    def shifted(dx, dy, dz):
        to_x, to_y, to_z = lax.rem(x + dx, n), lax.rem(y + dy, n), lax.rem(z + dz, n)
        return ((to_z * n + to_y) * 2 + core, to_x)

    def far(offsets):
        return sum(min(v, n - v) for v in offsets)

    everywhere = sorted(
        ((a, b, c) for c in range(n) for b in range(n) for a in range(n) if a or b or c),
        key=far,
        reverse=True,
    )
    sibling = (fluid + 1 - 2 * core, x)

    sources = (route_h, pattern_h, column_h, mass_h, prev_h, base_h, table_h, start_h, srow_h, scol_h, stiff_h, inverse_h)
    places = (route_v, pattern_v, column_v, mass_v, prev_v, base_v, table_v, start_v, srow_s, scol_s, stiff_v, inverse_v)
    names = ("route", "pattern", "column", "mass", "prev", "base", "table", "start", "srow", "scol", "stiff", "inverse")
    loads = {}
    for i, (name, src, dst) in enumerate(zip(names, sources, places)):
        loads[name] = pltpu.make_async_copy(src, dst, load_sem.at[i])
        loads[name].start()

    barrier = pltpu.get_barrier_semaphore()
    partners = [sibling] + [shifted(*o) for o in everywhere]
    for partner in partners:
        pl.semaphore_signal(barrier, inc=1, device_id=partner, device_id_type=MESH)

    for name in ("route", "pattern", "column"):
        loads[name].wait()
    route, column, pattern = route_v[...], column_v[...], pattern_v[...]
    bits = n.bit_length() - 1
    px = route & (n - 1)
    pcore = (route >> bits) & 1
    py = (route >> (bits + 1)) & (n - 1)
    pz = route >> (2 * bits + 1)
    where_is = (px, py, pz)
    code = [
        (((pcore * n + where_is[a]) * n + where_is[b]) * n + where_is[c]) * cols + column
        for a, b, c in axes
    ]
    codes[...] = jnp.zeros_like(codes)
    codes[0:1, :] = ((((pcore * n + pz) * n + py) * n + px) * cols + column).astype(F32)
    codes[1:2, :] = pattern.astype(F32)
    codes[2:3, :] = (((pcore * n + pz) * n + py) * n + px).astype(F32)
    codes[3:4, :] = (pattern * cols + column).astype(F32)
    flipped = codes[...].T
    for p in range(patterns):
        pmask[p] = jnp.broadcast_to(jnp.where(flipped[:, 1:2] == p, 1.0, 0.0), (blocks, points)).astype(BF16)
    sub = lax.broadcasted_iota(I32, (keys, blocks), 0)
    for part in range(3):
        scatter_hot[part] = jnp.where(sub == code[part], 1.0, 0.0).astype(BF16)

    loads["table"].wait()
    for p in range(patterns):
        th, tl = split(table_v[p])
        spot = slice(p * points, (p + 1) * points)
        nn_w[spot, :points] = th
        nn_w[spot, points:] = tl
        nt_w[spot, :points] = th
        nt_w[spot, points:] = th
        nt_lo[spot, :] = tl

    def folded(pair):
        return pair[:, :points] + pair[:, points:]

    def project(values):
        parts = []
        for value in values:
            parts.extend(split(value))
        wide = jnp.concatenate(
            [jnp.concatenate([v * pmask[p] for v in parts], axis=0) for p in range(patterns)], axis=1
        )
        got = dot(wide, nn_w[...])
        ends = []
        for i in range(3):
            both = got[2 * i * blocks : (2 * i + 1) * blocks] + got[(2 * i + 1) * blocks : (2 * i + 2) * blocks]
            ends.append(jnp.concatenate(split(folded(both)), axis=1))
        return ends

    other = pl.multiple_of((1 - core) * half, 8)
    mine = pl.multiple_of(core * half, 8)

    def to_sibling(group):
        low_t, high_t = 3 * group, 3 * group + 3
        copy = pltpu.make_async_remote_copy(
            src_ref=d_all.at[low_t:high_t, pl.ds(other, half), :],
            dst_ref=c_all.at[low_t:high_t],
            send_sem=core_send.at[group],
            recv_sem=core_recv.at[group],
            device_id=sibling,
            device_id_type=MESH,
        )
        copy.start()
        return copy

    done = []

    def stage0(group, copy):
        copy.wait_recv()
        done.append(copy)
        for t in range(3 * group, 3 * group + 3):
            c_all[t] = c_all[t] + d_all[t, pl.ds(mine, half), :]
        copies = []
        for step in range(1, n):
            for part in range(3):
                axis = axes[part][0]
                t = 3 * group + part
                to = lax.rem(place[axis] + step, n)
                slot = part * (n - 1) + step - 1
                target = shifted(*[step if a == axis else 0 for a in range(3)])
                copies.append(
                    pltpu.make_async_remote_copy(
                        src_ref=c_all.at[t, pl.ds(pl.multiple_of(to * rows1, 8), rows1), :],
                        dst_ref=r1_all.at[step - 1, t],
                        send_sem=axis_send.at[group, slot],
                        recv_sem=axis_recv.at[group, slot],
                        device_id=target,
                        device_id_type=MESH,
                    )
                )
                copies[-1].start()
        done.extend(copies)
        return copies

    loads["mass"].wait()
    loads["prev"].wait()
    loads["base"].wait()
    force = project([base_v[c] - mass_v[...] * prev_v[c] for c in range(3)])
    for c in range(3):
        d_all[c] = folded(dot(scatter_hot[c], force[c]))
    pl.semaphore_wait(barrier, len(partners))
    core0 = to_sibling(0)

    owner_col = lax.broadcast_in_dim(flipped[:, 2:3], (blocks, blocks), (0, 1))
    same = owner_col == codes[2:3, :]
    down = lax.broadcasted_iota(I32, (blocks, blocks), 0)
    along = lax.broadcasted_iota(I32, (blocks, blocks), 1)
    slot_row = jnp.sum(jnp.where(same & (down < along), 1.0, 0.0), axis=0, keepdims=True)
    slot_col = jnp.sum(jnp.where(same & (along < down), 1.0, 0.0), axis=1, keepdims=True)
    owners = 2 * chips
    spot_of = slot_row * owners + codes[2:3, :]
    hot = jnp.where(lax.broadcasted_iota(I32, (cap * owners, blocks), 0).astype(F32) == spot_of, 1.0, 0.0).astype(BF16)
    slots = folded(dot(hot, jnp.concatenate(split(mass_v[...]), axis=1)))
    mark = slot_col * tags + flipped[:, 3:4]
    marked = jnp.where(lax.broadcasted_iota(I32, (blocks, points), 1).astype(F32) == mark, 1.0, 0.0).astype(BF16)
    owner_hot = jnp.where(lax.broadcasted_iota(I32, (owners, blocks), 0).astype(F32) == codes[2:3, :], 1.0, 0.0).astype(BF16)
    marks = dot(owner_hot, marked)
    for s in range(2):
        for j in range(cap):
            slot_own[s, :, j, :] = slots[j * owners + s * chips : j * owners + (s + 1) * chips]
        slot_own[s, :, cap, :] = marks[s * chips : (s + 1) * chips]
    slot_copy = pltpu.make_async_remote_copy(
        src_ref=slot_own.at[1 - core],
        dst_ref=slot_out.at[core],
        send_sem=core_send.at[2],
        recv_sem=core_recv.at[2],
        device_id=sibling,
        device_id_type=MESH,
    )
    slot_copy.start()
    slot_out[core] = slot_own[core]
    chip = (z * n + y) * n + x
    axis0 = stage0(0, core0)
    load = project([base_v[c] for c in range(3)])
    for c in range(3):
        d_all[3 + c] = folded(dot(scatter_hot[c], load[c]))
    core1 = to_sibling(1)
    slot_copy.wait_recv()
    done.append(slot_copy)
    slot_in[:, chip] = slot_out[:, chip]
    for dx, dy, dz in everywhere:
        to = (lax.rem(z + dz, n) * n + lax.rem(y + dy, n)) * n + lax.rem(x + dx, n)
        pltpu.make_async_remote_copy(
            src_ref=slot_out.at[:, to],
            dst_ref=slot_in.at[:, chip],
            send_sem=slot_send,
            recv_sem=slot_recv,
            device_id=shifted(dx, dy, dz),
            device_id_type=MESH,
        ).start()

    loads["stiff"].wait()
    loads["srow"].wait()
    loads["scol"].wait()
    loads["start"].wait()
    for i in range(stiff_v.shape[0]):
        stiff_hi[i], stiff_lo[i] = split(stiff_v[i].T)

    axis1 = stage0(1, core1)

    flat = sorted(((a, b) for a in range(n) for b in range(n) if a or b), key=far, reverse=True)

    def stage1(group, copies):
        for copy in copies:
            copy.wait_recv()
        for part in range(3):
            own = pl.multiple_of(place[axes[part][0]] * rows1, 8)
            t = 3 * group + part
            total = c_all[t, pl.ds(own, rows1), :]
            for step in range(1, n):
                total = total + r1_all[step - 1, t]
            for s in range(n * n):
                f_all[t, s] = total[s * cols : (s + 1) * cols]
        for i, (da, db) in enumerate(flat):
            for part in range(3):
                _, a, b = axes[part]
                to = lax.rem(place[a] + da, n) * n + lax.rem(place[b] + db, n)
                step = [0, 0, 0]
                step[a], step[b] = da, db
                t = 3 * group + part
                pltpu.make_async_remote_copy(
                    src_ref=f_all.at[t, to],
                    dst_ref=r2_all.at[t, i],
                    send_sem=plane_send.at[group],
                    recv_sem=plane_recv.at[group],
                    device_id=shifted(*step),
                    device_id_type=MESH,
                ).start()

    def all_of(ref, send, recv):
        return pltpu.make_async_remote_copy(
            src_ref=ref, dst_ref=ref, send_sem=send, recv_sem=recv, device_id=sibling, device_id_type=MESH
        )

    def plane_end(group):
        copy = all_of(r2_all.at[3 * group : 3 * group + 3], plane_send.at[group], plane_recv.at[group])
        copy.wait_recv()
        done.append(copy)
        ends = []
        for part in range(3):
            _, a, b = axes[part]
            t = 3 * group + part
            total = f_all[t, place[a] * n + place[b]]
            for i in range(len(flat)):
                total = total + r2_all[t, i]
            ends.append(total)
        return jnp.concatenate(ends, axis=1)

    stage1(0, axis0)

    def stacked(value):
        vh, vl = split(value)
        vh, vl = vh.astype(F32), vl.astype(F32)
        return jnp.concatenate([vh, vl, jnp.zeros((8, value.shape[1]), F32)], axis=0).astype(BF16)

    group_rows = n * cols

    def couple(value, turn):
        lhs = stacked(value)
        total = jnp.zeros((group_rows, width), F32)
        row_at = lax.broadcasted_iota(I32, (group_rows, width), 0)
        col_at = lax.broadcasted_iota(I32, (cols, width), 0)
        for i in range(stiff_v.shape[0]):
            a = dot(lhs, stiff_hi[i])
            b = dot(lhs, stiff_lo[i])
            every = a[0:cols] + a[cols : 2 * cols] + b[0:cols]
            picked = jnp.sum(jnp.where(col_at == scol_s[i], every, 0.0), axis=0, keepdims=True)
            total = total + jnp.where(row_at == srow_s[i], picked, 0.0)
        for s in range(n):
            cpl_out[turn, s] = total[s * cols : (s + 1) * cols]
        copies = []
        for step in range(1, n):
            copies.append(
                pltpu.make_async_remote_copy(
                    src_ref=cpl_out.at[turn, lax.rem(x + step, n)],
                    dst_ref=cpl_in.at[turn, step - 1],
                    send_sem=cpl_send.at[turn, step - 1],
                    recv_sem=cpl_recv.at[turn, step - 1],
                    device_id=shifted(step, 0, 0),
                    device_id_type=MESH,
                )
            )
            copies[-1].start()
        done.extend(copies)
        return copies

    def coupled(turn, copies):
        total = cpl_out[turn, x]
        for step in range(1, n):
            copies[step - 1].wait_recv()
            total = total + cpl_in[turn, step - 1]
        return total

    field0 = jnp.concatenate([start_v[c] for c in range(3)], axis=1)
    cpl_copies0 = couple(field0, 0)

    loads["inverse"].wait()
    for i in range(cols):
        inverse_hi[i], inverse_lo[i] = split(inverse_v[i].T)
    flipped = codes[...].T
    lane = lax.broadcasted_iota(I32, (blocks, keys), 1).astype(F32)
    gather_hot[...] = jnp.where(lane == flipped[:, 0:1], 1.0, 0.0).astype(BF16)

    def correct(residual):
        lhs = stacked(residual)
        total = jnp.zeros((cols, width), F32)
        col_at = lax.broadcasted_iota(I32, (cols, width), 0)
        for k in range(cols):
            a = dot(lhs, inverse_hi[k])
            b = dot(lhs, inverse_lo[k])
            total = total + jnp.where(col_at == k, a[0:cols] + a[cols : 2 * cols] + b[0:cols], 0.0)
        return total

    stage1(1, axis1)
    field1 = field0 + correct(plane_end(0) - coupled(0, cpl_copies0))
    cpl_copies1 = couple(field1, 1)

    rows_s[...] = jnp.zeros_like(rows_s)
    for c in range(3):
        rows_s[c * cols : (c + 1) * cols, :] = field1[:, c * points : (c + 1) * points]
    uh, ul = split(rows_s[...])
    spread = dot(jnp.concatenate([uh, ul], axis=1), nt_w[...], NT) + dot(uh, nt_lo[...], NT)

    arrived = all_of(slot_in.at[:, pl.ds(0, chips - 1)], slot_send, slot_recv)
    arrived.wait_recv()
    done.append(arrived)
    marks = jnp.concatenate([slot_in[s, :, cap, :] for s in range(2)], axis=0).T
    summed = None
    for j in range(cap):
        values = jnp.concatenate([slot_in[s, :, j, :] for s in range(2)], axis=0)
        got = dot(
            marks[j * tags : (j + 1) * tags].astype(BF16), jnp.concatenate(split(values), axis=1)
        )
        summed = got if summed is None else summed + got
    summed = folded(summed)
    wide_s[...] = jnp.zeros_like(wide_s)
    for p in range(patterns):
        for c in range(3):
            wide_s[c * cols : (c + 1) * cols, p * points : (p + 1) * points] = summed[p * cols : (p + 1) * cols]
    eh, el = split(spread * wide_s[...])
    rows_s[...] = folded(dot(eh, nn_w[...]) + dot(el, nn_w[...]))
    load = plane_end(1) - jnp.concatenate([rows_s[c * cols : (c + 1) * cols, :] for c in range(3)], axis=1)
    field2 = field1 + correct(load - coupled(1, cpl_copies1))

    for c in range(3):
        out_u[c] = field2[:, c * points : (c + 1) * points]
    home = pl.multiple_of(core * chips, 8)
    field[home + chip] = field2
    for offsets in everywhere:
        pltpu.make_async_remote_copy(
            src_ref=field.at[home + chip],
            dst_ref=field.at[home + chip],
            send_sem=back_send,
            recv_sem=back_recv,
            device_id=shifted(*offsets),
            device_id_type=MESH,
        ).start()
    copy = all_of(field.at[pl.ds(home, chips - 1)], back_send, back_recv)
    copy.wait_recv()
    done.append(copy)
    view = field.at[pl.ds(home, chips)]
    copy = pltpu.make_async_remote_copy(
        src_ref=view,
        dst_ref=view,
        send_sem=home_send,
        recv_sem=home_recv,
        device_id=sibling,
        device_id_type=MESH,
    )
    copy.start()
    copy.wait_recv()
    done.append(copy)

    flipped = codes[...].T
    pattern_col = flipped[:, 1:2]
    fh, fl = split(field[...].reshape(keys, width))
    rows = []
    for c in range(3):
        spot = slice(c * points, (c + 1) * points)
        rows.append(dot(gather_hot[...], jnp.concatenate([fh[:, spot], fl[:, spot]], axis=1)).astype(BF16))
    got = jnp.concatenate(rows, axis=0)
    acc = [jnp.zeros((blocks, points), F32) for _ in range(3)]
    for j in range(patterns // 2):
        spot = slice(2 * j * points, 2 * (j + 1) * points)
        pair = dot(got, nt_w[spot, :], NT) + dot(got[:, :points], nt_lo[spot, :], NT)
        for c in range(3):
            mid = pair[c * blocks : (c + 1) * blocks]
            acc[c] = jnp.where(pattern_col == 2 * j, mid[:, :points], acc[c])
            acc[c] = jnp.where(pattern_col == 2 * j + 1, mid[:, points:], acc[c])
    for c in range(3):
        out_i[c] = acc[c]

    for copy in done:
        copy.wait_send()


def on_device(
    n,
    traction_base,
    added_mass,
    interface_prev,
    patch_route,
    basis_pattern,
    column_block,
    basis_values_table,
    stiffness,
    stiff_row,
    stiff_col,
    block_inverse,
    previous_shell_displacement,
):
    blocks = added_mass.shape[0]
    patterns, points, _ = basis_values_table.shape
    width = 3 * points
    cols = 4
    chips = n * n * n
    half, rows1 = chips * cols, n * n * cols
    keys = 2 * half
    stiffs = stiffness.shape[0]
    any_, vmem = (pl.BlockSpec(memory_space=m) for m in (pl.ANY, pltpu.VMEM))
    V = pltpu.VMEM
    dma = pltpu.SemaphoreType.DMA
    out_u, out_i = pl.pallas_call(
        functools.partial(kernel, n),
        out_shape=(
            jax.ShapeDtypeStruct((3, cols, points), F32),
            jax.ShapeDtypeStruct((3, blocks, points), F32),
        ),
        in_specs=[any_] * 12,
        out_specs=(vmem, vmem),
        scratch_shapes=[
            V((3, blocks, points), F32),
            V((blocks, points), F32),
            V((3, blocks, points), F32),
            V((1, blocks), I32),
            V((1, blocks), I32),
            V((1, blocks), I32),
            V((patterns, points, points), F32),
            V((stiffs, width, width), F32),
            pltpu.SMEM((stiffs,), I32),
            pltpu.SMEM((stiffs,), I32),
            V((cols, width, width), F32),
            V((3, cols, points), F32),
            V((stiffs, width, width), BF16),
            V((stiffs, width, width), BF16),
            V((cols, width, width), BF16),
            V((cols, width, width), BF16),
            V((patterns * points, 2 * points), BF16),
            V((patterns * points, 2 * points), BF16),
            V((patterns * points, points), BF16),
            V((128, blocks), F32),
            V((patterns, blocks, points), BF16),
            V((3, keys, blocks), BF16),
            V((blocks, keys), BF16),
            V((6, keys, points), F32),
            V((6, half, points), F32),
            V((n - 1, 6, rows1, points), F32),
            V((6, n * n, cols, points), F32),
            V((6, n * n - 1, cols, points), F32),
            V((2, chips, 5, points), F32),
            V((2, chips, 5, points), F32),
            V((2, chips, 5, points), F32),
            V((2, n, cols, width), F32),
            V((2, n - 1, cols, width), F32),
            V((16, points), F32),
            V((16, patterns * points), F32),
            V((2 * chips, cols, width), F32),
            dma((12,)),
            dma((3,)),
            dma((3,)),
            dma((2, 3 * (n - 1))),
            dma((2, 3 * (n - 1))),
            dma((2,)),
            dma((2,)),
            dma,
            dma,
            dma((2, n - 1)),
            dma((2, n - 1)),
            dma,
            dma,
            dma,
            dma,
        ],
        compiler_params=pltpu.CompilerParams(
            collective_id=0, has_side_effects=True, vmem_limit_bytes=62 * 1024 * 1024
        ),
    )(
        jnp.transpose(traction_base, (1, 0, 2)),
        added_mass,
        jnp.transpose(interface_prev, (1, 0, 2)),
        patch_route.reshape(1, blocks),
        basis_pattern.reshape(1, blocks),
        column_block.reshape(1, blocks),
        basis_values_table,
        stiffness,
        stiff_row,
        stiff_col,
        block_inverse,
        jnp.transpose(previous_shell_displacement, (1, 0, 2)),
    )
    return jnp.transpose(out_u, (1, 0, 2)), jnp.transpose(out_i, (1, 0, 2))


def solution(mesh):
    both = P(("fluid", "shell"))
    n = mesh.shape["shell"]
    return jax.shard_map(
        functools.partial(on_device, n),
        mesh=mesh,
        in_specs=(
            P(("fluid", "shell"), None, None),
            P(("fluid", "shell"), None),
            P(("fluid", "shell"), None, None),
            P(("fluid", "shell"), None),
            both,
            both,
            P(),
            P(("fluid", "shell"), None, None),
            both,
            both,
            P(("fluid", "shell"), None, None),
            P(("fluid", "shell"), None, None),
        ),
        out_specs=(P(("fluid", "shell"), None, None), P(("fluid", "shell"), None, None)),
        check_vma=False,
    )
```

```python
import functools

import jax
import jax.numpy as jnp
from jax import lax
from jax.experimental import pallas as pl
from jax.experimental.pallas import tpu as pltpu
from jax.sharding import PartitionSpec as P

F32, BF16, I32 = jnp.float32, jnp.bfloat16, jnp.int32
NT = (((1,), (1,)), ((), ()))
NN = (((1,), (0,)), ((), ()))
def split(value):
    high = value.astype(BF16)
    low = (value - high.astype(F32)).astype(BF16)
    return high, low


def dot(a, b, dims=NN):
    return lax.dot_general(a, b, dims, preferred_element_type=F32)


def kernel(
    n,
    base_h,
    mass_h,
    prev_h,
    route_h,
    pattern_h,
    column_h,
    table_h,
    stiff_h,
    srow_h,
    scol_h,
    inverse_h,
    start_h,
    out_u,
    out_i,
    base_v,
    mass_v,
    prev_v,
    route_v,
    pattern_v,
    column_v,
    table_v,
    stiff_v,
    srow_s,
    scol_s,
    inverse_v,
    start_v,
    stiff_hi,
    stiff_lo,
    inverse_hi,
    inverse_lo,
    nn_w,
    nt_w,
    nt_lo,
    codes,
    pmask,
    scatter_hot,
    gather_hot,
    d_all,
    c_all,
    r1_all,
    f_all,
    r2_all,
    slot_own,
    slot_out,
    slot_in,
    cpl_out,
    cpl_in,
    rows_s,
    wide_s,
    field,
    load_sem,
    core_send,
    core_recv,
    axis_send,
    axis_recv,
    plane_send,
    plane_recv,
    slot_send,
    slot_recv,
    cpl_send,
    cpl_recv,
    back_send,
    back_recv,
    home_send,
    home_recv,
):
    fluid, x = lax.axis_index("fluid"), lax.axis_index("shell")
    core = lax.rem(fluid, 2)
    y = lax.rem(lax.div(fluid, 2), n)
    z = lax.div(fluid, 2 * n)
    cols = 4
    half, rows1 = n * n * n * cols, n * n * cols
    blocks = mass_v.shape[0]
    patterns = table_v.shape[0]
    points = table_v.shape[1]
    keys = 2 * half
    chips = n * n * n
    width = 3 * points
    cap = 4
    tags = patterns * cols
    place = (x, y, z)
    axes = ((0, 1, 2), (1, 2, 0), (2, 0, 1))
    MESH = pl.DeviceIdType.MESH

    def shifted(dx, dy, dz):
        to_x, to_y, to_z = lax.rem(x + dx, n), lax.rem(y + dy, n), lax.rem(z + dz, n)
        return ((to_z * n + to_y) * 2 + core, to_x)

    def far(offsets):
        return sum(min(v, n - v) for v in offsets)

    everywhere = sorted(
        ((a, b, c) for c in range(n) for b in range(n) for a in range(n) if a or b or c),
        key=far,
        reverse=True,
    )
    sibling = (fluid + 1 - 2 * core, x)

    sources = (route_h, pattern_h, column_h, mass_h, prev_h, base_h, table_h, start_h, srow_h, scol_h, stiff_h, inverse_h)
    places = (route_v, pattern_v, column_v, mass_v, prev_v, base_v, table_v, start_v, srow_s, scol_s, stiff_v, inverse_v)
    names = ("route", "pattern", "column", "mass", "prev", "base", "table", "start", "srow", "scol", "stiff", "inverse")
    loads = {}
    for i, (name, src, dst) in enumerate(zip(names, sources, places)):
        loads[name] = pltpu.make_async_copy(src, dst, load_sem.at[i])
        loads[name].start()

    barrier = pltpu.get_barrier_semaphore()
    partners = [sibling] + [shifted(*o) for o in everywhere]
    for partner in partners:
        pl.semaphore_signal(barrier, inc=1, device_id=partner, device_id_type=MESH)

    def folded(pair):
        return pair[:, :points] + pair[:, points:]

    for name in ("route", "pattern", "column"):
        loads[name].wait()
    route, column, pattern = route_v[...], column_v[...], pattern_v[...]
    bits = n.bit_length() - 1
    px = route & (n - 1)
    pcore = (route >> bits) & 1
    py = (route >> (bits + 1)) & (n - 1)
    pz = route >> (2 * bits + 1)
    where_is = (px, py, pz)
    code = [
        (((pcore * n + where_is[a]) * n + where_is[b]) * n + where_is[c]) * cols + column
        for a, b, c in axes
    ]
    codes[...] = jnp.zeros_like(codes)
    codes[0:1, :] = ((((pcore * n + pz) * n + py) * n + px) * cols + column).astype(F32)
    codes[1:2, :] = pattern.astype(F32)
    codes[2:3, :] = (((pcore * n + pz) * n + py) * n + px).astype(F32)
    codes[3:4, :] = (pattern * cols + column).astype(F32)
    flipped = codes[...].T
    for p in range(patterns):
        pmask[p] = jnp.broadcast_to(jnp.where(flipped[:, 1:2] == p, 1.0, 0.0), (blocks, points)).astype(BF16)
    sub = lax.broadcasted_iota(I32, (keys, blocks), 0)
    for part in range(3):
        scatter_hot[part] = jnp.where(sub == code[part], 1.0, 0.0).astype(BF16)

    loads["mass"].wait()
    owner_col = lax.broadcast_in_dim(flipped[:, 2:3], (blocks, blocks), (0, 1))
    same = owner_col == codes[2:3, :]
    down = lax.broadcasted_iota(I32, (blocks, blocks), 0)
    along = lax.broadcasted_iota(I32, (blocks, blocks), 1)
    slot_row = jnp.sum(jnp.where(same & (down < along), 1.0, 0.0), axis=0, keepdims=True)
    slot_col = jnp.sum(jnp.where(same & (along < down), 1.0, 0.0), axis=1, keepdims=True)
    owners = 2 * chips
    spot_of = slot_row * owners + codes[2:3, :]
    hot = jnp.where(lax.broadcasted_iota(I32, (cap * owners, blocks), 0).astype(F32) == spot_of, 1.0, 0.0).astype(BF16)
    slots = folded(dot(hot, jnp.concatenate(split(mass_v[...]), axis=1)))
    mark = slot_col * tags + flipped[:, 3:4]
    marked = jnp.where(lax.broadcasted_iota(I32, (blocks, points), 1).astype(F32) == mark, 1.0, 0.0).astype(BF16)
    owner_hot = jnp.where(lax.broadcasted_iota(I32, (owners, blocks), 0).astype(F32) == codes[2:3, :], 1.0, 0.0).astype(BF16)
    marks = dot(owner_hot, marked)
    for s in range(2):
        for j in range(cap):
            slot_own[s, :, j, :] = slots[j * owners + s * chips : j * owners + (s + 1) * chips]
        slot_own[s, :, cap, :] = marks[s * chips : (s + 1) * chips]

    loads["table"].wait()
    for p in range(patterns):
        th, tl = split(table_v[p])
        spot = slice(p * points, (p + 1) * points)
        nn_w[spot, :points] = th
        nn_w[spot, points:] = tl

    def project(values):
        parts = []
        for value in values:
            parts.extend(split(value))
        wide = jnp.concatenate(
            [jnp.concatenate([v * pmask[p] for v in parts], axis=0) for p in range(patterns)], axis=1
        )
        got = dot(wide, nn_w[...])
        ends = []
        for i in range(3):
            both = got[2 * i * blocks : (2 * i + 1) * blocks] + got[(2 * i + 1) * blocks : (2 * i + 2) * blocks]
            ends.append(jnp.concatenate(split(folded(both)), axis=1))
        return ends

    other = pl.multiple_of((1 - core) * half, 8)
    mine = pl.multiple_of(core * half, 8)

    def to_sibling(group):
        low_t, high_t = 3 * group, 3 * group + 3
        copy = pltpu.make_async_remote_copy(
            src_ref=d_all.at[low_t:high_t, pl.ds(other, half), :],
            dst_ref=c_all.at[low_t:high_t],
            send_sem=core_send.at[group],
            recv_sem=core_recv.at[group],
            device_id=sibling,
            device_id_type=MESH,
        )
        copy.start()
        return copy

    done = []

    def stage0(group, copy):
        copy.wait_recv()
        done.append(copy)
        for t in range(3 * group, 3 * group + 3):
            c_all[t] = c_all[t] + d_all[t, pl.ds(mine, half), :]
        copies = []
        for step in range(1, n):
            for part in range(3):
                axis = axes[part][0]
                t = 3 * group + part
                to = lax.rem(place[axis] + step, n)
                slot = part * (n - 1) + step - 1
                target = shifted(*[step if a == axis else 0 for a in range(3)])
                copies.append(
                    pltpu.make_async_remote_copy(
                        src_ref=c_all.at[t, pl.ds(pl.multiple_of(to * rows1, 8), rows1), :],
                        dst_ref=r1_all.at[step - 1, t],
                        send_sem=axis_send.at[group, slot],
                        recv_sem=axis_recv.at[group, slot],
                        device_id=target,
                        device_id_type=MESH,
                    )
                )
                copies[-1].start()
        done.extend(copies)
        return copies

    loads["prev"].wait()
    loads["base"].wait()
    force = project([base_v[c] - mass_v[...] * prev_v[c] for c in range(3)])
    for c in range(3):
        d_all[c] = folded(dot(scatter_hot[c], force[c]))
    pl.semaphore_wait(barrier, len(partners))
    slot_copy = pltpu.make_async_remote_copy(
        src_ref=slot_own.at[1 - core],
        dst_ref=slot_out.at[core],
        send_sem=core_send.at[2],
        recv_sem=core_recv.at[2],
        device_id=sibling,
        device_id_type=MESH,
    )
    slot_copy.start()
    core0 = to_sibling(0)
    slot_out[core] = slot_own[core]
    chip = (z * n + y) * n + x
    axis0 = stage0(0, core0)
    slot_copy.wait_recv()
    done.append(slot_copy)
    slot_in[:, chip] = slot_out[:, chip]
    for dx, dy, dz in everywhere:
        to = (lax.rem(z + dz, n) * n + lax.rem(y + dy, n)) * n + lax.rem(x + dx, n)
        pltpu.make_async_remote_copy(
            src_ref=slot_out.at[:, to],
            dst_ref=slot_in.at[:, chip],
            send_sem=slot_send,
            recv_sem=slot_recv,
            device_id=shifted(dx, dy, dz),
            device_id_type=MESH,
        ).start()
    load = project([base_v[c] for c in range(3)])
    for c in range(3):
        d_all[3 + c] = folded(dot(scatter_hot[c], load[c]))
    core1 = to_sibling(1)

    loads["stiff"].wait()
    loads["srow"].wait()
    loads["scol"].wait()
    loads["start"].wait()
    for i in range(stiff_v.shape[0]):
        stiff_hi[i], stiff_lo[i] = split(stiff_v[i].T)


    flat = sorted(((a, b) for a in range(n) for b in range(n) if a or b), key=far, reverse=True)

    def stage1(group, copies):
        for copy in copies:
            copy.wait_recv()
        for part in range(3):
            own = pl.multiple_of(place[axes[part][0]] * rows1, 8)
            t = 3 * group + part
            total = c_all[t, pl.ds(own, rows1), :]
            for step in range(1, n):
                total = total + r1_all[step - 1, t]
            for s in range(n * n):
                f_all[t, s] = total[s * cols : (s + 1) * cols]
        for i, (da, db) in enumerate(flat):
            for part in range(3):
                _, a, b = axes[part]
                to = lax.rem(place[a] + da, n) * n + lax.rem(place[b] + db, n)
                step = [0, 0, 0]
                step[a], step[b] = da, db
                t = 3 * group + part
                pltpu.make_async_remote_copy(
                    src_ref=f_all.at[t, to],
                    dst_ref=r2_all.at[t, i],
                    send_sem=plane_send.at[group],
                    recv_sem=plane_recv.at[group],
                    device_id=shifted(*step),
                    device_id_type=MESH,
                ).start()

    def all_of(ref, send, recv):
        return pltpu.make_async_remote_copy(
            src_ref=ref, dst_ref=ref, send_sem=send, recv_sem=recv, device_id=sibling, device_id_type=MESH
        )

    def plane_end(group):
        copy = all_of(r2_all.at[3 * group : 3 * group + 3], plane_send.at[group], plane_recv.at[group])
        copy.wait_recv()
        done.append(copy)
        ends = []
        for part in range(3):
            _, a, b = axes[part]
            t = 3 * group + part
            total = f_all[t, place[a] * n + place[b]]
            for i in range(len(flat)):
                total = total + r2_all[t, i]
            ends.append(total)
        return jnp.concatenate(ends, axis=1)

    stage1(0, axis0)
    axis1 = stage0(1, core1)

    def stacked(value):
        vh, vl = split(value)
        vh, vl = vh.astype(F32), vl.astype(F32)
        return jnp.concatenate([vh, vl, jnp.zeros((8, value.shape[1]), F32)], axis=0).astype(BF16)

    group_rows = n * cols

    def couple(value, turn):
        lhs = stacked(value)
        total = jnp.zeros((group_rows, width), F32)
        row_at = lax.broadcasted_iota(I32, (group_rows, width), 0)
        col_at = lax.broadcasted_iota(I32, (cols, width), 0)
        for i in range(stiff_v.shape[0]):
            a = dot(lhs, stiff_hi[i])
            b = dot(lhs, stiff_lo[i])
            every = a[0:cols] + a[cols : 2 * cols] + b[0:cols]
            picked = jnp.sum(jnp.where(col_at == scol_s[i], every, 0.0), axis=0, keepdims=True)
            total = total + jnp.where(row_at == srow_s[i], picked, 0.0)
        for s in range(n):
            cpl_out[turn, s] = total[s * cols : (s + 1) * cols]
        copies = []
        for step in range(1, n):
            copies.append(
                pltpu.make_async_remote_copy(
                    src_ref=cpl_out.at[turn, lax.rem(x + step, n)],
                    dst_ref=cpl_in.at[turn, step - 1],
                    send_sem=cpl_send.at[turn, step - 1],
                    recv_sem=cpl_recv.at[turn, step - 1],
                    device_id=shifted(step, 0, 0),
                    device_id_type=MESH,
                )
            )
            copies[-1].start()
        done.extend(copies)
        return copies

    def coupled(turn, copies):
        total = cpl_out[turn, x]
        for step in range(1, n):
            copies[step - 1].wait_recv()
            total = total + cpl_in[turn, step - 1]
        return total

    field0 = jnp.concatenate([start_v[c] for c in range(3)], axis=1)
    cpl_copies0 = couple(field0, 0)

    loads["inverse"].wait()
    for i in range(cols):
        inverse_hi[i], inverse_lo[i] = split(inverse_v[i].T)
    flipped = codes[...].T
    lane = lax.broadcasted_iota(I32, (blocks, half), 1).astype(F32)
    for side in range(2):
        gather_hot[side] = jnp.where(lane == flipped[:, 0:1] - side * half, 1.0, 0.0).astype(BF16)

    def correct(residual):
        lhs = stacked(residual)
        total = jnp.zeros((cols, width), F32)
        col_at = lax.broadcasted_iota(I32, (cols, width), 0)
        for k in range(cols):
            a = dot(lhs, inverse_hi[k])
            b = dot(lhs, inverse_lo[k])
            total = total + jnp.where(col_at == k, a[0:cols] + a[cols : 2 * cols] + b[0:cols], 0.0)
        return total

    for p in range(patterns):
        th, tl = split(table_v[p].T)
        spot = slice(p * points, (p + 1) * points)
        nt_w[:points, spot] = th
        nt_w[points:, spot] = th
        nt_lo[:, spot] = tl
    stage1(1, axis1)
    field1 = field0 + correct(plane_end(0) - coupled(0, cpl_copies0))
    cpl_copies1 = couple(field1, 1)

    rows_s[...] = jnp.zeros_like(rows_s)
    for c in range(3):
        rows_s[c * cols : (c + 1) * cols, :] = field1[:, c * points : (c + 1) * points]
    uh, ul = split(rows_s[...])
    spread = dot(jnp.concatenate([uh, ul], axis=1), nt_w[...]) + dot(uh, nt_lo[...])

    arrived = all_of(slot_in.at[:, pl.ds(0, chips - 1)], slot_send, slot_recv)
    arrived.wait_recv()
    done.append(arrived)
    marks = jnp.concatenate([slot_in[s, :, cap, :] for s in range(2)], axis=0).T
    summed = None
    for j in range(cap):
        values = jnp.concatenate([slot_in[s, :, j, :] for s in range(2)], axis=0)
        got = dot(
            marks[j * tags : (j + 1) * tags].astype(BF16), jnp.concatenate(split(values), axis=1)
        )
        summed = got if summed is None else summed + got
    summed = folded(summed)
    wide_s[...] = jnp.zeros_like(wide_s)
    for p in range(patterns):
        for c in range(3):
            wide_s[c * cols : (c + 1) * cols, p * points : (p + 1) * points] = summed[p * cols : (p + 1) * cols]
    eh, el = split(spread * wide_s[...])
    rows_s[...] = folded(dot(eh, nn_w[...]) + dot(el, nn_w[...]))
    load = plane_end(1) - jnp.concatenate([rows_s[c * cols : (c + 1) * cols, :] for c in range(3)], axis=1)
    field2 = field1 + correct(load - coupled(1, cpl_copies1))

    for c in range(3):
        out_u[c] = field2[:, c * points : (c + 1) * points]
    home = pl.multiple_of(core * chips, 8)
    field[home + chip] = field2
    planes = sorted(range(n), key=lambda d: -min(d, n - d))
    for dz in planes:
        for offsets in everywhere:
            if offsets[2] == dz:
                pltpu.make_async_remote_copy(
                    src_ref=field.at[home + chip],
                    dst_ref=field.at[home + chip],
                    send_sem=back_send.at[dz],
                    recv_sem=back_recv.at[dz],
                    device_id=shifted(*offsets),
                    device_id_type=MESH,
                ).start()
    homes = []
    for dz in planes:
        first_row = home + lax.rem(z - dz + n, n) * (n * n)
        copy = all_of(field.at[pl.ds(first_row, n * n if dz else n * n - 1)], back_send.at[dz], back_recv.at[dz])
        copy.wait_recv()
        done.append(copy)
        view = field.at[pl.ds(first_row, n * n)]
        copy = pltpu.make_async_remote_copy(
            src_ref=view,
            dst_ref=view,
            send_sem=home_send.at[dz],
            recv_sem=home_recv.at[dz],
            device_id=sibling,
            device_id_type=MESH,
        )
        copy.start()
        homes.append(copy)
        done.append(copy)

    def gathered(side):
        fh, fl = split(field[pl.ds(side * chips, chips)].reshape(half, width))
        hot = gather_hot[side]
        spots = [slice(c * points, (c + 1) * points) for c in range(3)]
        return [dot(hot, jnp.concatenate([fh[:, spot], fl[:, spot]], axis=1)) for spot in spots]

    near = gathered(core)
    for copy in homes:
        copy.wait_recv()
    flipped = codes[...].T
    pattern_col = flipped[:, 1:2]
    rows = [(u + v).astype(BF16) for u, v in zip(near, gathered(1 - core))]
    got = jnp.concatenate(rows, axis=0)
    acc = [jnp.zeros((blocks, points), F32) for _ in range(3)]
    for j in range(patterns // 2):
        spot = slice(2 * j * points, 2 * (j + 1) * points)
        pair = dot(got, nt_w[:, spot]) + dot(got[:, :points], nt_lo[:, spot])
        for c in range(3):
            mid = pair[c * blocks : (c + 1) * blocks]
            acc[c] = jnp.where(pattern_col == 2 * j, mid[:, :points], acc[c])
            acc[c] = jnp.where(pattern_col == 2 * j + 1, mid[:, points:], acc[c])
    for c in range(3):
        out_i[c] = acc[c]

    for copy in done:
        copy.wait_send()


def on_device(
    n,
    traction_base,
    added_mass,
    interface_prev,
    patch_route,
    basis_pattern,
    column_block,
    basis_values_table,
    stiffness,
    stiff_row,
    stiff_col,
    block_inverse,
    previous_shell_displacement,
):
    blocks = added_mass.shape[0]
    patterns, points, _ = basis_values_table.shape
    width = 3 * points
    cols = 4
    chips = n * n * n
    half, rows1 = chips * cols, n * n * cols
    keys = 2 * half
    stiffs = stiffness.shape[0]
    any_, vmem = (pl.BlockSpec(memory_space=m) for m in (pl.ANY, pltpu.VMEM))
    V = pltpu.VMEM
    dma = pltpu.SemaphoreType.DMA
    out_u, out_i = pl.pallas_call(
        functools.partial(kernel, n),
        out_shape=(
            pltpu.VMEM((3, cols, points), F32),
            pltpu.VMEM((3, blocks, points), F32),
        ),
        in_specs=[any_] * 12,
        out_specs=(vmem, vmem),
        scratch_shapes=[
            V((3, blocks, points), F32),
            V((blocks, points), F32),
            V((3, blocks, points), F32),
            V((1, blocks), I32),
            V((1, blocks), I32),
            V((1, blocks), I32),
            V((patterns, points, points), F32),
            V((stiffs, width, width), F32),
            pltpu.SMEM((stiffs,), I32),
            pltpu.SMEM((stiffs,), I32),
            V((cols, width, width), F32),
            V((3, cols, points), F32),
            V((stiffs, width, width), BF16),
            V((stiffs, width, width), BF16),
            V((cols, width, width), BF16),
            V((cols, width, width), BF16),
            V((patterns * points, 2 * points), BF16),
            V((2 * points, patterns * points), BF16),
            V((points, patterns * points), BF16),
            V((128, blocks), F32),
            V((patterns, blocks, points), BF16),
            V((3, keys, blocks), BF16),
            V((2, blocks, half), BF16),
            V((6, keys, points), F32),
            V((6, half, points), F32),
            V((n - 1, 6, rows1, points), F32),
            V((6, n * n, cols, points), F32),
            V((6, n * n - 1, cols, points), F32),
            V((2, chips, 5, points), F32),
            V((2, chips, 5, points), F32),
            V((2, chips, 5, points), F32),
            V((2, n, cols, width), F32),
            V((2, n - 1, cols, width), F32),
            V((16, points), F32),
            V((16, patterns * points), F32),
            V((2 * chips, cols, width), F32),
            dma((12,)),
            dma((3,)),
            dma((3,)),
            dma((2, 3 * (n - 1))),
            dma((2, 3 * (n - 1))),
            dma((2,)),
            dma((2,)),
            dma,
            dma,
            dma((2, n - 1)),
            dma((2, n - 1)),
            dma((n,)),
            dma((n,)),
            dma((n,)),
            dma((n,)),
        ],
        compiler_params=pltpu.CompilerParams(
            collective_id=0, has_side_effects=True, vmem_limit_bytes=62 * 1024 * 1024
        ),
    )(
        jnp.transpose(traction_base, (1, 0, 2)),
        added_mass,
        jnp.transpose(interface_prev, (1, 0, 2)),
        patch_route.reshape(1, blocks),
        basis_pattern.reshape(1, blocks),
        column_block.reshape(1, blocks),
        basis_values_table,
        stiffness,
        stiff_row,
        stiff_col,
        block_inverse,
        jnp.transpose(previous_shell_displacement, (1, 0, 2)),
    )
    return jnp.transpose(out_u, (1, 0, 2)), jnp.transpose(out_i, (1, 0, 2))


def solution(mesh):
    both = P(("fluid", "shell"))
    n = mesh.shape["shell"]
    return jax.shard_map(
        functools.partial(on_device, n),
        mesh=mesh,
        in_specs=(
            P(("fluid", "shell"), None, None),
            P(("fluid", "shell"), None),
            P(("fluid", "shell"), None, None),
            P(("fluid", "shell"), None),
            both,
            both,
            P(),
            P(("fluid", "shell"), None, None),
            both,
            both,
            P(("fluid", "shell"), None, None),
            P(("fluid", "shell"), None, None),
        ),
        out_specs=(P(("fluid", "shell"), None, None), P(("fluid", "shell"), None, None)),
        check_vma=False,
    )
```

```python
import functools

import jax
import jax.numpy as jnp
from jax import lax
from jax.experimental import pallas as pl
from jax.experimental.pallas import tpu as pltpu
from jax.sharding import PartitionSpec as P

F32, BF16, I32 = jnp.float32, jnp.bfloat16, jnp.int32
NT = (((1,), (1,)), ((), ()))
NN = (((1,), (0,)), ((), ()))
def split(value):
    high = value.astype(BF16)
    low = (value - high.astype(F32)).astype(BF16)
    return high, low


def dot(a, b, dims=NN):
    return lax.dot_general(a, b, dims, preferred_element_type=F32)


def kernel(
    n,
    base_h,
    mass_h,
    prev_h,
    route_h,
    pattern_h,
    column_h,
    table_h,
    stiff_h,
    srow_h,
    scol_h,
    inverse_h,
    start_h,
    out_u,
    out_i,
    base_v,
    mass_v,
    prev_v,
    route_v,
    pattern_v,
    column_v,
    table_v,
    stiff_v,
    srow_s,
    scol_s,
    inverse_v,
    start_v,
    stiff_hi,
    stiff_lo,
    inverse_hi,
    inverse_lo,
    nn_w,
    nt_w,
    nt_lo,
    codes,
    pmask,
    scatter_hot,
    gather_hot,
    d_all,
    c_all,
    r1_all,
    f_all,
    r2_all,
    slot_own,
    slot_out,
    slot_in,
    cpl_out,
    cpl_in,
    rows_s,
    wide_s,
    field,
    load_sem,
    core_send,
    core_recv,
    axis_send,
    axis_recv,
    plane_send,
    plane_recv,
    slot_send,
    slot_recv,
    cpl_send,
    cpl_recv,
    back_send,
    back_recv,
    home_send,
    home_recv,
):
    fluid, x = lax.axis_index("fluid"), lax.axis_index("shell")
    core = lax.rem(fluid, 2)
    y = lax.rem(lax.div(fluid, 2), n)
    z = lax.div(fluid, 2 * n)
    cols = 4
    half, rows1 = n * n * n * cols, n * n * cols
    blocks = mass_v.shape[0]
    patterns = table_v.shape[0]
    points = table_v.shape[1]
    keys = 2 * half
    chips = n * n * n
    width = 3 * points
    cap = 4
    tags = patterns * cols
    place = (x, y, z)
    axes = ((0, 1, 2), (1, 2, 0), (2, 0, 1))
    MESH = pl.DeviceIdType.MESH

    def shifted(dx, dy, dz):
        to_x, to_y, to_z = lax.rem(x + dx, n), lax.rem(y + dy, n), lax.rem(z + dz, n)
        return ((to_z * n + to_y) * 2 + core, to_x)

    def far(offsets):
        return sum(min(v, n - v) for v in offsets)

    everywhere = sorted(
        ((a, b, c) for c in range(n) for b in range(n) for a in range(n) if a or b or c),
        key=far,
        reverse=True,
    )
    sibling = (fluid + 1 - 2 * core, x)

    sources = (route_h, pattern_h, column_h, mass_h, prev_h, base_h, table_h, start_h, srow_h, scol_h, stiff_h, inverse_h)
    places = (route_v, pattern_v, column_v, mass_v, prev_v, base_v, table_v, start_v, srow_s, scol_s, stiff_v, inverse_v)
    names = ("route", "pattern", "column", "mass", "prev", "base", "table", "start", "srow", "scol", "stiff", "inverse")
    loads = {}
    for i, (name, src, dst) in enumerate(zip(names, sources, places)):
        loads[name] = pltpu.make_async_copy(src, dst, load_sem.at[i])
        loads[name].start()

    barrier = pltpu.get_barrier_semaphore()
    partners = [sibling] + [shifted(*o) for o in everywhere]
    for partner in partners:
        pl.semaphore_signal(barrier, inc=1, device_id=partner, device_id_type=MESH)

    def folded(pair):
        return pair[:, :points] + pair[:, points:]

    for name in ("route", "pattern", "column"):
        loads[name].wait()
    route, column, pattern = route_v[...], column_v[...], pattern_v[...]
    bits = n.bit_length() - 1
    px = route & (n - 1)
    pcore = (route >> bits) & 1
    py = (route >> (bits + 1)) & (n - 1)
    pz = route >> (2 * bits + 1)
    where_is = (px, py, pz)
    code = [
        (((pcore * n + where_is[a]) * n + where_is[b]) * n + where_is[c]) * cols + column
        for a, b, c in axes
    ]
    codes[...] = jnp.zeros_like(codes)
    codes[0:1, :] = ((((pcore * n + pz) * n + py) * n + px) * cols + column).astype(F32)
    codes[1:2, :] = pattern.astype(F32)
    codes[2:3, :] = (((pcore * n + pz) * n + py) * n + px).astype(F32)
    codes[3:4, :] = (pattern * cols + column).astype(F32)
    flipped = codes[...].T
    for p in range(patterns):
        pmask[p] = jnp.broadcast_to(jnp.where(flipped[:, 1:2] == p, 1.0, 0.0), (blocks, points)).astype(BF16)
    sub = lax.broadcasted_iota(I32, (keys, blocks), 0)
    for part in range(3):
        scatter_hot[part] = jnp.where(sub == code[part], 1.0, 0.0).astype(BF16)

    loads["mass"].wait()
    owner_col = lax.broadcast_in_dim(flipped[:, 2:3], (blocks, blocks), (0, 1))
    same = owner_col == codes[2:3, :]
    down = lax.broadcasted_iota(I32, (blocks, blocks), 0)
    along = lax.broadcasted_iota(I32, (blocks, blocks), 1)
    slot_row = jnp.sum(jnp.where(same & (down < along), 1.0, 0.0), axis=0, keepdims=True)
    slot_col = jnp.sum(jnp.where(same & (along < down), 1.0, 0.0), axis=1, keepdims=True)
    owners = 2 * chips
    spot_of = slot_row * owners + codes[2:3, :]
    hot = jnp.where(lax.broadcasted_iota(I32, (cap * owners, blocks), 0).astype(F32) == spot_of, 1.0, 0.0).astype(BF16)
    slots = folded(dot(hot, jnp.concatenate(split(mass_v[...]), axis=1)))
    mark = slot_col * tags + flipped[:, 3:4]
    marked = jnp.where(lax.broadcasted_iota(I32, (blocks, points), 1).astype(F32) == mark, 1.0, 0.0).astype(BF16)
    owner_hot = jnp.where(lax.broadcasted_iota(I32, (owners, blocks), 0).astype(F32) == codes[2:3, :], 1.0, 0.0).astype(BF16)
    marks = dot(owner_hot, marked)
    for s in range(2):
        for j in range(cap):
            slot_own[s, :, j, :] = slots[j * owners + s * chips : j * owners + (s + 1) * chips]
        slot_own[s, :, cap, :] = marks[s * chips : (s + 1) * chips]

    loads["table"].wait()
    for p in range(patterns):
        th, tl = split(table_v[p])
        spot = slice(p * points, (p + 1) * points)
        nn_w[spot, :points] = th
        nn_w[spot, points:] = tl

    def project(values):
        parts = []
        for value in values:
            parts.extend(split(value))
        wide = jnp.concatenate(
            [jnp.concatenate([v * pmask[p] for v in parts], axis=0) for p in range(patterns)], axis=1
        )
        got = dot(wide, nn_w[...])
        ends = []
        for i in range(3):
            both = got[2 * i * blocks : (2 * i + 1) * blocks] + got[(2 * i + 1) * blocks : (2 * i + 2) * blocks]
            ends.append(jnp.concatenate(split(folded(both)), axis=1))
        return ends

    other = pl.multiple_of((1 - core) * half, 8)
    mine = pl.multiple_of(core * half, 8)

    def to_sibling(group):
        low_t, high_t = 3 * group, 3 * group + 3
        copy = pltpu.make_async_remote_copy(
            src_ref=d_all.at[low_t:high_t, pl.ds(other, half), :],
            dst_ref=c_all.at[low_t:high_t],
            send_sem=core_send.at[group],
            recv_sem=core_recv.at[group],
            device_id=sibling,
            device_id_type=MESH,
        )
        copy.start()
        return copy

    done = []

    def stage0(group, copy):
        copy.wait_recv()
        done.append(copy)
        for t in range(3 * group, 3 * group + 3):
            c_all[t] = c_all[t] + d_all[t, pl.ds(mine, half), :]
        copies = []
        for step in range(1, n):
            for part in range(3):
                axis = axes[part][0]
                t = 3 * group + part
                to = lax.rem(place[axis] + step, n)
                slot = part * (n - 1) + step - 1
                target = shifted(*[step if a == axis else 0 for a in range(3)])
                copies.append(
                    pltpu.make_async_remote_copy(
                        src_ref=c_all.at[t, pl.ds(pl.multiple_of(to * rows1, 8), rows1), :],
                        dst_ref=r1_all.at[step - 1, t],
                        send_sem=axis_send.at[group, slot],
                        recv_sem=axis_recv.at[group, slot],
                        device_id=target,
                        device_id_type=MESH,
                    )
                )
                copies[-1].start()
        done.extend(copies)
        return copies

    loads["prev"].wait()
    loads["base"].wait()
    force = project([base_v[c] - mass_v[...] * prev_v[c] for c in range(3)])
    for c in range(3):
        d_all[c] = folded(dot(scatter_hot[c], force[c]))
    pl.semaphore_wait(barrier, len(partners))
    slot_copy = pltpu.make_async_remote_copy(
        src_ref=slot_own.at[1 - core],
        dst_ref=slot_out.at[core],
        send_sem=core_send.at[2],
        recv_sem=core_recv.at[2],
        device_id=sibling,
        device_id_type=MESH,
    )
    slot_copy.start()
    core0 = to_sibling(0)
    slot_out[core] = slot_own[core]
    chip = (z * n + y) * n + x
    axis0 = stage0(0, core0)
    load = project([base_v[c] for c in range(3)])
    for c in range(3):
        d_all[3 + c] = folded(dot(scatter_hot[c], load[c]))
    core1 = to_sibling(1)

    loads["stiff"].wait()
    loads["srow"].wait()
    loads["scol"].wait()
    loads["start"].wait()
    for i in range(stiff_v.shape[0]):
        stiff_hi[i], stiff_lo[i] = split(stiff_v[i].T)


    axis1 = stage0(1, core1)

    flat = sorted(((a, b) for a in range(n) for b in range(n) if a or b), key=far, reverse=True)

    def stage1(group, copies):
        for copy in copies:
            copy.wait_recv()
        for part in range(3):
            own = pl.multiple_of(place[axes[part][0]] * rows1, 8)
            t = 3 * group + part
            total = c_all[t, pl.ds(own, rows1), :]
            for step in range(1, n):
                total = total + r1_all[step - 1, t]
            for s in range(n * n):
                f_all[t, s] = total[s * cols : (s + 1) * cols]
        for i, (da, db) in enumerate(flat):
            for part in range(3):
                _, a, b = axes[part]
                to = lax.rem(place[a] + da, n) * n + lax.rem(place[b] + db, n)
                step = [0, 0, 0]
                step[a], step[b] = da, db
                t = 3 * group + part
                pltpu.make_async_remote_copy(
                    src_ref=f_all.at[t, to],
                    dst_ref=r2_all.at[t, i],
                    send_sem=plane_send.at[group],
                    recv_sem=plane_recv.at[group],
                    device_id=shifted(*step),
                    device_id_type=MESH,
                ).start()

    def all_of(ref, send, recv):
        return pltpu.make_async_remote_copy(
            src_ref=ref, dst_ref=ref, send_sem=send, recv_sem=recv, device_id=sibling, device_id_type=MESH
        )

    def plane_end(group):
        copy = all_of(r2_all.at[3 * group : 3 * group + 3], plane_send.at[group], plane_recv.at[group])
        copy.wait_recv()
        done.append(copy)
        ends = []
        for part in range(3):
            _, a, b = axes[part]
            t = 3 * group + part
            total = f_all[t, place[a] * n + place[b]]
            for i in range(len(flat)):
                total = total + r2_all[t, i]
            ends.append(total)
        return jnp.concatenate(ends, axis=1)

    stage1(0, axis0)

    def stacked(value):
        vh, vl = split(value)
        vh, vl = vh.astype(F32), vl.astype(F32)
        return jnp.concatenate([vh, vl, jnp.zeros((8, value.shape[1]), F32)], axis=0).astype(BF16)

    group_rows = n * cols

    def couple(value, turn):
        lhs = stacked(value)
        total = jnp.zeros((group_rows, width), F32)
        row_at = lax.broadcasted_iota(I32, (group_rows, width), 0)
        col_at = lax.broadcasted_iota(I32, (cols, width), 0)
        for i in range(stiff_v.shape[0]):
            a = dot(lhs, stiff_hi[i])
            b = dot(lhs, stiff_lo[i])
            every = a[0:cols] + a[cols : 2 * cols] + b[0:cols]
            picked = jnp.sum(jnp.where(col_at == scol_s[i], every, 0.0), axis=0, keepdims=True)
            total = total + jnp.where(row_at == srow_s[i], picked, 0.0)
        for s in range(n):
            cpl_out[turn, s] = total[s * cols : (s + 1) * cols]
        copies = []
        for step in range(1, n):
            copies.append(
                pltpu.make_async_remote_copy(
                    src_ref=cpl_out.at[turn, lax.rem(x + step, n)],
                    dst_ref=cpl_in.at[turn, step - 1],
                    send_sem=cpl_send.at[turn, step - 1],
                    recv_sem=cpl_recv.at[turn, step - 1],
                    device_id=shifted(step, 0, 0),
                    device_id_type=MESH,
                )
            )
            copies[-1].start()
        done.extend(copies)
        return copies

    def coupled(turn, copies):
        total = cpl_out[turn, x]
        for step in range(1, n):
            copies[step - 1].wait_recv()
            total = total + cpl_in[turn, step - 1]
        return total

    field0 = jnp.concatenate([start_v[c] for c in range(3)], axis=1)
    cpl_copies0 = couple(field0, 0)

    slot_copy.wait_recv()
    done.append(slot_copy)
    slot_in[:, chip] = slot_out[:, chip]
    for dx, dy, dz in everywhere:
        to = (lax.rem(z + dz, n) * n + lax.rem(y + dy, n)) * n + lax.rem(x + dx, n)
        pltpu.make_async_remote_copy(
            src_ref=slot_out.at[:, to],
            dst_ref=slot_in.at[:, chip],
            send_sem=slot_send,
            recv_sem=slot_recv,
            device_id=shifted(dx, dy, dz),
            device_id_type=MESH,
        ).start()

    loads["inverse"].wait()
    for i in range(cols):
        inverse_hi[i], inverse_lo[i] = split(inverse_v[i].T)
    flipped = codes[...].T
    lane = lax.broadcasted_iota(I32, (blocks, half), 1).astype(F32)
    for side in range(2):
        gather_hot[side] = jnp.where(lane == flipped[:, 0:1] - side * half, 1.0, 0.0).astype(BF16)

    def correct(residual):
        lhs = stacked(residual)
        total = jnp.zeros((cols, width), F32)
        col_at = lax.broadcasted_iota(I32, (cols, width), 0)
        for k in range(cols):
            a = dot(lhs, inverse_hi[k])
            b = dot(lhs, inverse_lo[k])
            total = total + jnp.where(col_at == k, a[0:cols] + a[cols : 2 * cols] + b[0:cols], 0.0)
        return total

    for p in range(patterns):
        th, tl = split(table_v[p].T)
        spot = slice(p * points, (p + 1) * points)
        nt_w[:points, spot] = th
        nt_w[points:, spot] = th
        nt_lo[:, spot] = tl
    stage1(1, axis1)
    field1 = field0 + correct(plane_end(0) - coupled(0, cpl_copies0))
    cpl_copies1 = couple(field1, 1)

    rows_s[...] = jnp.zeros_like(rows_s)
    for c in range(3):
        rows_s[c * cols : (c + 1) * cols, :] = field1[:, c * points : (c + 1) * points]
    uh, ul = split(rows_s[...])
    spread = dot(jnp.concatenate([uh, ul], axis=1), nt_w[...]) + dot(uh, nt_lo[...])

    arrived = all_of(slot_in.at[:, pl.ds(0, chips - 1)], slot_send, slot_recv)
    arrived.wait_recv()
    done.append(arrived)
    marks = jnp.concatenate([slot_in[s, :, cap, :] for s in range(2)], axis=0).T
    summed = None
    for j in range(cap):
        values = jnp.concatenate([slot_in[s, :, j, :] for s in range(2)], axis=0)
        got = dot(
            marks[j * tags : (j + 1) * tags].astype(BF16), jnp.concatenate(split(values), axis=1)
        )
        summed = got if summed is None else summed + got
    summed = folded(summed)
    wide_s[...] = jnp.zeros_like(wide_s)
    for p in range(patterns):
        for c in range(3):
            wide_s[c * cols : (c + 1) * cols, p * points : (p + 1) * points] = summed[p * cols : (p + 1) * cols]
    eh, el = split(spread * wide_s[...])
    rows_s[...] = folded(dot(eh, nn_w[...]) + dot(el, nn_w[...]))
    load = plane_end(1) - jnp.concatenate([rows_s[c * cols : (c + 1) * cols, :] for c in range(3)], axis=1)
    field2 = field1 + correct(load - coupled(1, cpl_copies1))

    for c in range(3):
        out_u[c] = field2[:, c * points : (c + 1) * points]
    home = pl.multiple_of(core * chips, 8)
    field[home + chip] = field2
    planes = sorted(range(n), key=lambda d: -min(d, n - d))
    for dz in planes:
        for offsets in everywhere:
            if offsets[2] == dz:
                pltpu.make_async_remote_copy(
                    src_ref=field.at[home + chip],
                    dst_ref=field.at[home + chip],
                    send_sem=back_send.at[dz],
                    recv_sem=back_recv.at[dz],
                    device_id=shifted(*offsets),
                    device_id_type=MESH,
                ).start()
    homes = []
    for dz in planes:
        first_row = home + lax.rem(z - dz + n, n) * (n * n)
        copy = all_of(field.at[pl.ds(first_row, n * n if dz else n * n - 1)], back_send.at[dz], back_recv.at[dz])
        copy.wait_recv()
        done.append(copy)
        view = field.at[pl.ds(first_row, n * n)]
        copy = pltpu.make_async_remote_copy(
            src_ref=view,
            dst_ref=view,
            send_sem=home_send.at[dz],
            recv_sem=home_recv.at[dz],
            device_id=sibling,
            device_id_type=MESH,
        )
        copy.start()
        homes.append(copy)
        done.append(copy)

    def gathered(side):
        fh, fl = split(field[pl.ds(side * chips, chips)].reshape(half, width))
        hot = gather_hot[side]
        spots = [slice(c * points, (c + 1) * points) for c in range(3)]
        return [dot(hot, jnp.concatenate([fh[:, spot], fl[:, spot]], axis=1)) for spot in spots]

    near = gathered(core)
    for copy in homes:
        copy.wait_recv()
    flipped = codes[...].T
    pattern_col = flipped[:, 1:2]
    rows = [(u + v).astype(BF16) for u, v in zip(near, gathered(1 - core))]
    got = jnp.concatenate(rows, axis=0)
    acc = [jnp.zeros((blocks, points), F32) for _ in range(3)]
    for j in range(patterns // 2):
        spot = slice(2 * j * points, 2 * (j + 1) * points)
        pair = dot(got, nt_w[:, spot]) + dot(got[:, :points], nt_lo[:, spot])
        for c in range(3):
            mid = pair[c * blocks : (c + 1) * blocks]
            acc[c] = jnp.where(pattern_col == 2 * j, mid[:, :points], acc[c])
            acc[c] = jnp.where(pattern_col == 2 * j + 1, mid[:, points:], acc[c])
    for c in range(3):
        out_i[c] = acc[c]

    for copy in done:
        copy.wait_send()


def deliver(u_ref, i_ref, out_u, out_i, sem):
    copies = [pltpu.make_async_copy(src, dst, sem.at[k]) for k, (src, dst) in enumerate(((i_ref, out_i), (u_ref, out_u)))]
    for copy in copies:
        copy.start()
    for copy in copies:
        copy.wait()


def on_device(
    n,
    traction_base,
    added_mass,
    interface_prev,
    patch_route,
    basis_pattern,
    column_block,
    basis_values_table,
    stiffness,
    stiff_row,
    stiff_col,
    block_inverse,
    previous_shell_displacement,
):
    blocks = added_mass.shape[0]
    patterns, points, _ = basis_values_table.shape
    width = 3 * points
    cols = 4
    chips = n * n * n
    half, rows1 = chips * cols, n * n * cols
    keys = 2 * half
    stiffs = stiffness.shape[0]
    any_, vmem = (pl.BlockSpec(memory_space=m) for m in (pl.ANY, pltpu.VMEM))
    V = pltpu.VMEM
    dma = pltpu.SemaphoreType.DMA
    out_u, out_i = pl.pallas_call(
        functools.partial(kernel, n),
        out_shape=(
            pltpu.VMEM((3, cols, points), F32),
            pltpu.VMEM((3, blocks, points), F32),
        ),
        in_specs=[any_] * 12,
        out_specs=(vmem, vmem),
        scratch_shapes=[
            V((3, blocks, points), F32),
            V((blocks, points), F32),
            V((3, blocks, points), F32),
            V((1, blocks), I32),
            V((1, blocks), I32),
            V((1, blocks), I32),
            V((patterns, points, points), F32),
            V((stiffs, width, width), F32),
            pltpu.SMEM((stiffs,), I32),
            pltpu.SMEM((stiffs,), I32),
            V((cols, width, width), F32),
            V((3, cols, points), F32),
            V((stiffs, width, width), BF16),
            V((stiffs, width, width), BF16),
            V((cols, width, width), BF16),
            V((cols, width, width), BF16),
            V((patterns * points, 2 * points), BF16),
            V((2 * points, patterns * points), BF16),
            V((points, patterns * points), BF16),
            V((128, blocks), F32),
            V((patterns, blocks, points), BF16),
            V((3, keys, blocks), BF16),
            V((2, blocks, half), BF16),
            V((6, keys, points), F32),
            V((6, half, points), F32),
            V((n - 1, 6, rows1, points), F32),
            V((6, n * n, cols, points), F32),
            V((6, n * n - 1, cols, points), F32),
            V((2, chips, 5, points), F32),
            V((2, chips, 5, points), F32),
            V((2, chips, 5, points), F32),
            V((2, n, cols, width), F32),
            V((2, n - 1, cols, width), F32),
            V((16, points), F32),
            V((16, patterns * points), F32),
            V((2 * chips, cols, width), F32),
            dma((12,)),
            dma((3,)),
            dma((3,)),
            dma((2, 3 * (n - 1))),
            dma((2, 3 * (n - 1))),
            dma((2,)),
            dma((2,)),
            dma,
            dma,
            dma((2, n - 1)),
            dma((2, n - 1)),
            dma((n,)),
            dma((n,)),
            dma((n,)),
            dma((n,)),
        ],
        compiler_params=pltpu.CompilerParams(
            collective_id=0, has_side_effects=True, vmem_limit_bytes=62 * 1024 * 1024
        ),
    )(
        jnp.transpose(traction_base, (1, 0, 2)),
        added_mass,
        jnp.transpose(interface_prev, (1, 0, 2)),
        patch_route.reshape(1, blocks),
        basis_pattern.reshape(1, blocks),
        column_block.reshape(1, blocks),
        basis_values_table,
        stiffness,
        stiff_row,
        stiff_col,
        block_inverse,
        jnp.transpose(previous_shell_displacement, (1, 0, 2)),
    )
    out_u, out_i = pl.pallas_call(
        deliver,
        out_shape=(
            jax.ShapeDtypeStruct((3, cols, points), F32),
            jax.ShapeDtypeStruct((3, blocks, points), F32),
        ),
        in_specs=[vmem, vmem],
        out_specs=(any_, any_),
        scratch_shapes=[dma((2,))],
        compiler_params=pltpu.CompilerParams(vmem_limit_bytes=4 * 1024 * 1024),
    )(*(pltpu.with_memory_space_constraint(v, pltpu.VMEM) for v in (out_u, out_i)))
    return jnp.transpose(out_u, (1, 0, 2)), jnp.transpose(out_i, (1, 0, 2))


def solution(mesh):
    both = P(("fluid", "shell"))
    n = mesh.shape["shell"]
    return jax.shard_map(
        functools.partial(on_device, n),
        mesh=mesh,
        in_specs=(
            P(("fluid", "shell"), None, None),
            P(("fluid", "shell"), None),
            P(("fluid", "shell"), None, None),
            P(("fluid", "shell"), None),
            both,
            both,
            P(),
            P(("fluid", "shell"), None, None),
            both,
            both,
            P(("fluid", "shell"), None, None),
            P(("fluid", "shell"), None, None),
        ),
        out_specs=(P(("fluid", "shell"), None, None), P(("fluid", "shell"), None, None)),
        check_vma=False,
    )
```

```python
import functools

import jax
import jax.numpy as jnp
from jax import lax
from jax.experimental import pallas as pl
from jax.experimental.pallas import tpu as pltpu
from jax.sharding import PartitionSpec as P

F32, BF16, I32 = jnp.float32, jnp.bfloat16, jnp.int32
NT = (((1,), (1,)), ((), ()))
NN = (((1,), (0,)), ((), ()))
def split(value):
    high = value.astype(BF16)
    low = (value - high.astype(F32)).astype(BF16)
    return high, low


def dot(a, b, dims=NN):
    return lax.dot_general(a, b, dims, preferred_element_type=F32)


def kernel(
    n,
    base_h,
    mass_h,
    prev_h,
    route_h,
    pattern_h,
    column_h,
    table_h,
    stiff_h,
    srow_h,
    scol_h,
    inverse_h,
    start_h,
    out_u,
    out_i,
    base_v,
    mass_v,
    prev_v,
    route_v,
    pattern_v,
    column_v,
    table_v,
    stiff_v,
    srow_s,
    scol_s,
    inverse_v,
    start_v,
    stiff_hi,
    stiff_lo,
    inverse_hi,
    inverse_lo,
    nn_w,
    nt_w,
    nt_lo,
    codes,
    pmask,
    scatter_hot,
    gather_hot,
    pattern_wide,
    d_all,
    c_all,
    r1_all,
    f_all,
    r2_all,
    slot_own,
    slot_out,
    slot_in,
    cpl_out,
    cpl_in,
    rows_s,
    wide_s,
    field,
    load_sem,
    core_send,
    core_recv,
    ready,
    axis_send,
    axis_recv,
    plane_send,
    plane_recv,
    slot_send,
    slot_recv,
    cpl_send,
    cpl_recv,
    back_send,
    back_recv,
    home_send,
    home_recv,
):
    fluid, x = lax.axis_index("fluid"), lax.axis_index("shell")
    core = lax.rem(fluid, 2)
    y = lax.rem(lax.div(fluid, 2), n)
    z = lax.div(fluid, 2 * n)
    cols = 4
    half, rows1 = n * n * n * cols, n * n * cols
    blocks = mass_v.shape[0]
    patterns = table_v.shape[0]
    points = table_v.shape[1]
    keys = 2 * half
    chips = n * n * n
    width = 3 * points
    cap = 4
    tags = patterns * cols
    place = (x, y, z)
    axes = ((0, 1, 2), (1, 2, 0), (2, 0, 1))
    MESH = pl.DeviceIdType.MESH

    def shifted(dx, dy, dz):
        to_x, to_y, to_z = lax.rem(x + dx, n), lax.rem(y + dy, n), lax.rem(z + dz, n)
        return ((to_z * n + to_y) * 2 + core, to_x)

    def far(offsets):
        return sum(min(v, n - v) for v in offsets)

    everywhere = sorted(
        ((a, b, c) for c in range(n) for b in range(n) for a in range(n) if a or b or c),
        key=far,
        reverse=True,
    )
    sibling = (fluid + 1 - 2 * core, x)

    sources = (route_h, pattern_h, column_h, mass_h, prev_h, base_h, table_h, start_h, srow_h, scol_h, stiff_h, inverse_h)
    places = (route_v, pattern_v, column_v, mass_v, prev_v, base_v, table_v, start_v, srow_s, scol_s, stiff_v, inverse_v)
    names = ("route", "pattern", "column", "mass", "prev", "base", "table", "start", "srow", "scol", "stiff", "inverse")
    loads = {}
    for i, (name, src, dst) in enumerate(zip(names, sources, places)):
        loads[name] = pltpu.make_async_copy(src, dst, load_sem.at[i])
        loads[name].start()

    barrier = pltpu.get_barrier_semaphore()
    beside = [shifted(*[step if a == axis else 0 for a in range(3)]) for axis in range(3) for step in range(1, n)]
    partners = [sibling] + beside
    for partner in partners:
        pl.semaphore_signal(barrier, inc=1, device_id=partner, device_id_type=MESH)

    def folded(pair):
        return pair[:, :points] + pair[:, points:]

    for name in ("route", "pattern", "column"):
        loads[name].wait()
    route, column, pattern = route_v[...], column_v[...], pattern_v[...]
    bits = n.bit_length() - 1
    px = route & (n - 1)
    pcore = (route >> bits) & 1
    py = (route >> (bits + 1)) & (n - 1)
    pz = route >> (2 * bits + 1)
    where_is = (px, py, pz)
    code = [
        (((pcore * n + where_is[a]) * n + where_is[b]) * n + where_is[c]) * cols + column
        for a, b, c in axes
    ]
    codes[...] = jnp.zeros_like(codes)
    codes[0:1, :] = ((((pcore * n + pz) * n + py) * n + px) * cols + column).astype(F32)
    codes[1:2, :] = pattern.astype(F32)
    codes[2:3, :] = (((pcore * n + pz) * n + py) * n + px).astype(F32)
    codes[3:4, :] = (pattern * cols + column).astype(F32)
    flipped = codes[...].T
    for p in range(patterns):
        pmask[p] = jnp.broadcast_to(jnp.where(flipped[:, 1:2] == p, 1.0, 0.0), (blocks, points)).astype(BF16)
    sub = lax.broadcasted_iota(I32, (keys, blocks), 0)
    for part in range(3):
        scatter_hot[part] = jnp.where(sub == code[part], 1.0, 0.0).astype(BF16)

    loads["table"].wait()
    for p in range(patterns):
        th, tl = split(table_v[p])
        spot = slice(p * points, (p + 1) * points)
        nn_w[spot, :points] = th
        nn_w[spot, points:] = tl

    def project(values):
        parts = []
        for value in values:
            parts.extend(split(value))
        wide = jnp.concatenate(
            [jnp.concatenate([v * pmask[p] for v in parts], axis=0) for p in range(patterns)], axis=1
        )
        got = dot(wide, nn_w[...])
        ends = []
        for i in range(3):
            both = got[2 * i * blocks : (2 * i + 1) * blocks] + got[(2 * i + 1) * blocks : (2 * i + 2) * blocks]
            ends.append(jnp.concatenate(split(folded(both)), axis=1))
        return ends

    other = pl.multiple_of((1 - core) * half, 8)
    mine = pl.multiple_of(core * half, 8)

    def to_sibling(t, count):
        copy = pltpu.make_async_remote_copy(
            src_ref=d_all.at[t : t + count, pl.ds(other, half), :],
            dst_ref=c_all.at[t : t + count],
            send_sem=core_send.at[t],
            recv_sem=core_recv.at[t],
            device_id=sibling,
            device_id_type=MESH,
        )
        copy.start()
        return copy

    done = []

    def stage0(group, arriving):
        copies = []
        for part in range(3):
            if part < len(arriving):
                arriving[part].wait_recv()
                done.append(arriving[part])
            t = 3 * group + part
            c_all[t] = c_all[t] + d_all[t, pl.ds(mine, half), :]
            axis = axes[part][0]
            for step in range(1, n):
                to = lax.rem(place[axis] + step, n)
                slot = part * (n - 1) + step - 1
                copies.append(
                    pltpu.make_async_remote_copy(
                        src_ref=c_all.at[t, pl.ds(pl.multiple_of(to * rows1, 8), rows1), :],
                        dst_ref=r1_all.at[step - 1, t],
                        send_sem=axis_send.at[group, slot],
                        recv_sem=axis_recv.at[group, slot],
                        device_id=shifted(*[step if a == axis else 0 for a in range(3)]),
                        device_id_type=MESH,
                    )
                )
                copies[-1].start()
        done.extend(copies)
        return copies

    loads["mass"].wait()
    loads["prev"].wait()
    loads["base"].wait()
    force = project([base_v[c] - mass_v[...] * prev_v[c] for c in range(3)])
    pl.semaphore_wait(barrier, len(partners))
    for partner in beside:
        pl.semaphore_signal(ready.at[0], inc=1, device_id=partner, device_id_type=MESH)
    core0 = []
    for c in range(3):
        d_all[c] = folded(dot(scatter_hot[c], force[c]))
        core0.append(to_sibling(c, 1))
    owner_col = lax.broadcast_in_dim(flipped[:, 2:3], (blocks, blocks), (0, 1))
    same = owner_col == codes[2:3, :]
    down = lax.broadcasted_iota(I32, (blocks, blocks), 0)
    along = lax.broadcasted_iota(I32, (blocks, blocks), 1)
    slot_row = jnp.sum(jnp.where(same & (down < along), 1.0, 0.0), axis=0, keepdims=True)
    slot_col = jnp.sum(jnp.where(same & (along < down), 1.0, 0.0), axis=1, keepdims=True)
    owners = 2 * chips
    spot_of = slot_row * owners + codes[2:3, :]
    hot = jnp.where(lax.broadcasted_iota(I32, (cap * owners, blocks), 0).astype(F32) == spot_of, 1.0, 0.0).astype(BF16)
    slots = folded(dot(hot, jnp.concatenate(split(mass_v[...]), axis=1)))
    mark = slot_col * tags + flipped[:, 3:4]
    marked = jnp.where(lax.broadcasted_iota(I32, (blocks, points), 1).astype(F32) == mark, 1.0, 0.0).astype(BF16)
    owner_hot = jnp.where(lax.broadcasted_iota(I32, (owners, blocks), 0).astype(F32) == codes[2:3, :], 1.0, 0.0).astype(BF16)
    marks = dot(owner_hot, marked)
    for s in range(2):
        for j in range(cap):
            slot_own[s, :, j, :] = slots[j * owners + s * chips : j * owners + (s + 1) * chips]
        slot_own[s, :, cap, :] = marks[s * chips : (s + 1) * chips]
    slot_copy = pltpu.make_async_remote_copy(
        src_ref=slot_own.at[1 - core],
        dst_ref=slot_out.at[core],
        send_sem=core_send.at[4],
        recv_sem=core_recv.at[4],
        device_id=sibling,
        device_id_type=MESH,
    )
    slot_copy.start()
    slot_out[core] = slot_own[core]
    chip = (z * n + y) * n + x
    axis0 = stage0(0, core0)
    pl.semaphore_wait(ready.at[0], len(beside))
    for partner in beside:
        pl.semaphore_signal(ready.at[1], inc=1, device_id=partner, device_id_type=MESH)
    load = project([base_v[c] for c in range(3)])
    for c in range(3):
        d_all[3 + c] = folded(dot(scatter_hot[c], load[c]))
    core1 = to_sibling(3, 3)
    pl.semaphore_wait(ready.at[1], len(beside))
    slot_copy.wait_recv()
    done.append(slot_copy)
    slot_in[:, chip] = slot_out[:, chip]

    def send_slots(some):
        for dx, dy, dz in some:
            to = (lax.rem(z + dz, n) * n + lax.rem(y + dy, n)) * n + lax.rem(x + dx, n)
            pltpu.make_async_remote_copy(
                src_ref=slot_out.at[:, to],
                dst_ref=slot_in.at[:, chip],
                send_sem=slot_send,
                recv_sem=slot_recv,
                device_id=shifted(dx, dy, dz),
                device_id_type=MESH,
            ).start()


    loads["stiff"].wait()
    loads["srow"].wait()
    loads["scol"].wait()
    loads["start"].wait()
    for i in range(stiff_v.shape[0]):
        stiff_hi[i], stiff_lo[i] = split(stiff_v[i].T)


    axis1 = stage0(1, [core1])

    flat = sorted(((a, b) for a in range(n) for b in range(n) if a or b), key=far, reverse=True)

    def stage1(group, copies):
        for copy in copies:
            copy.wait_recv()
        for part in range(3):
            own = pl.multiple_of(place[axes[part][0]] * rows1, 8)
            t = 3 * group + part
            total = c_all[t, pl.ds(own, rows1), :]
            for step in range(1, n):
                total = total + r1_all[step - 1, t]
            for s in range(n * n):
                f_all[t, s] = total[s * cols : (s + 1) * cols]
        for i, (da, db) in enumerate(flat):
            for part in range(3):
                _, a, b = axes[part]
                to = lax.rem(place[a] + da, n) * n + lax.rem(place[b] + db, n)
                step = [0, 0, 0]
                step[a], step[b] = da, db
                t = 3 * group + part
                pltpu.make_async_remote_copy(
                    src_ref=f_all.at[t, to],
                    dst_ref=r2_all.at[t, i],
                    send_sem=plane_send.at[group],
                    recv_sem=plane_recv.at[group],
                    device_id=shifted(*step),
                    device_id_type=MESH,
                ).start()

    def all_of(ref, send, recv):
        return pltpu.make_async_remote_copy(
            src_ref=ref, dst_ref=ref, send_sem=send, recv_sem=recv, device_id=sibling, device_id_type=MESH
        )

    def plane_end(group):
        copy = all_of(r2_all.at[3 * group : 3 * group + 3], plane_send.at[group], plane_recv.at[group])
        copy.wait_recv()
        done.append(copy)
        ends = []
        for part in range(3):
            _, a, b = axes[part]
            t = 3 * group + part
            total = f_all[t, place[a] * n + place[b]]
            for i in range(len(flat)):
                total = total + r2_all[t, i]
            ends.append(total)
        return jnp.concatenate(ends, axis=1)

    stage1(0, axis0)

    def stacked(value):
        vh, vl = split(value)
        vh, vl = vh.astype(F32), vl.astype(F32)
        return jnp.concatenate([vh, vl, jnp.zeros((8, value.shape[1]), F32)], axis=0).astype(BF16)

    group_rows = n * cols

    def couple(value, turn):
        lhs = stacked(value)
        total = jnp.zeros((group_rows, width), F32)
        row_at = lax.broadcasted_iota(I32, (group_rows, width), 0)
        col_at = lax.broadcasted_iota(I32, (cols, width), 0)
        for i in range(stiff_v.shape[0]):
            a = dot(lhs, stiff_hi[i])
            b = dot(lhs, stiff_lo[i])
            every = a[0:cols] + a[cols : 2 * cols] + b[0:cols]
            picked = jnp.sum(jnp.where(col_at == scol_s[i], every, 0.0), axis=0, keepdims=True)
            total = total + jnp.where(row_at == srow_s[i], picked, 0.0)
        for s in range(n):
            cpl_out[turn, s] = total[s * cols : (s + 1) * cols]
        copies = []
        for step in range(1, n):
            copies.append(
                pltpu.make_async_remote_copy(
                    src_ref=cpl_out.at[turn, lax.rem(x + step, n)],
                    dst_ref=cpl_in.at[turn, step - 1],
                    send_sem=cpl_send.at[turn, step - 1],
                    recv_sem=cpl_recv.at[turn, step - 1],
                    device_id=shifted(step, 0, 0),
                    device_id_type=MESH,
                )
            )
            copies[-1].start()
        done.extend(copies)
        return copies

    def coupled(turn, copies):
        total = cpl_out[turn, x]
        for step in range(1, n):
            copies[step - 1].wait_recv()
            total = total + cpl_in[turn, step - 1]
        return total

    field0 = jnp.concatenate([start_v[c] for c in range(3)], axis=1)
    cpl_copies0 = couple(field0, 0)

    send_slots(everywhere)

    loads["inverse"].wait()
    for i in range(cols):
        inverse_hi[i], inverse_lo[i] = split(inverse_v[i].T)
    flipped = codes[...].T
    lane = lax.broadcasted_iota(I32, (blocks, half), 1).astype(F32)
    pattern_wide[...] = jnp.broadcast_to(flipped[:, 1:2], (blocks, points))
    for side in range(2):
        gather_hot[side] = jnp.where(lane == flipped[:, 0:1] - side * half, 1.0, 0.0).astype(BF16)

    def correct(residual):
        lhs = stacked(residual)
        total = jnp.zeros((cols, width), F32)
        col_at = lax.broadcasted_iota(I32, (cols, width), 0)
        for k in range(cols):
            a = dot(lhs, inverse_hi[k])
            b = dot(lhs, inverse_lo[k])
            total = total + jnp.where(col_at == k, a[0:cols] + a[cols : 2 * cols] + b[0:cols], 0.0)
        return total


    for p in range(patterns):
        th, tl = split(table_v[p].T)
        spot = slice(p * points, (p + 1) * points)
        nt_w[:points, spot] = th
        nt_w[points:, spot] = th
        nt_lo[:, spot] = tl
    stage1(1, axis1)
    field1 = field0 + correct(plane_end(0) - coupled(0, cpl_copies0))
    cpl_copies1 = couple(field1, 1)

    rows_s[...] = jnp.zeros_like(rows_s)
    for c in range(3):
        rows_s[c * cols : (c + 1) * cols, :] = field1[:, c * points : (c + 1) * points]
    uh, ul = split(rows_s[...])
    spread = dot(jnp.concatenate([uh, ul], axis=1), nt_w[...]) + dot(uh, nt_lo[...])

    arrived = all_of(slot_in.at[:, pl.ds(0, chips - 1)], slot_send, slot_recv)
    arrived.wait_recv()
    done.append(arrived)
    marks = jnp.concatenate([slot_in[s, :, cap, :] for s in range(2)], axis=0).T
    summed = None
    for j in range(cap):
        values = jnp.concatenate([slot_in[s, :, j, :] for s in range(2)], axis=0)
        got = dot(
            marks[j * tags : (j + 1) * tags].astype(BF16), jnp.concatenate(split(values), axis=1)
        )
        summed = got if summed is None else summed + got
    summed = folded(summed)
    wide_s[...] = jnp.zeros_like(wide_s)
    for p in range(patterns):
        for c in range(3):
            wide_s[c * cols : (c + 1) * cols, p * points : (p + 1) * points] = summed[p * cols : (p + 1) * cols]
    eh, el = split(spread * wide_s[...])
    rows_s[...] = folded(dot(eh, nn_w[...]) + dot(el, nn_w[...]))
    load = plane_end(1) - jnp.concatenate([rows_s[c * cols : (c + 1) * cols, :] for c in range(3)], axis=1)
    field2 = field1 + correct(load - coupled(1, cpl_copies1))

    for c in range(3):
        out_u[c] = field2[:, c * points : (c + 1) * points]
    home = pl.multiple_of(core * chips, 8)
    field[home + chip] = field2
    planes = sorted(range(n), key=lambda d: -min(d, n - d))
    for dz in planes:
        for offsets in everywhere:
            if offsets[2] == dz:
                pltpu.make_async_remote_copy(
                    src_ref=field.at[home + chip],
                    dst_ref=field.at[home + chip],
                    send_sem=back_send.at[dz],
                    recv_sem=back_recv.at[dz],
                    device_id=shifted(*offsets),
                    device_id_type=MESH,
                ).start()
    homes = []
    for dz in planes:
        first_row = home + lax.rem(z - dz + n, n) * (n * n)
        copy = all_of(field.at[pl.ds(first_row, n * n if dz else n * n - 1)], back_send.at[dz], back_recv.at[dz])
        copy.wait_recv()
        done.append(copy)
        view = field.at[pl.ds(first_row, n * n)]
        copy = pltpu.make_async_remote_copy(
            src_ref=view,
            dst_ref=view,
            send_sem=home_send.at[dz],
            recv_sem=home_recv.at[dz],
            device_id=sibling,
            device_id_type=MESH,
        )
        copy.start()
        homes.append(copy)
        done.append(copy)

    def gathered(side):
        fh, fl = split(field[pl.ds(side * chips, chips)].reshape(half, width))
        hot = gather_hot[side]
        spots = [slice(c * points, (c + 1) * points) for c in range(3)]
        return [dot(hot, jnp.concatenate([fh[:, spot], fl[:, spot]], axis=1)) for spot in spots]

    near = gathered(core)
    for copy in homes:
        copy.wait_recv()
    rows = [(u + v).astype(BF16) for u, v in zip(near, gathered(1 - core))]
    got = jnp.concatenate(rows, axis=0)
    pattern_at = pattern_wide[...]
    acc = [jnp.zeros((blocks, points), F32) for _ in range(3)]
    for j in range(patterns // 2):
        spot = slice(2 * j * points, 2 * (j + 1) * points)
        pair = dot(got, nt_w[:, spot]) + dot(got[:, :points], nt_lo[:, spot])
        for c in range(3):
            mid = pair[c * blocks : (c + 1) * blocks]
            acc[c] = jnp.where(pattern_at == 2 * j, mid[:, :points], acc[c])
            acc[c] = jnp.where(pattern_at == 2 * j + 1, mid[:, points:], acc[c])
    for c in range(3):
        out_i[c] = acc[c]

    for copy in done:
        copy.wait_send()


def deliver(u_ref, i_ref, out_u, out_i, sem):
    copies = [pltpu.make_async_copy(src, dst, sem.at[k]) for k, (src, dst) in enumerate(((i_ref, out_i), (u_ref, out_u)))]
    for copy in copies:
        copy.start()
    for copy in copies:
        copy.wait()


def on_device(
    n,
    traction_base,
    added_mass,
    interface_prev,
    patch_route,
    basis_pattern,
    column_block,
    basis_values_table,
    stiffness,
    stiff_row,
    stiff_col,
    block_inverse,
    previous_shell_displacement,
):
    blocks = added_mass.shape[0]
    patterns, points, _ = basis_values_table.shape
    width = 3 * points
    cols = 4
    chips = n * n * n
    half, rows1 = chips * cols, n * n * cols
    keys = 2 * half
    stiffs = stiffness.shape[0]
    any_, vmem = (pl.BlockSpec(memory_space=m) for m in (pl.ANY, pltpu.VMEM))
    V = pltpu.VMEM
    dma = pltpu.SemaphoreType.DMA
    out_u, out_i = pl.pallas_call(
        functools.partial(kernel, n),
        out_shape=(
            pltpu.VMEM((3, cols, points), F32),
            pltpu.VMEM((3, blocks, points), F32),
        ),
        in_specs=[any_] * 12,
        out_specs=(vmem, vmem),
        scratch_shapes=[
            V((3, blocks, points), F32),
            V((blocks, points), F32),
            V((3, blocks, points), F32),
            V((1, blocks), I32),
            V((1, blocks), I32),
            V((1, blocks), I32),
            V((patterns, points, points), F32),
            V((stiffs, width, width), F32),
            pltpu.SMEM((stiffs,), I32),
            pltpu.SMEM((stiffs,), I32),
            V((cols, width, width), F32),
            V((3, cols, points), F32),
            V((stiffs, width, width), BF16),
            V((stiffs, width, width), BF16),
            V((cols, width, width), BF16),
            V((cols, width, width), BF16),
            V((patterns * points, 2 * points), BF16),
            V((2 * points, patterns * points), BF16),
            V((points, patterns * points), BF16),
            V((128, blocks), F32),
            V((patterns, blocks, points), BF16),
            V((3, keys, blocks), BF16),
            V((2, blocks, half), BF16),
            V((blocks, points), F32),
            V((6, keys, points), F32),
            V((6, half, points), F32),
            V((n - 1, 6, rows1, points), F32),
            V((6, n * n, cols, points), F32),
            V((6, n * n - 1, cols, points), F32),
            V((2, chips, 5, points), F32),
            V((2, chips, 5, points), F32),
            V((2, chips, 5, points), F32),
            V((2, n, cols, width), F32),
            V((2, n - 1, cols, width), F32),
            V((16, points), F32),
            V((16, patterns * points), F32),
            V((2 * chips, cols, width), F32),
            dma((12,)),
            dma((5,)),
            dma((5,)),
            pltpu.SemaphoreType.REGULAR((2,)),
            dma((2, 3 * (n - 1))),
            dma((2, 3 * (n - 1))),
            dma((2,)),
            dma((2,)),
            dma,
            dma,
            dma((2, n - 1)),
            dma((2, n - 1)),
            dma((n,)),
            dma((n,)),
            dma((n,)),
            dma((n,)),
        ],
        compiler_params=pltpu.CompilerParams(
            collective_id=0, has_side_effects=True, vmem_limit_bytes=62 * 1024 * 1024
        ),
    )(
        jnp.transpose(traction_base, (1, 0, 2)),
        added_mass,
        jnp.transpose(interface_prev, (1, 0, 2)),
        patch_route.reshape(1, blocks),
        basis_pattern.reshape(1, blocks),
        column_block.reshape(1, blocks),
        basis_values_table,
        stiffness,
        stiff_row,
        stiff_col,
        block_inverse,
        jnp.transpose(previous_shell_displacement, (1, 0, 2)),
    )
    out_u, out_i = pl.pallas_call(
        deliver,
        out_shape=(
            jax.ShapeDtypeStruct((3, cols, points), F32),
            jax.ShapeDtypeStruct((3, blocks, points), F32),
        ),
        in_specs=[vmem, vmem],
        out_specs=(any_, any_),
        scratch_shapes=[dma((2,))],
        compiler_params=pltpu.CompilerParams(vmem_limit_bytes=4 * 1024 * 1024),
    )(*(pltpu.with_memory_space_constraint(v, pltpu.VMEM) for v in (out_u, out_i)))
    return jnp.transpose(out_u, (1, 0, 2)), jnp.transpose(out_i, (1, 0, 2))


def solution(mesh):
    both = P(("fluid", "shell"))
    n = mesh.shape["shell"]
    return jax.shard_map(
        functools.partial(on_device, n),
        mesh=mesh,
        in_specs=(
            P(("fluid", "shell"), None, None),
            P(("fluid", "shell"), None),
            P(("fluid", "shell"), None, None),
            P(("fluid", "shell"), None),
            both,
            both,
            P(),
            P(("fluid", "shell"), None, None),
            both,
            both,
            P(("fluid", "shell"), None, None),
            P(("fluid", "shell"), None, None),
        ),
        out_specs=(P(("fluid", "shell"), None, None), P(("fluid", "shell"), None, None)),
        check_vma=False,
    )
```

```python
import functools

import jax
import jax.numpy as jnp
from jax import lax
from jax.experimental import pallas as pl
from jax.experimental.pallas import tpu as pltpu
from jax.sharding import PartitionSpec as P

F32, BF16, I32 = jnp.float32, jnp.bfloat16, jnp.int32
NT = (((1,), (1,)), ((), ()))
NN = (((1,), (0,)), ((), ()))
def split(value):
    high = value.astype(BF16)
    low = (value - high.astype(F32)).astype(BF16)
    return high, low


def dot(a, b, dims=NN):
    return lax.dot_general(a, b, dims, preferred_element_type=F32)


def kernel(
    n,
    base_h,
    mass_h,
    prev_h,
    route_h,
    pattern_h,
    column_h,
    table_h,
    stiff_h,
    srow_h,
    scol_h,
    inverse_h,
    start_h,
    out_u,
    out_i,
    base_v,
    mass_v,
    prev_v,
    route_v,
    pattern_v,
    column_v,
    table_v,
    stiff_v,
    srow_s,
    scol_s,
    inverse_v,
    start_v,
    stiff_hi,
    stiff_lo,
    inverse_hi,
    inverse_lo,
    nn_w,
    nt_w,
    nt_lo,
    codes,
    pmask,
    scatter_hot,
    gather_hot,
    pattern_wide,
    d_all,
    c_all,
    r1_all,
    f_all,
    r2_all,
    slot_own,
    slot_out,
    slot_in,
    cpl_out,
    cpl_in,
    rows_s,
    wide_s,
    field,
    own_field,
    load_sem,
    core_send,
    core_recv,
    ready,
    axis_send,
    axis_recv,
    plane_send,
    plane_recv,
    slot_send,
    slot_recv,
    cpl_send,
    cpl_recv,
    back_send,
    back_recv,
    home_send,
    home_recv,
):
    fluid, x = lax.axis_index("fluid"), lax.axis_index("shell")
    core = lax.rem(fluid, 2)
    y = lax.rem(lax.div(fluid, 2), n)
    z = lax.div(fluid, 2 * n)
    cols = 4
    half, rows1 = n * n * n * cols, n * n * cols
    blocks = mass_v.shape[0]
    patterns = table_v.shape[0]
    points = table_v.shape[1]
    keys = 2 * half
    chips = n * n * n
    width = 3 * points
    cap = 4
    tags = patterns * cols
    place = (x, y, z)
    axes = ((0, 1, 2), (1, 2, 0), (2, 0, 1))
    MESH = pl.DeviceIdType.MESH

    def shifted(dx, dy, dz):
        to_x, to_y, to_z = lax.rem(x + dx, n), lax.rem(y + dy, n), lax.rem(z + dz, n)
        return ((to_z * n + to_y) * 2 + core, to_x)

    def crossed(dx, dy, dz):
        to_x, to_y, to_z = lax.rem(x + dx, n), lax.rem(y + dy, n), lax.rem(z + dz, n)
        return ((to_z * n + to_y) * 2 + 1 - core, to_x)

    def far(offsets):
        return sum(min(v, n - v) for v in offsets)

    everywhere = sorted(
        ((a, b, c) for c in range(n) for b in range(n) for a in range(n) if a or b or c),
        key=far,
        reverse=True,
    )
    sibling = (fluid + 1 - 2 * core, x)

    sources = (route_h, pattern_h, column_h, mass_h, prev_h, base_h, table_h, start_h, srow_h, scol_h, stiff_h, inverse_h)
    places = (route_v, pattern_v, column_v, mass_v, prev_v, base_v, table_v, start_v, srow_s, scol_s, stiff_v, inverse_v)
    names = ("route", "pattern", "column", "mass", "prev", "base", "table", "start", "srow", "scol", "stiff", "inverse")
    loads = {}
    for i, (name, src, dst) in enumerate(zip(names, sources, places)):
        loads[name] = pltpu.make_async_copy(src, dst, load_sem.at[i])
        loads[name].start()

    barrier = pltpu.get_barrier_semaphore()
    beside = [shifted(*[step if a == axis else 0 for a in range(3)]) for axis in range(3) for step in range(1, n)]
    partners = [sibling] + beside
    for partner in partners:
        pl.semaphore_signal(barrier, inc=1, device_id=partner, device_id_type=MESH)

    def folded(pair):
        return pair[:, :points] + pair[:, points:]

    for name in ("route", "pattern", "column"):
        loads[name].wait()
    route, column, pattern = route_v[...], column_v[...], pattern_v[...]
    bits = n.bit_length() - 1
    px = route & (n - 1)
    pcore = (route >> bits) & 1
    py = (route >> (bits + 1)) & (n - 1)
    pz = route >> (2 * bits + 1)
    where_is = (px, py, pz)
    code = [
        (((pcore * n + where_is[a]) * n + where_is[b]) * n + where_is[c]) * cols + column
        for a, b, c in axes
    ]
    codes[...] = jnp.zeros_like(codes)
    codes[0:1, :] = ((((pcore * n + pz) * n + py) * n + px) * cols + column).astype(F32)
    codes[1:2, :] = pattern.astype(F32)
    codes[2:3, :] = (((pcore * n + pz) * n + py) * n + px).astype(F32)
    codes[3:4, :] = (pattern * cols + column).astype(F32)
    flipped = codes[...].T
    for p in range(patterns):
        pmask[p] = jnp.broadcast_to(jnp.where(flipped[:, 1:2] == p, 1.0, 0.0), (blocks, points)).astype(BF16)
    sub = lax.broadcasted_iota(I32, (keys, blocks), 0)
    for part in range(3):
        scatter_hot[part] = jnp.where(sub == code[part], 1.0, 0.0).astype(BF16)

    loads["table"].wait()
    for p in range(patterns):
        th, tl = split(table_v[p])
        spot = slice(p * points, (p + 1) * points)
        nn_w[spot, :points] = th
        nn_w[spot, points:] = tl

    def project(values):
        parts = []
        for value in values:
            parts.extend(split(value))
        wide = jnp.concatenate(
            [jnp.concatenate([v * pmask[p] for v in parts], axis=0) for p in range(patterns)], axis=1
        )
        got = dot(wide, nn_w[...])
        ends = []
        for i in range(3):
            both = got[2 * i * blocks : (2 * i + 1) * blocks] + got[(2 * i + 1) * blocks : (2 * i + 2) * blocks]
            ends.append(jnp.concatenate(split(folded(both)), axis=1))
        return ends

    other = pl.multiple_of((1 - core) * half, 8)
    mine = pl.multiple_of(core * half, 8)

    def to_sibling(t, count):
        copy = pltpu.make_async_remote_copy(
            src_ref=d_all.at[t : t + count, pl.ds(other, half), :],
            dst_ref=c_all.at[t : t + count],
            send_sem=core_send.at[t],
            recv_sem=core_recv.at[t],
            device_id=sibling,
            device_id_type=MESH,
        )
        copy.start()
        return copy

    done = []

    def stage0(group, arriving):
        copies = []
        for part in range(3):
            if part < len(arriving):
                arriving[part].wait_recv()
                done.append(arriving[part])
            t = 3 * group + part
            c_all[t] = c_all[t] + d_all[t, pl.ds(mine, half), :]
            axis = axes[part][0]
            for step in range(1, n):
                to = lax.rem(place[axis] + step, n)
                slot = part * (n - 1) + step - 1
                copies.append(
                    pltpu.make_async_remote_copy(
                        src_ref=c_all.at[t, pl.ds(pl.multiple_of(to * rows1, 8), rows1), :],
                        dst_ref=r1_all.at[step - 1, t],
                        send_sem=axis_send.at[group, slot],
                        recv_sem=axis_recv.at[group, slot],
                        device_id=shifted(*[step if a == axis else 0 for a in range(3)]),
                        device_id_type=MESH,
                    )
                )
                copies[-1].start()
        done.extend(copies)
        return copies

    loads["mass"].wait()
    loads["prev"].wait()
    loads["base"].wait()
    force = project([base_v[c] - mass_v[...] * prev_v[c] for c in range(3)])
    pl.semaphore_wait(barrier, len(partners))
    for partner in beside:
        pl.semaphore_signal(ready.at[0], inc=1, device_id=partner, device_id_type=MESH)
    core0 = []
    for c in range(3):
        d_all[c] = folded(dot(scatter_hot[c], force[c]))
        core0.append(to_sibling(c, 1))
    owner_col = lax.broadcast_in_dim(flipped[:, 2:3], (blocks, blocks), (0, 1))
    same = owner_col == codes[2:3, :]
    down = lax.broadcasted_iota(I32, (blocks, blocks), 0)
    along = lax.broadcasted_iota(I32, (blocks, blocks), 1)
    slot_row = jnp.sum(jnp.where(same & (down < along), 1.0, 0.0), axis=0, keepdims=True)
    slot_col = jnp.sum(jnp.where(same & (along < down), 1.0, 0.0), axis=1, keepdims=True)
    owners = 2 * chips
    spot_of = slot_row * owners + codes[2:3, :]
    hot = jnp.where(lax.broadcasted_iota(I32, (cap * owners, blocks), 0).astype(F32) == spot_of, 1.0, 0.0).astype(BF16)
    slots = folded(dot(hot, jnp.concatenate(split(mass_v[...]), axis=1)))
    mark = slot_col * tags + flipped[:, 3:4]
    marked = jnp.where(lax.broadcasted_iota(I32, (blocks, points), 1).astype(F32) == mark, 1.0, 0.0).astype(BF16)
    owner_hot = jnp.where(lax.broadcasted_iota(I32, (owners, blocks), 0).astype(F32) == codes[2:3, :], 1.0, 0.0).astype(BF16)
    marks = dot(owner_hot, marked)
    for s in range(2):
        for j in range(cap):
            slot_own[s, :, j, :] = slots[j * owners + s * chips : j * owners + (s + 1) * chips]
        slot_own[s, :, cap, :] = marks[s * chips : (s + 1) * chips]
    slot_copy = pltpu.make_async_remote_copy(
        src_ref=slot_own.at[1 - core],
        dst_ref=slot_out.at[core],
        send_sem=core_send.at[4],
        recv_sem=core_recv.at[4],
        device_id=sibling,
        device_id_type=MESH,
    )
    slot_copy.start()
    slot_out[core] = slot_own[core]
    chip = (z * n + y) * n + x
    axis0 = stage0(0, core0)
    pl.semaphore_wait(ready.at[0], len(beside))
    for partner in beside:
        pl.semaphore_signal(ready.at[1], inc=1, device_id=partner, device_id_type=MESH)
    load = project([base_v[c] for c in range(3)])
    for c in range(3):
        d_all[3 + c] = folded(dot(scatter_hot[c], load[c]))
    core1 = to_sibling(3, 3)
    pl.semaphore_wait(ready.at[1], len(beside))
    slot_copy.wait_recv()
    done.append(slot_copy)
    slot_in[:, chip] = slot_out[:, chip]

    def send_slots(some):
        for dx, dy, dz in some:
            to = (lax.rem(z + dz, n) * n + lax.rem(y + dy, n)) * n + lax.rem(x + dx, n)
            pltpu.make_async_remote_copy(
                src_ref=slot_out.at[:, to],
                dst_ref=slot_in.at[:, chip],
                send_sem=slot_send,
                recv_sem=slot_recv,
                device_id=shifted(dx, dy, dz),
                device_id_type=MESH,
            ).start()


    loads["stiff"].wait()
    loads["srow"].wait()
    loads["scol"].wait()
    loads["start"].wait()
    for i in range(stiff_v.shape[0]):
        stiff_hi[i], stiff_lo[i] = split(stiff_v[i].T)


    axis1 = stage0(1, [core1])

    flat = sorted(((a, b) for a in range(n) for b in range(n) if a or b), key=far, reverse=True)

    def stage1(group, copies):
        for copy in copies:
            copy.wait_recv()
        for part in range(3):
            own = pl.multiple_of(place[axes[part][0]] * rows1, 8)
            t = 3 * group + part
            total = c_all[t, pl.ds(own, rows1), :]
            for step in range(1, n):
                total = total + r1_all[step - 1, t]
            for s in range(n * n):
                f_all[t, s] = total[s * cols : (s + 1) * cols]
        for i, (da, db) in enumerate(flat):
            for part in range(3):
                _, a, b = axes[part]
                to = lax.rem(place[a] + da, n) * n + lax.rem(place[b] + db, n)
                step = [0, 0, 0]
                step[a], step[b] = da, db
                t = 3 * group + part
                pltpu.make_async_remote_copy(
                    src_ref=f_all.at[t, to],
                    dst_ref=r2_all.at[t, i],
                    send_sem=plane_send.at[group],
                    recv_sem=plane_recv.at[group],
                    device_id=shifted(*step),
                    device_id_type=MESH,
                ).start()

    def all_of(ref, send, recv):
        return pltpu.make_async_remote_copy(
            src_ref=ref, dst_ref=ref, send_sem=send, recv_sem=recv, device_id=sibling, device_id_type=MESH
        )

    def plane_end(group):
        copy = all_of(r2_all.at[3 * group : 3 * group + 3], plane_send.at[group], plane_recv.at[group])
        copy.wait_recv()
        done.append(copy)
        ends = []
        for part in range(3):
            _, a, b = axes[part]
            t = 3 * group + part
            total = f_all[t, place[a] * n + place[b]]
            for i in range(len(flat)):
                total = total + r2_all[t, i]
            ends.append(total)
        return jnp.concatenate(ends, axis=1)

    stage1(0, axis0)

    def stacked(value):
        vh, vl = split(value)
        vh, vl = vh.astype(F32), vl.astype(F32)
        return jnp.concatenate([vh, vl, jnp.zeros((8, value.shape[1]), F32)], axis=0).astype(BF16)

    group_rows = n * cols

    def couple(value, turn):
        lhs = stacked(value)
        total = jnp.zeros((group_rows, width), F32)
        row_at = lax.broadcasted_iota(I32, (group_rows, width), 0)
        col_at = lax.broadcasted_iota(I32, (cols, width), 0)
        for i in range(stiff_v.shape[0]):
            a = dot(lhs, stiff_hi[i])
            b = dot(lhs, stiff_lo[i])
            every = a[0:cols] + a[cols : 2 * cols] + b[0:cols]
            picked = jnp.sum(jnp.where(col_at == scol_s[i], every, 0.0), axis=0, keepdims=True)
            total = total + jnp.where(row_at == srow_s[i], picked, 0.0)
        for s in range(n):
            cpl_out[turn, s] = total[s * cols : (s + 1) * cols]
        copies = []
        for step in range(1, n):
            copies.append(
                pltpu.make_async_remote_copy(
                    src_ref=cpl_out.at[turn, lax.rem(x + step, n)],
                    dst_ref=cpl_in.at[turn, step - 1],
                    send_sem=cpl_send.at[turn, step - 1],
                    recv_sem=cpl_recv.at[turn, step - 1],
                    device_id=shifted(step, 0, 0),
                    device_id_type=MESH,
                )
            )
            copies[-1].start()
        done.extend(copies)
        return copies

    def coupled(turn, copies):
        total = cpl_out[turn, x]
        for step in range(1, n):
            copies[step - 1].wait_recv()
            total = total + cpl_in[turn, step - 1]
        return total

    field0 = jnp.concatenate([start_v[c] for c in range(3)], axis=1)
    cpl_copies0 = couple(field0, 0)

    send_slots(everywhere)

    loads["inverse"].wait()
    for i in range(cols):
        inverse_hi[i], inverse_lo[i] = split(inverse_v[i].T)
    flipped = codes[...].T
    lane = lax.broadcasted_iota(I32, (blocks, half), 1).astype(F32)
    pattern_wide[...] = jnp.broadcast_to(flipped[:, 1:2], (blocks, points))
    for side in range(2):
        gather_hot[side] = jnp.where(lane == flipped[:, 0:1] - side * half, 1.0, 0.0).astype(BF16)

    def correct(residual):
        lhs = stacked(residual)
        total = jnp.zeros((cols, width), F32)
        col_at = lax.broadcasted_iota(I32, (cols, width), 0)
        for k in range(cols):
            a = dot(lhs, inverse_hi[k])
            b = dot(lhs, inverse_lo[k])
            total = total + jnp.where(col_at == k, a[0:cols] + a[cols : 2 * cols] + b[0:cols], 0.0)
        return total


    for p in range(patterns):
        th, tl = split(table_v[p].T)
        spot = slice(p * points, (p + 1) * points)
        nt_w[:points, spot] = th
        nt_w[points:, spot] = th
        nt_lo[:, spot] = tl
    stage1(1, axis1)
    field1 = field0 + correct(plane_end(0) - coupled(0, cpl_copies0))
    cpl_copies1 = couple(field1, 1)

    rows_s[...] = jnp.zeros_like(rows_s)
    for c in range(3):
        rows_s[c * cols : (c + 1) * cols, :] = field1[:, c * points : (c + 1) * points]
    uh, ul = split(rows_s[...])
    spread = dot(jnp.concatenate([uh, ul], axis=1), nt_w[...]) + dot(uh, nt_lo[...])

    arrived = all_of(slot_in.at[:, pl.ds(0, chips - 1)], slot_send, slot_recv)
    arrived.wait_recv()
    done.append(arrived)
    marks = jnp.concatenate([slot_in[s, :, cap, :] for s in range(2)], axis=0).T
    summed = None
    for j in range(cap):
        values = jnp.concatenate([slot_in[s, :, j, :] for s in range(2)], axis=0)
        got = dot(
            marks[j * tags : (j + 1) * tags].astype(BF16), jnp.concatenate(split(values), axis=1)
        )
        summed = got if summed is None else summed + got
    summed = folded(summed)
    wide_s[...] = jnp.zeros_like(wide_s)
    for p in range(patterns):
        for c in range(3):
            wide_s[c * cols : (c + 1) * cols, p * points : (p + 1) * points] = summed[p * cols : (p + 1) * cols]
    eh, el = split(spread * wide_s[...])
    rows_s[...] = folded(dot(eh, nn_w[...]) + dot(el, nn_w[...]))
    load = plane_end(1) - jnp.concatenate([rows_s[c * cols : (c + 1) * cols, :] for c in range(3)], axis=1)
    field2 = field1 + correct(load - coupled(1, cpl_copies1))

    for c in range(3):
        out_u[c] = field2[:, c * points : (c + 1) * points]
    home = pl.multiple_of((1 - core) * chips, 8)
    away = core * chips + chip
    own_field[...] = field2
    planes = sorted(range(n), key=lambda d: -min(d, n - d))
    for dz in planes:
        for offsets in everywhere + [(0, 0, 0)]:
            if offsets[2] == dz:
                pltpu.make_async_remote_copy(
                    src_ref=own_field,
                    dst_ref=field.at[away],
                    send_sem=back_send.at[dz],
                    recv_sem=back_recv.at[dz],
                    device_id=crossed(*offsets),
                    device_id_type=MESH,
                ).start()
    homes = []
    for dz in planes:
        first_row = home + lax.rem(z - dz + n, n) * (n * n)
        copy = all_of(field.at[pl.ds(first_row, n * n)], back_send.at[dz], back_recv.at[dz])
        copy.wait_recv()
        done.append(copy)
        view = field.at[pl.ds(first_row, n * n)]
        copy = pltpu.make_async_remote_copy(
            src_ref=view,
            dst_ref=view,
            send_sem=home_send.at[dz],
            recv_sem=home_recv.at[dz],
            device_id=sibling,
            device_id_type=MESH,
        )
        copy.start()
        homes.append(copy)
        done.append(copy)

    def gathered(side):
        fh, fl = split(field[pl.ds(side * chips, chips)].reshape(half, width))
        hot = gather_hot[side]
        spots = [slice(c * points, (c + 1) * points) for c in range(3)]
        return [dot(hot, jnp.concatenate([fh[:, spot], fl[:, spot]], axis=1)) for spot in spots]

    near = gathered(1 - core)
    for copy in homes:
        copy.wait_recv()
    rows = [(u + v).astype(BF16) for u, v in zip(near, gathered(core))]
    got = jnp.concatenate(rows, axis=0)
    pattern_at = pattern_wide[...]
    acc = [jnp.zeros((blocks, points), F32) for _ in range(3)]
    for j in range(patterns // 2):
        spot = slice(2 * j * points, 2 * (j + 1) * points)
        pair = dot(got, nt_w[:, spot]) + dot(got[:, :points], nt_lo[:, spot])
        for c in range(3):
            mid = pair[c * blocks : (c + 1) * blocks]
            acc[c] = jnp.where(pattern_at == 2 * j, mid[:, :points], acc[c])
            acc[c] = jnp.where(pattern_at == 2 * j + 1, mid[:, points:], acc[c])
    for c in range(3):
        out_i[c] = acc[c]

    for copy in done:
        copy.wait_send()


def deliver(u_ref, i_ref, out_u, out_i, sem):
    copies = [pltpu.make_async_copy(src, dst, sem.at[k]) for k, (src, dst) in enumerate(((i_ref, out_i), (u_ref, out_u)))]
    for copy in copies:
        copy.start()
    for copy in copies:
        copy.wait()


def on_device(
    n,
    traction_base,
    added_mass,
    interface_prev,
    patch_route,
    basis_pattern,
    column_block,
    basis_values_table,
    stiffness,
    stiff_row,
    stiff_col,
    block_inverse,
    previous_shell_displacement,
):
    blocks = added_mass.shape[0]
    patterns, points, _ = basis_values_table.shape
    width = 3 * points
    cols = 4
    chips = n * n * n
    half, rows1 = chips * cols, n * n * cols
    keys = 2 * half
    stiffs = stiffness.shape[0]
    any_, vmem = (pl.BlockSpec(memory_space=m) for m in (pl.ANY, pltpu.VMEM))
    V = pltpu.VMEM
    dma = pltpu.SemaphoreType.DMA
    out_u, out_i = pl.pallas_call(
        functools.partial(kernel, n),
        out_shape=(
            pltpu.VMEM((3, cols, points), F32),
            pltpu.VMEM((3, blocks, points), F32),
        ),
        in_specs=[any_] * 12,
        out_specs=(vmem, vmem),
        scratch_shapes=[
            V((3, blocks, points), F32),
            V((blocks, points), F32),
            V((3, blocks, points), F32),
            V((1, blocks), I32),
            V((1, blocks), I32),
            V((1, blocks), I32),
            V((patterns, points, points), F32),
            V((stiffs, width, width), F32),
            pltpu.SMEM((stiffs,), I32),
            pltpu.SMEM((stiffs,), I32),
            V((cols, width, width), F32),
            V((3, cols, points), F32),
            V((stiffs, width, width), BF16),
            V((stiffs, width, width), BF16),
            V((cols, width, width), BF16),
            V((cols, width, width), BF16),
            V((patterns * points, 2 * points), BF16),
            V((2 * points, patterns * points), BF16),
            V((points, patterns * points), BF16),
            V((128, blocks), F32),
            V((patterns, blocks, points), BF16),
            V((3, keys, blocks), BF16),
            V((2, blocks, half), BF16),
            V((blocks, points), F32),
            V((6, keys, points), F32),
            V((6, half, points), F32),
            V((n - 1, 6, rows1, points), F32),
            V((6, n * n, cols, points), F32),
            V((6, n * n - 1, cols, points), F32),
            V((2, chips, 5, points), F32),
            V((2, chips, 5, points), F32),
            V((2, chips, 5, points), F32),
            V((2, n, cols, width), F32),
            V((2, n - 1, cols, width), F32),
            V((16, points), F32),
            V((16, patterns * points), F32),
            V((2 * chips, cols, width), F32),
            V((cols, width), F32),
            dma((12,)),
            dma((5,)),
            dma((5,)),
            pltpu.SemaphoreType.REGULAR((2,)),
            dma((2, 3 * (n - 1))),
            dma((2, 3 * (n - 1))),
            dma((2,)),
            dma((2,)),
            dma,
            dma,
            dma((2, n - 1)),
            dma((2, n - 1)),
            dma((n,)),
            dma((n,)),
            dma((n,)),
            dma((n,)),
        ],
        compiler_params=pltpu.CompilerParams(
            collective_id=0, has_side_effects=True, vmem_limit_bytes=62 * 1024 * 1024
        ),
    )(
        jnp.transpose(traction_base, (1, 0, 2)),
        added_mass,
        jnp.transpose(interface_prev, (1, 0, 2)),
        patch_route.reshape(1, blocks),
        basis_pattern.reshape(1, blocks),
        column_block.reshape(1, blocks),
        basis_values_table,
        stiffness,
        stiff_row,
        stiff_col,
        block_inverse,
        jnp.transpose(previous_shell_displacement, (1, 0, 2)),
    )
    out_u, out_i = pl.pallas_call(
        deliver,
        out_shape=(
            jax.ShapeDtypeStruct((3, cols, points), F32),
            jax.ShapeDtypeStruct((3, blocks, points), F32),
        ),
        in_specs=[vmem, vmem],
        out_specs=(any_, any_),
        scratch_shapes=[dma((2,))],
        compiler_params=pltpu.CompilerParams(vmem_limit_bytes=4 * 1024 * 1024),
    )(*(pltpu.with_memory_space_constraint(v, pltpu.VMEM) for v in (out_u, out_i)))
    return jnp.transpose(out_u, (1, 0, 2)), jnp.transpose(out_i, (1, 0, 2))


def solution(mesh):
    both = P(("fluid", "shell"))
    n = mesh.shape["shell"]
    return jax.shard_map(
        functools.partial(on_device, n),
        mesh=mesh,
        in_specs=(
            P(("fluid", "shell"), None, None),
            P(("fluid", "shell"), None),
            P(("fluid", "shell"), None, None),
            P(("fluid", "shell"), None),
            both,
            both,
            P(),
            P(("fluid", "shell"), None, None),
            both,
            both,
            P(("fluid", "shell"), None, None),
            P(("fluid", "shell"), None, None),
        ),
        out_specs=(P(("fluid", "shell"), None, None), P(("fluid", "shell"), None, None)),
        check_vma=False,
    )
```

```python
import functools

import jax
import jax.numpy as jnp
from jax import lax
from jax.experimental import pallas as pl
from jax.experimental.pallas import tpu as pltpu
from jax.sharding import PartitionSpec as P

F32, BF16, I32 = jnp.float32, jnp.bfloat16, jnp.int32
NT = (((1,), (1,)), ((), ()))
NN = (((1,), (0,)), ((), ()))
def split(value):
    high = value.astype(BF16)
    low = (value - high.astype(F32)).astype(BF16)
    return high, low


def dot(a, b, dims=NN):
    return lax.dot_general(a, b, dims, preferred_element_type=F32)


def kernel(
    n,
    base_h,
    mass_h,
    prev_h,
    route_h,
    pattern_h,
    column_h,
    table_h,
    stiff_h,
    srow_h,
    scol_h,
    inverse_h,
    start_h,
    out_u,
    out_i,
    base_v,
    mass_v,
    prev_v,
    route_v,
    pattern_v,
    column_v,
    table_v,
    stiff_v,
    srow_s,
    scol_s,
    inverse_v,
    start_v,
    stiff_hi,
    stiff_lo,
    inverse_hi,
    inverse_lo,
    nn_w,
    nt_w,
    codes,
    pmask,
    scatter_hot,
    gather_hot,
    pattern_wide,
    d_all,
    c_all,
    r1_all,
    f_all,
    r2_all,
    slot_own,
    slot_out,
    slot_in,
    cpl_out,
    cpl_in,
    rows_s,
    wide_s,
    field,
    own_field,
    load_sem,
    core_send,
    core_recv,
    ready,
    axis_send,
    axis_recv,
    plane_send,
    plane_recv,
    slot_send,
    slot_recv,
    cpl_send,
    cpl_recv,
    back_send,
    back_recv,
    home_send,
    home_recv,
):
    fluid, x = lax.axis_index("fluid"), lax.axis_index("shell")
    core = lax.rem(fluid, 2)
    y = lax.rem(lax.div(fluid, 2), n)
    z = lax.div(fluid, 2 * n)
    cols = 4
    half, rows1 = n * n * n * cols, n * n * cols
    blocks = mass_v.shape[0]
    patterns = table_v.shape[0]
    points = table_v.shape[1]
    keys = 2 * half
    chips = n * n * n
    width = 3 * points
    cap = 4
    tags = patterns * cols
    place = (x, y, z)
    axes = ((0, 1, 2), (1, 2, 0), (2, 0, 1))
    MESH = pl.DeviceIdType.MESH

    def shifted(dx, dy, dz):
        to_x, to_y, to_z = lax.rem(x + dx, n), lax.rem(y + dy, n), lax.rem(z + dz, n)
        return ((to_z * n + to_y) * 2 + core, to_x)

    def crossed(dx, dy, dz):
        to_x, to_y, to_z = lax.rem(x + dx, n), lax.rem(y + dy, n), lax.rem(z + dz, n)
        return ((to_z * n + to_y) * 2 + 1 - core, to_x)

    def far(offsets):
        return sum(min(v, n - v) for v in offsets)

    everywhere = sorted(
        ((a, b, c) for c in range(n) for b in range(n) for a in range(n) if a or b or c),
        key=far,
        reverse=True,
    )
    sibling = (fluid + 1 - 2 * core, x)

    sources = (route_h, pattern_h, column_h, mass_h, prev_h, base_h, table_h, start_h, srow_h, scol_h, stiff_h, inverse_h)
    places = (route_v, pattern_v, column_v, mass_v, prev_v, base_v, table_v, start_v, srow_s, scol_s, stiff_v, inverse_v)
    names = ("route", "pattern", "column", "mass", "prev", "base", "table", "start", "srow", "scol", "stiff", "inverse")
    loads = {}
    for i, (name, src, dst) in enumerate(zip(names, sources, places)):
        loads[name] = pltpu.make_async_copy(src, dst, load_sem.at[i])
        loads[name].start()

    barrier = pltpu.get_barrier_semaphore()
    beside = [shifted(*[step if a == axis else 0 for a in range(3)]) for axis in range(3) for step in range(1, n)]
    partners = [sibling] + beside
    for partner in partners:
        pl.semaphore_signal(barrier, inc=1, device_id=partner, device_id_type=MESH)

    def folded(pair):
        return pair[:, :points] + pair[:, points:]

    for name in ("route", "pattern", "column"):
        loads[name].wait()
    route, column, pattern = route_v[...], column_v[...], pattern_v[...]
    bits = n.bit_length() - 1
    px = route & (n - 1)
    pcore = (route >> bits) & 1
    py = (route >> (bits + 1)) & (n - 1)
    pz = route >> (2 * bits + 1)
    where_is = (px, py, pz)
    code = [
        (((pcore * n + where_is[a]) * n + where_is[b]) * n + where_is[c]) * cols + column
        for a, b, c in axes
    ]
    codes[...] = jnp.zeros_like(codes)
    codes[0:1, :] = ((((pcore * n + pz) * n + py) * n + px) * cols + column).astype(F32)
    codes[1:2, :] = pattern.astype(F32)
    codes[2:3, :] = (((pcore * n + pz) * n + py) * n + px).astype(F32)
    codes[3:4, :] = (pattern * cols + column).astype(F32)
    flipped = codes[...].T
    for p in range(patterns):
        pmask[p] = jnp.broadcast_to(jnp.where(flipped[:, 1:2] == p, 1.0, 0.0), (blocks, points)).astype(BF16)
    sub = lax.broadcasted_iota(I32, (keys, blocks), 0)
    for part in range(3):
        scatter_hot[part] = jnp.where(sub == code[part], 1.0, 0.0).astype(BF16)

    loads["table"].wait()
    for p in range(patterns):
        th, tl = split(table_v[p])
        spot = slice(p * points, (p + 1) * points)
        nn_w[spot, :points] = th
        nn_w[spot, points:] = tl

    def project(values):
        parts = []
        for value in values:
            parts.extend(split(value))
        wide = jnp.concatenate(
            [jnp.concatenate([v * pmask[p] for v in parts], axis=0) for p in range(patterns)], axis=1
        )
        got = dot(wide, nn_w[...])
        ends = []
        for i in range(3):
            both = got[2 * i * blocks : (2 * i + 1) * blocks] + got[(2 * i + 1) * blocks : (2 * i + 2) * blocks]
            ends.append(jnp.concatenate(split(folded(both)), axis=1))
        return ends

    other = pl.multiple_of((1 - core) * half, 8)
    mine = pl.multiple_of(core * half, 8)

    def to_sibling(t, count):
        copy = pltpu.make_async_remote_copy(
            src_ref=d_all.at[t : t + count, pl.ds(other, half), :],
            dst_ref=c_all.at[t : t + count],
            send_sem=core_send.at[t],
            recv_sem=core_recv.at[t],
            device_id=sibling,
            device_id_type=MESH,
        )
        copy.start()
        return copy

    done = []

    def stage0(group, arriving):
        copies = []
        for part in range(3):
            if part < len(arriving):
                arriving[part].wait_recv()
                done.append(arriving[part])
            t = 3 * group + part
            c_all[t] = c_all[t] + d_all[t, pl.ds(mine, half), :]
            axis = axes[part][0]
            for step in range(1, n):
                to = lax.rem(place[axis] + step, n)
                slot = part * (n - 1) + step - 1
                copies.append(
                    pltpu.make_async_remote_copy(
                        src_ref=c_all.at[t, pl.ds(pl.multiple_of(to * rows1, 8), rows1), :],
                        dst_ref=r1_all.at[step - 1, t],
                        send_sem=axis_send.at[group, slot],
                        recv_sem=axis_recv.at[group, slot],
                        device_id=shifted(*[step if a == axis else 0 for a in range(3)]),
                        device_id_type=MESH,
                    )
                )
                copies[-1].start()
        done.extend(copies)
        return copies

    loads["mass"].wait()
    loads["prev"].wait()
    loads["base"].wait()
    force = project([base_v[c] - mass_v[...] * prev_v[c] for c in range(3)])
    pl.semaphore_wait(barrier, len(partners))
    for partner in beside:
        pl.semaphore_signal(ready.at[0], inc=1, device_id=partner, device_id_type=MESH)
    core0 = []
    for c in range(3):
        d_all[c] = folded(dot(scatter_hot[c], force[c]))
        core0.append(to_sibling(c, 1))
    owner_col = lax.broadcast_in_dim(flipped[:, 2:3], (blocks, blocks), (0, 1))
    same = owner_col == codes[2:3, :]
    down = lax.broadcasted_iota(I32, (blocks, blocks), 0)
    along = lax.broadcasted_iota(I32, (blocks, blocks), 1)
    slot_row = jnp.sum(jnp.where(same & (down < along), 1.0, 0.0), axis=0, keepdims=True)
    slot_col = jnp.sum(jnp.where(same & (along < down), 1.0, 0.0), axis=1, keepdims=True)
    owners = 2 * chips
    spot_of = slot_row * owners + codes[2:3, :]
    hot = jnp.where(lax.broadcasted_iota(I32, (cap * owners, blocks), 0).astype(F32) == spot_of, 1.0, 0.0).astype(BF16)
    slots = folded(dot(hot, jnp.concatenate(split(mass_v[...]), axis=1)))
    mark = slot_col * tags + flipped[:, 3:4]
    marked = jnp.where(lax.broadcasted_iota(I32, (blocks, points), 1).astype(F32) == mark, 1.0, 0.0).astype(BF16)
    owner_hot = jnp.where(lax.broadcasted_iota(I32, (owners, blocks), 0).astype(F32) == codes[2:3, :], 1.0, 0.0).astype(BF16)
    marks = dot(owner_hot, marked)
    for s in range(2):
        for j in range(cap):
            slot_own[s, :, j, :] = slots[j * owners + s * chips : j * owners + (s + 1) * chips]
        slot_own[s, :, cap, :] = marks[s * chips : (s + 1) * chips]
    slot_copy = pltpu.make_async_remote_copy(
        src_ref=slot_own.at[1 - core],
        dst_ref=slot_out.at[core],
        send_sem=core_send.at[4],
        recv_sem=core_recv.at[4],
        device_id=sibling,
        device_id_type=MESH,
    )
    slot_copy.start()
    slot_out[core] = slot_own[core]
    chip = (z * n + y) * n + x
    axis0 = stage0(0, core0)
    pl.semaphore_wait(ready.at[0], len(beside))
    for partner in beside:
        pl.semaphore_signal(ready.at[1], inc=1, device_id=partner, device_id_type=MESH)
    load = project([base_v[c] for c in range(3)])
    for c in range(3):
        d_all[3 + c] = folded(dot(scatter_hot[c], load[c]))
    core1 = to_sibling(3, 3)
    pl.semaphore_wait(ready.at[1], len(beside))
    slot_copy.wait_recv()
    done.append(slot_copy)
    slot_in[:, chip] = slot_out[:, chip]

    def send_slots(some):
        for dx, dy, dz in some:
            to = (lax.rem(z + dz, n) * n + lax.rem(y + dy, n)) * n + lax.rem(x + dx, n)
            pltpu.make_async_remote_copy(
                src_ref=slot_out.at[:, to],
                dst_ref=slot_in.at[:, chip],
                send_sem=slot_send,
                recv_sem=slot_recv,
                device_id=shifted(dx, dy, dz),
                device_id_type=MESH,
            ).start()


    loads["stiff"].wait()
    loads["srow"].wait()
    loads["scol"].wait()
    loads["start"].wait()
    for i in range(stiff_v.shape[0]):
        stiff_hi[i], stiff_lo[i] = split(stiff_v[i].T)


    axis1 = stage0(1, [core1])

    flat = sorted(((a, b) for a in range(n) for b in range(n) if a or b), key=far, reverse=True)

    def stage1(group, copies):
        for copy in copies:
            copy.wait_recv()
        for part in range(3):
            own = pl.multiple_of(place[axes[part][0]] * rows1, 8)
            t = 3 * group + part
            total = c_all[t, pl.ds(own, rows1), :]
            for step in range(1, n):
                total = total + r1_all[step - 1, t]
            for s in range(n * n):
                f_all[t, s] = total[s * cols : (s + 1) * cols]
        for i, (da, db) in enumerate(flat):
            for part in range(3):
                _, a, b = axes[part]
                to = lax.rem(place[a] + da, n) * n + lax.rem(place[b] + db, n)
                step = [0, 0, 0]
                step[a], step[b] = da, db
                t = 3 * group + part
                pltpu.make_async_remote_copy(
                    src_ref=f_all.at[t, to],
                    dst_ref=r2_all.at[t, i],
                    send_sem=plane_send.at[group],
                    recv_sem=plane_recv.at[group],
                    device_id=shifted(*step),
                    device_id_type=MESH,
                ).start()

    def all_of(ref, send, recv):
        return pltpu.make_async_remote_copy(
            src_ref=ref, dst_ref=ref, send_sem=send, recv_sem=recv, device_id=sibling, device_id_type=MESH
        )

    def plane_end(group):
        copy = all_of(r2_all.at[3 * group : 3 * group + 3], plane_send.at[group], plane_recv.at[group])
        copy.wait_recv()
        done.append(copy)
        ends = []
        for part in range(3):
            _, a, b = axes[part]
            t = 3 * group + part
            total = f_all[t, place[a] * n + place[b]]
            for i in range(len(flat)):
                total = total + r2_all[t, i]
            ends.append(total)
        return jnp.concatenate(ends, axis=1)

    stage1(0, axis0)

    def stacked(value):
        vh, vl = split(value)
        vh, vl = vh.astype(F32), vl.astype(F32)
        return jnp.concatenate([vh, vl, jnp.zeros((8, value.shape[1]), F32)], axis=0).astype(BF16)

    group_rows = n * cols

    def couple(value, turn):
        lhs = stacked(value)
        total = jnp.zeros((group_rows, width), F32)
        row_at = lax.broadcasted_iota(I32, (group_rows, width), 0)
        col_at = lax.broadcasted_iota(I32, (cols, width), 0)
        for i in range(stiff_v.shape[0]):
            a = dot(lhs, stiff_hi[i])
            b = dot(lhs, stiff_lo[i])
            every = a[0:cols] + a[cols : 2 * cols] + b[0:cols]
            picked = jnp.sum(jnp.where(col_at == scol_s[i], every, 0.0), axis=0, keepdims=True)
            total = total + jnp.where(row_at == srow_s[i], picked, 0.0)
        for s in range(n):
            cpl_out[turn, s] = total[s * cols : (s + 1) * cols]
        copies = []
        for step in range(1, n):
            copies.append(
                pltpu.make_async_remote_copy(
                    src_ref=cpl_out.at[turn, lax.rem(x + step, n)],
                    dst_ref=cpl_in.at[turn, step - 1],
                    send_sem=cpl_send.at[turn, step - 1],
                    recv_sem=cpl_recv.at[turn, step - 1],
                    device_id=shifted(step, 0, 0),
                    device_id_type=MESH,
                )
            )
            copies[-1].start()
        done.extend(copies)
        return copies

    def coupled(turn, copies):
        total = cpl_out[turn, x]
        for step in range(1, n):
            copies[step - 1].wait_recv()
            total = total + cpl_in[turn, step - 1]
        return total

    field0 = jnp.concatenate([start_v[c] for c in range(3)], axis=1)
    cpl_copies0 = couple(field0, 0)

    send_slots(everywhere)

    loads["inverse"].wait()
    for i in range(cols):
        inverse_hi[i], inverse_lo[i] = split(inverse_v[i].T)
    flipped = codes[...].T
    lane = lax.broadcasted_iota(I32, (blocks, half), 1).astype(F32)
    pattern_wide[...] = jnp.broadcast_to(flipped[:, 1:2], (blocks, points))
    for side in range(2):
        gather_hot[side] = jnp.where(lane == flipped[:, 0:1] - side * half, 1.0, 0.0).astype(BF16)

    def correct(residual):
        lhs = stacked(residual)
        total = jnp.zeros((cols, width), F32)
        col_at = lax.broadcasted_iota(I32, (cols, width), 0)
        for k in range(cols):
            a = dot(lhs, inverse_hi[k])
            b = dot(lhs, inverse_lo[k])
            total = total + jnp.where(col_at == k, a[0:cols] + a[cols : 2 * cols] + b[0:cols], 0.0)
        return total


    for p in range(patterns):
        th, tl = split(table_v[p].T)
        spot = slice(p * points, (p + 1) * points)
        nt_w[:points, spot] = th
        nt_w[points : 2 * points, spot] = th
        nt_w[2 * points :, spot] = tl
    stage1(1, axis1)
    field1 = field0 + correct(plane_end(0) - coupled(0, cpl_copies0))
    cpl_copies1 = couple(field1, 1)

    rows_s[...] = jnp.zeros_like(rows_s)
    for c in range(3):
        rows_s[c * cols : (c + 1) * cols, :] = field1[:, c * points : (c + 1) * points]
    uh, ul = split(rows_s[...])
    spread = dot(jnp.concatenate([uh, ul, uh], axis=1), nt_w[...])

    arrived = all_of(slot_in.at[:, pl.ds(0, chips - 1)], slot_send, slot_recv)
    arrived.wait_recv()
    done.append(arrived)
    marks = jnp.concatenate([slot_in[s, :, cap, :] for s in range(2)], axis=0).T
    summed = None
    for j in range(cap):
        values = jnp.concatenate([slot_in[s, :, j, :] for s in range(2)], axis=0)
        got = dot(
            marks[j * tags : (j + 1) * tags].astype(BF16), jnp.concatenate(split(values), axis=1)
        )
        summed = got if summed is None else summed + got
    summed = folded(summed)
    wide_s[...] = jnp.zeros_like(wide_s)
    for p in range(patterns):
        for c in range(3):
            wide_s[c * cols : (c + 1) * cols, p * points : (p + 1) * points] = summed[p * cols : (p + 1) * cols]
    eh, el = split(spread * wide_s[...])
    rows_s[...] = folded(dot(eh, nn_w[...]) + dot(el, nn_w[...]))
    load = plane_end(1) - jnp.concatenate([rows_s[c * cols : (c + 1) * cols, :] for c in range(3)], axis=1)
    field2 = field1 + correct(load - coupled(1, cpl_copies1))

    for c in range(3):
        out_u[c] = field2[:, c * points : (c + 1) * points]
    home = pl.multiple_of((1 - core) * chips, 8)
    away = core * chips + chip
    own_field[...] = field2
    planes = sorted(range(n), key=lambda d: -min(d, n - d))
    for dz in planes:
        for offsets in everywhere + [(0, 0, 0)]:
            if offsets[2] == dz:
                pltpu.make_async_remote_copy(
                    src_ref=own_field,
                    dst_ref=field.at[away],
                    send_sem=back_send.at[dz],
                    recv_sem=back_recv.at[dz],
                    device_id=crossed(*offsets),
                    device_id_type=MESH,
                ).start()
    homes = []
    for dz in planes:
        first_row = home + lax.rem(z - dz + n, n) * (n * n)
        copy = all_of(field.at[pl.ds(first_row, n * n)], back_send.at[dz], back_recv.at[dz])
        copy.wait_recv()
        done.append(copy)
        view = field.at[pl.ds(first_row, n * n)]
        copy = pltpu.make_async_remote_copy(
            src_ref=view,
            dst_ref=view,
            send_sem=home_send.at[dz],
            recv_sem=home_recv.at[dz],
            device_id=sibling,
            device_id_type=MESH,
        )
        copy.start()
        homes.append(copy)
        done.append(copy)

    def gathered(side):
        fh, fl = split(field[pl.ds(side * chips, chips)].reshape(half, width))
        hot = gather_hot[side]
        spots = [slice(c * points, (c + 1) * points) for c in range(3)]
        return [dot(hot, jnp.concatenate([fh[:, spot], fl[:, spot]], axis=1)) for spot in spots]

    near = gathered(1 - core)
    for copy in homes:
        copy.wait_recv()
    rows = [(u + v).astype(BF16) for u, v in zip(near, gathered(core))]
    got = jnp.concatenate(rows, axis=0)
    got = jnp.concatenate([got, got[:, :points]], axis=1)
    pattern_at = pattern_wide[...]
    acc = [jnp.zeros((blocks, points), F32) for _ in range(3)]
    for j in range(patterns // 2):
        spot = slice(2 * j * points, 2 * (j + 1) * points)
        pair = dot(got, nt_w[:, spot])
        for c in range(3):
            mid = pair[c * blocks : (c + 1) * blocks]
            acc[c] = jnp.where(pattern_at == 2 * j, mid[:, :points], acc[c])
            acc[c] = jnp.where(pattern_at == 2 * j + 1, mid[:, points:], acc[c])
    for c in range(3):
        out_i[c] = acc[c]

    for copy in done:
        copy.wait_send()


def deliver(u_ref, i_ref, out_u, out_i, sem):
    pairs = [(u_ref, out_u)] + [(i_ref.at[c], out_i.at[c]) for c in range(3)]
    copies = [pltpu.make_async_copy(src, dst, sem.at[k]) for k, (src, dst) in enumerate(pairs)]
    for copy in copies:
        copy.start()
    for copy in copies:
        copy.wait()


def on_device(
    n,
    traction_base,
    added_mass,
    interface_prev,
    patch_route,
    basis_pattern,
    column_block,
    basis_values_table,
    stiffness,
    stiff_row,
    stiff_col,
    block_inverse,
    previous_shell_displacement,
):
    blocks = added_mass.shape[0]
    patterns, points, _ = basis_values_table.shape
    width = 3 * points
    cols = 4
    chips = n * n * n
    half, rows1 = chips * cols, n * n * cols
    keys = 2 * half
    stiffs = stiffness.shape[0]
    any_, vmem = (pl.BlockSpec(memory_space=m) for m in (pl.ANY, pltpu.VMEM))
    V = pltpu.VMEM
    dma = pltpu.SemaphoreType.DMA
    out_u, out_i = pl.pallas_call(
        functools.partial(kernel, n),
        out_shape=(
            pltpu.VMEM((3, cols, points), F32),
            pltpu.VMEM((3, blocks, points), F32),
        ),
        in_specs=[any_] * 12,
        out_specs=(vmem, vmem),
        scratch_shapes=[
            V((3, blocks, points), F32),
            V((blocks, points), F32),
            V((3, blocks, points), F32),
            V((1, blocks), I32),
            V((1, blocks), I32),
            V((1, blocks), I32),
            V((patterns, points, points), F32),
            V((stiffs, width, width), F32),
            pltpu.SMEM((stiffs,), I32),
            pltpu.SMEM((stiffs,), I32),
            V((cols, width, width), F32),
            V((3, cols, points), F32),
            V((stiffs, width, width), BF16),
            V((stiffs, width, width), BF16),
            V((cols, width, width), BF16),
            V((cols, width, width), BF16),
            V((patterns * points, 2 * points), BF16),
            V((3 * points, patterns * points), BF16),
            V((128, blocks), F32),
            V((patterns, blocks, points), BF16),
            V((3, keys, blocks), BF16),
            V((2, blocks, half), BF16),
            V((blocks, points), F32),
            V((6, keys, points), F32),
            V((6, half, points), F32),
            V((n - 1, 6, rows1, points), F32),
            V((6, n * n, cols, points), F32),
            V((6, n * n - 1, cols, points), F32),
            V((2, chips, 5, points), F32),
            V((2, chips, 5, points), F32),
            V((2, chips, 5, points), F32),
            V((2, n, cols, width), F32),
            V((2, n - 1, cols, width), F32),
            V((16, points), F32),
            V((16, patterns * points), F32),
            V((2 * chips, cols, width), F32),
            V((cols, width), F32),
            dma((12,)),
            dma((5,)),
            dma((5,)),
            pltpu.SemaphoreType.REGULAR((2,)),
            dma((2, 3 * (n - 1))),
            dma((2, 3 * (n - 1))),
            dma((2,)),
            dma((2,)),
            dma,
            dma,
            dma((2, n - 1)),
            dma((2, n - 1)),
            dma((n,)),
            dma((n,)),
            dma((n,)),
            dma((n,)),
        ],
        compiler_params=pltpu.CompilerParams(
            collective_id=0, has_side_effects=True, vmem_limit_bytes=62 * 1024 * 1024
        ),
    )(
        jnp.transpose(traction_base, (1, 0, 2)),
        added_mass,
        jnp.transpose(interface_prev, (1, 0, 2)),
        patch_route.reshape(1, blocks),
        basis_pattern.reshape(1, blocks),
        column_block.reshape(1, blocks),
        basis_values_table,
        stiffness,
        stiff_row,
        stiff_col,
        block_inverse,
        jnp.transpose(previous_shell_displacement, (1, 0, 2)),
    )
    out_u, out_i = pl.pallas_call(
        deliver,
        out_shape=(
            jax.ShapeDtypeStruct((3, cols, points), F32),
            jax.ShapeDtypeStruct((3, blocks, points), F32),
        ),
        in_specs=[vmem, vmem],
        out_specs=(any_, any_),
        scratch_shapes=[dma((4,))],
        compiler_params=pltpu.CompilerParams(vmem_limit_bytes=4 * 1024 * 1024),
    )(*(pltpu.with_memory_space_constraint(v, pltpu.VMEM) for v in (out_u, out_i)))
    return jnp.transpose(out_u, (1, 0, 2)), jnp.transpose(out_i, (1, 0, 2))


def solution(mesh):
    both = P(("fluid", "shell"))
    n = mesh.shape["shell"]
    return jax.shard_map(
        functools.partial(on_device, n),
        mesh=mesh,
        in_specs=(
            P(("fluid", "shell"), None, None),
            P(("fluid", "shell"), None),
            P(("fluid", "shell"), None, None),
            P(("fluid", "shell"), None),
            both,
            both,
            P(),
            P(("fluid", "shell"), None, None),
            both,
            both,
            P(("fluid", "shell"), None, None),
            P(("fluid", "shell"), None, None),
        ),
        out_specs=(P(("fluid", "shell"), None, None), P(("fluid", "shell"), None, None)),
        check_vma=False,
    )
```
